256 devices in a mesh: grp: 2 (over core), seq: 32 (over x, z), mdl: 4 (over y).
Axes of the slice: x: 4, y: 4, z: 8, core: 2. Of those that a mesh axis runs over, the one named last changes fastest.
Arguments:
- queries: bfloat16 [4096, 8, 2048], P(('grp', 'seq'), None, 'mdl'), may hold values from -7 to 7
- out_grads: bfloat16 [4096, 8, 2048], P(('grp', 'seq'), None, 'mdl'), may hold values from -12 to 12
- owners: int32 [4096], P(('grp', 'seq')), may hold values from 0 to 63, as said below
- src_keys: bfloat16 [64, 512, 2048], P(('grp', 'seq'), None, 'mdl'), may hold values from -7 to 7
- src_values: bfloat16 [64, 512, 2048], P(('grp', 'seq'), None, 'mdl'), may hold values from -6 to 6
- states: bfloat16 [64, 512, 2048], P(('grp', 'seq'), None, 'mdl'), may hold values from -0.59765625 to 0.59765625
- kv_weight: bfloat16 [2048, 2, 2048], P(('grp', 'seq'), None, 'mdl'), may hold values from -0.125 to 0.125
- src_lengths: int32 [64], P(('grp', 'seq')), may hold values from 128 to 512, as said below
Outputs:
- query_grads: bfloat16 [4096, 8, 2048], P(('grp', 'seq'), None, 'mdl')
- state_grads: bfloat16 [64, 512, 2048], P(('grp', 'seq'), None, 'mdl')
- weight_grads: float32 [2048, 2, 2048], P(('grp', 'seq'), None, 'mdl')
The draws below stay inside these ranges and needn't reach their ends.
Inputs may be any that keep to these rules, and one draw needn't show every extreme that they name: `owners`: the 64 targets of each index of grp and seq (an aligned block) name any one source at most 2 times; one source, the same for every block, is named exactly 2 times by every block. `src_lengths`: each length is a multiple of 128; the largest is 512.
All inputs are finite; a program needn't handle non-finite values.
Results may differ from the reference program's by a relative error of at most 0.012.
Values may be sent and summed in bfloat16 or wider, within the bound.
A program may use at most 64 MiB of HBM per device.

```python
import jax
import jax.numpy as jnp
from jax import lax

D = 2048
HEADS = 32
HEAD_DIM = 64
INNER = 2048
SRC = 512
TGT = 8
TGT_DEV = 64
SOURCES = 64
TARGETS = 4096
MOST = 2


def draw_queries(key, part):
    inner_key = jax.random.fold_in(key, 11)
    shape = (TARGETS, TGT, HEADS, HEAD_DIM)
    values = jnp.clip(jax.random.normal(inner_key, shape, jnp.float32), -4.0, 4.0)
    return values.reshape(TARGETS, TGT, INNER).astype(jnp.bfloat16)


def draw_src_keys(key, part):
    inner_key = jax.random.fold_in(key, 23)
    shape = (SOURCES, SRC, HEADS, HEAD_DIM)
    values = jnp.clip(jax.random.normal(inner_key, shape, jnp.float32), -4.0, 4.0)
    return values.reshape(SOURCES, SRC, INNER).astype(jnp.bfloat16)


def draw_owners(key, part):
    busiest = jax.random.randint(jax.random.fold_in(key, 5), (), 0, SOURCES)

    def one_block(block_id):
        block_key = jax.random.fold_in(key, 100 + block_id)
        pool = jnp.arange((SOURCES - 1) * MOST, dtype=jnp.int32) // MOST
        pool = jax.random.permutation(jax.random.fold_in(block_key, 1), pool)
        others = pool[:TGT_DEV - MOST]
        others = others + (others >= busiest).astype(jnp.int32)
        names = jnp.concatenate([jnp.full((MOST,), busiest, jnp.int32), others.astype(jnp.int32)])
        order = jax.random.permutation(jax.random.fold_in(block_key, 2), TGT_DEV)
        return names[order]
    return jax.vmap(one_block)(jnp.arange(SOURCES, dtype=jnp.int32)).reshape(TARGETS).astype(jnp.int32)


def draw_src_lengths(key, part):
    blocks = jax.random.randint(jax.random.fold_in(key, 7), (SOURCES,), 1, SRC // 128 + 1)
    longest = jax.random.randint(jax.random.fold_in(key, 8), (), 0, SOURCES)
    blocks = jnp.where(jnp.arange(SOURCES, dtype=jnp.int32) == longest, SRC // 128, blocks)
    return (blocks * 128).astype(jnp.int32)


def block_scale(key, dims, pieces, least, top_value):
    factor_of, own = 1.0, jax.random.fold_in(key, 6)
    for dim, parts in pieces:
        draws = jnp.exp(jax.random.uniform(jax.random.fold_in(own, dim), (parts,), jnp.float32, least / len(pieces), top_value / len(pieces)))
        factor_of = factor_of * jnp.repeat(draws, dims[dim] // parts).reshape([-1 if axis == dim else 1 for axis in range(len(dims))])
    return factor_of


def noise(key, extent, deviation, limit, split=(), kind=jnp.bfloat16):
    values = deviation * jax.random.normal(key, extent, jnp.float32)
    if split:
        values = values * block_scale(key, extent, split, -0.22, 0.18)
    return jnp.clip(values, -limit, limit).astype(kind)


def setup_inputs(seed: int = 0) -> dict:
    arg_keys = jax.random.split(jax.random.key(seed), 9)
    return {
        "queries": draw_queries(jax.random.fold_in(arg_keys[8], 71), 0),
        "out_grads": noise(arg_keys[1], (TARGETS, TGT, INNER), 2.0, 12.0, ((0, 64), (2, 4))),
        "owners": draw_owners(jax.random.fold_in(arg_keys[8], 71), 0),
        "src_keys": draw_src_keys(jax.random.fold_in(arg_keys[8], 71), 0),
        "src_values": noise(arg_keys[4], (SOURCES, SRC, INNER), 1.0, 6.0, ((0, 64), (2, 4))),
        "states": noise(arg_keys[5], (SOURCES, SRC, D), 0.1, 0.59765625, ((0, 64), (2, 4))),
        "kv_weight": noise(arg_keys[6], (INNER, 2, D), INNER ** -0.5, 0.125, ((0, 64), (2, 4))),
        "src_lengths": draw_src_lengths(jax.random.fold_in(arg_keys[8], 71), 0),
    }


def block_grads(query_block, grad_block, key_block, value_block, key_valid):
    score_scale = HEAD_DIM ** -0.5
    query_f = query_block.astype(jnp.float32)
    grad_f = grad_block.astype(jnp.float32)
    key_f = key_block.astype(jnp.float32)
    value_f = value_block.astype(jnp.float32)
    scores = jnp.einsum('bqhe,bkhe->bhqk', query_f, key_f) * score_scale
    scores = jnp.where(key_valid[:, None, None, :], scores, -1e30)
    row_peak = jnp.max(scores, axis=-1, keepdims=True)
    exp_terms = jnp.exp(scores - row_peak)
    attn_probs = exp_terms / jnp.sum(exp_terms, axis=-1, keepdims=True)
    probs_b = lax.optimization_barrier(attn_probs.astype(jnp.bfloat16))
    probs_back = probs_b.astype(jnp.float32)
    context = jnp.einsum('bhqk,bkhe->bqhe', probs_back, value_f)
    row_delta = jnp.sum(grad_f * context, axis=-1)
    prob_grad = jnp.einsum('bqhe,bkhe->bhqk', grad_f, value_f)
    centred = prob_grad - jnp.transpose(row_delta, (0, 2, 1))[..., None]
    score_grad = lax.optimization_barrier((attn_probs * centred * score_scale).astype(jnp.bfloat16))
    score_back = score_grad.astype(jnp.float32)
    query_grad = jnp.einsum('bhqk,bkhe->bqhe', score_back, key_f).astype(jnp.bfloat16)
    key_grad = jnp.einsum('bhqk,bqhe->bkhe', score_back, query_f)
    value_grad = jnp.einsum('bhqk,bqhe->bkhe', probs_back, grad_f)
    return query_grad, key_grad, value_grad


def reference(queries, out_grads, owners, src_keys, src_values, states, kv_weight, src_lengths):
    query_all = queries.reshape(SOURCES, TGT_DEV, TGT, HEADS, HEAD_DIM)
    grad_all = out_grads.reshape(SOURCES, TGT_DEV, TGT, HEADS, HEAD_DIM)
    owner_all = owners.reshape(SOURCES, TGT_DEV).astype(jnp.int32)
    key_all = src_keys.reshape(SOURCES, SRC, HEADS, HEAD_DIM)
    value_all = src_values.reshape(SOURCES, SRC, HEADS, HEAD_DIM)
    positions = jnp.arange(SRC, dtype=jnp.int32)

    def attend_step(totals, block_pair):
        query_block, grad_block, owner_block = block_pair
        key_block = key_all[owner_block]
        value_block = value_all[owner_block]
        key_valid = positions[None, :] < src_lengths[owner_block][:, None]
        query_grad, key_grad, value_grad = block_grads(query_block, grad_block, key_block, value_block, key_valid)
        key_total = totals[0].at[owner_block].add(key_grad)
        value_total = totals[1].at[owner_block].add(value_grad)
        return (key_total, value_total), query_grad

    zero_grads = jnp.zeros((SOURCES, SRC, HEADS, HEAD_DIM), jnp.float32)
    (key_total, value_total), query_out = lax.scan(attend_step, (zero_grads, zero_grads), (query_all, grad_all, owner_all))
    query_grads = query_out.reshape(TARGETS, TGT, INNER)
    key_flat = key_total.astype(jnp.bfloat16).reshape(SOURCES * SRC, INNER)
    value_flat = value_total.astype(jnp.bfloat16).reshape(SOURCES * SRC, INNER)
    state_sum = jnp.dot(key_flat, kv_weight[:, 0, :], preferred_element_type=jnp.float32)
    state_sum = state_sum + jnp.dot(value_flat, kv_weight[:, 1, :], preferred_element_type=jnp.float32)
    state_grads = state_sum.astype(jnp.bfloat16).reshape(SOURCES, SRC, D)
    flat_states = states.reshape(SOURCES * SRC, D)
    grad_key = lax.dot_general(key_flat, flat_states, (((0,), (0,)), ((), ())), preferred_element_type=jnp.float32)
    grad_value = lax.dot_general(value_flat, flat_states, (((0,), (0,)), ((), ())), preferred_element_type=jnp.float32)
    weight_grads = jnp.stack([grad_key, grad_value], axis=1)
    return (query_grads, state_grads, weight_grads)
```

```python
import jax
import jax.numpy as jnp
from jax import lax
from jax.sharding import PartitionSpec as P

HEAD_DIM = 64
ROWS = ("grp", "seq")
ALL = ("grp", "seq", "mdl")


def block_grads(query_block, grad_block, key_local, value_local, key_valid):
    score_scale = key_local.shape[-1] ** (-0.5)
    scores = (
        jnp.einsum("rhe,khe->hrk", query_block, key_local, preferred_element_type=jnp.float32)
        * score_scale
    )
    scores = jnp.where(key_valid[None, None, :], scores, -1e30)
    row_peak = jnp.max(scores, axis=-1, keepdims=True)
    exp_terms = jnp.exp(scores - row_peak)
    attn_probs = exp_terms / jnp.sum(exp_terms, axis=-1, keepdims=True)
    probs_b = attn_probs.astype(jnp.bfloat16)
    context = jnp.einsum("hrk,khe->rhe", probs_b, value_local, preferred_element_type=jnp.float32)
    row_delta = jnp.sum(grad_block.astype(jnp.float32) * context, axis=-1)
    prob_grad = jnp.einsum(
        "rhe,khe->hrk", grad_block, value_local, preferred_element_type=jnp.float32
    )
    score_grad = (attn_probs * (prob_grad - row_delta.T[:, :, None]) * score_scale).astype(
        jnp.bfloat16
    )
    query_grad = jnp.einsum(
        "hrk,khe->rhe", score_grad, key_local, preferred_element_type=jnp.float32
    ).astype(jnp.bfloat16)
    key_grad = jnp.einsum(
        "hrk,rhe->khe", score_grad, query_block, preferred_element_type=jnp.float32
    )
    value_grad = jnp.einsum("hrk,rhe->khe", probs_b, grad_block, preferred_element_type=jnp.float32)
    return (query_grad, key_grad, value_grad)


def plane_moves(peers, planes):
    per_plane = peers // planes
    moves = []
    for owner in range(peers):
        plane, row = divmod(owner, per_plane)
        for part in range(planes):
            place = part * per_plane + row
            moves.append((owner * planes + part, place * planes + plane))
    return moves


def on_device(queries, out_grads, owners, src_keys, src_values, states, kv_weight, src_lengths):
    peer_count = lax.axis_size(ROWS)
    planes = lax.axis_size("mdl")
    seqs = lax.axis_size("seq")
    grps = lax.axis_size("grp")
    tgt_dev, tgt_len, inner_dev = queries.shape
    features = states.shape[2]
    unit_rows = kv_weight.shape[0]
    per_peer = max(2, 2 * tgt_dev // peer_count)
    slot_count = peer_count * per_peer
    row_width = tgt_len * inner_dev
    local_heads = inner_dev // HEAD_DIM
    src_len = src_keys.shape[1]
    moves = plane_moves(peer_count, planes)
    member = (owners[:, None] == jnp.arange(peer_count, dtype=jnp.int32)[None, :]).astype(jnp.int32)
    earlier = jnp.cumsum(member, axis=0) - member
    rank_own = jnp.sum(earlier * member, axis=1)
    slot_of = owners * per_peer + rank_own
    selector = (jnp.arange(slot_count, dtype=jnp.int32)[:, None] == slot_of[None, :]).astype(
        jnp.bfloat16
    )

    weight_piece = jnp.transpose(kv_weight, (1, 0, 2))
    weight_piece = lax.ppermute(weight_piece, ALL, moves)
    weight_half = lax.all_gather(weight_piece, "seq", axis=0)
    weight_all = lax.all_gather(weight_half, "grp", axis=0)
    states_all = lax.all_gather(states[0], "mdl", axis=0)

    send_query = jnp.dot(
        selector, queries.reshape(tgt_dev, row_width), preferred_element_type=jnp.float32
    ).astype(jnp.bfloat16)
    send_grad = jnp.dot(
        selector, out_grads.reshape(tgt_dev, row_width), preferred_element_type=jnp.float32
    ).astype(jnp.bfloat16)
    got_query, got_grad = (
        lax.all_to_all(send_query, ROWS, split_axis=0, concat_axis=0, tiled=True),
        lax.all_to_all(send_grad, ROWS, split_axis=0, concat_axis=0, tiled=True),
    )
    total_rows = slot_count * tgt_len
    block_rows = 512
    block_count = total_rows // block_rows
    query_rows = got_query.reshape(block_count, block_rows, local_heads, HEAD_DIM)
    grad_rows = got_grad.reshape(block_count, block_rows, local_heads, HEAD_DIM)
    key_local = src_keys[0].reshape(src_len, local_heads, HEAD_DIM)
    value_local = src_values[0].reshape(src_len, local_heads, HEAD_DIM)
    key_valid = jnp.arange(src_len, dtype=jnp.int32) < src_lengths[0]

    def attend_step(totals, block_pair):
        query_grad, key_grad, value_grad = block_grads(
            block_pair[0], block_pair[1], key_local, value_local, key_valid
        )
        return ((totals[0] + key_grad, totals[1] + value_grad), query_grad)

    zero_grads = jnp.zeros((src_len, local_heads, HEAD_DIM), jnp.float32)
    (key_total, value_total), query_blocks = lax.scan(
        attend_step, (zero_grads, zero_grads), (query_rows, grad_rows)
    )
    key_bf = key_total.reshape(src_len, inner_dev).astype(jnp.bfloat16)
    value_bf = value_total.reshape(src_len, inner_dev).astype(jnp.bfloat16)

    def weight_term(grads):
        terms = lax.dot_general(
            grads, states_all, (((0,), (1,)), ((), ())), preferred_element_type=jnp.float32
        )
        terms = jnp.transpose(terms, (1, 0, 2)).astype(jnp.bfloat16)
        terms = terms.reshape(grps, seqs * unit_rows, features)
        terms = lax.psum_scatter(terms, "grp", scatter_dimension=0)
        return lax.psum_scatter(terms, "seq", scatter_dimension=0, tiled=True)

    key_piece = weight_term(key_bf)
    value_piece = weight_term(value_bf)
    weight_out = lax.ppermute(
        jnp.stack([key_piece, value_piece], axis=0), ALL, [(b, a) for a, b in moves]
    )
    weight_out = jnp.transpose(weight_out.astype(jnp.float32), (1, 0, 2))

    weight_all = weight_all.reshape(planes, inner_dev // unit_rows, 2, unit_rows, features)
    weight_key = weight_all[:, :, 0].reshape(planes, inner_dev, features)
    weight_value = weight_all[:, :, 1].reshape(planes, inner_dev, features)
    part = jnp.einsum("ij,mjd->mid", key_bf, weight_key, preferred_element_type=jnp.float32)
    part = part + jnp.einsum(
        "ij,mjd->mid", value_bf, weight_value, preferred_element_type=jnp.float32
    )
    state_out = lax.psum_scatter(part.astype(jnp.bfloat16), "mdl", scatter_dimension=0)
    state_out = state_out.reshape(1, src_len, features)

    back_rows = query_blocks.reshape(slot_count, row_width)
    returned = lax.all_to_all(back_rows, ROWS, split_axis=0, concat_axis=0, tiled=True)
    query_out = lax.dot_general(
        selector, returned, (((0,), (0,)), ((), ())), preferred_element_type=jnp.float32
    )
    query_out = query_out.astype(jnp.bfloat16).reshape(tgt_dev, tgt_len, inner_dev)
    return (query_out, state_out, weight_out)


def solution(mesh):
    rows = P(ROWS, None, "mdl")
    return jax.shard_map(
        on_device,
        mesh=mesh,
        in_specs=(rows, rows, P(ROWS), rows, rows, rows, rows, P(ROWS)),
        out_specs=(rows, rows, rows),
        check_vma=False,
    )
```

```python
import functools
import math

import jax
import jax.numpy as jnp
from jax import lax
from jax.experimental import pallas as pl
from jax.experimental.pallas import tpu as pltpu
from jax.sharding import PartitionSpec as P

HEAD_DIM = 64
LANES = 128
ROWS = ("grp", "seq")
ALL = ("grp", "seq", "mdl")
MESH = pl.DeviceIdType.MESH
XS, ZS = 4, 8


def place():
    seq = lax.axis_index("seq")
    return lax.axis_index("grp"), lax.div(seq, ZS), lax.axis_index("mdl"), lax.rem(seq, ZS)


def in_plane(core, x, y, z, offset, cores):
    to_core = lax.rem(core + lax.div(offset, XS * ZS), cores)
    to_x = lax.rem(x + lax.rem(lax.div(offset, ZS), XS), XS)
    to_z = lax.rem(z + lax.rem(offset, ZS), ZS)
    return (to_core, to_x * ZS + to_z, y)


def back_in_plane(core, x, y, z, offset, cores):
    to_core = lax.rem(core + cores - lax.div(offset, XS * ZS), cores)
    to_x = lax.rem(x + XS - lax.rem(lax.div(offset, ZS), XS), XS)
    to_z = lax.rem(z + ZS - lax.rem(offset, ZS), ZS)
    return (to_core, to_x * ZS + to_z, y)


def greet(core, x, y, z, cores, ys):
    barrier = pltpu.get_barrier_semaphore()
    peers = cores * XS * ZS

    @pl.loop(1, peers)
    def _(offset):
        there = in_plane(core, x, y, z, offset, cores)
        pl.semaphore_signal(barrier, inc=1, device_id=there, device_id_type=MESH)

    @pl.loop(1, ys)
    def _(offset):
        there = (core, x * ZS + z, lax.rem(y + offset, ys))
        pl.semaphore_signal(barrier, inc=1, device_id=there, device_id_type=MESH)

    pl.semaphore_wait(barrier, peers + ys - 2)


def send(source, target, send_sem, recv_sem, there):
    pltpu.make_async_remote_copy(
        src_ref=source,
        dst_ref=target,
        send_sem=send_sem,
        recv_sem=recv_sem,
        device_id=there,
        device_id_type=MESH,
    ).start()


def wait_bytes(ref, sem):
    pltpu.make_async_copy(ref, ref, sem).wait()


def dot(left, right, dims):
    return lax.dot_general(left, right, (dims, ((), ())), preferred_element_type=jnp.float32)


def slot_of(owner, place_ref):
    core, x, z = place_ref[0], place_ref[1], place_ref[2]
    cores = place_ref[3]
    to_core = lax.rem(lax.div(owner, XS * ZS) + cores - core, cores)
    to_x = lax.rem(lax.rem(lax.div(owner, ZS), XS) + XS - x, XS)
    to_z = lax.rem(lax.rem(owner, ZS) + ZS - z, ZS)
    return (to_core * XS + to_x) * ZS + to_z


def pack_kernel(place_ref, owners_ref, query_ref, grad_ref, out_ref, used_ref):
    tgt_len = query_ref.shape[1]
    out_ref[...] = jnp.zeros_like(out_ref)

    @pl.loop(0, out_ref.shape[0])
    def _(peer):
        used_ref[peer] = 0

    @pl.loop(0, query_ref.shape[0])
    def _(target):
        peer = slot_of(owners_ref[target], place_ref)
        used = used_ref[peer]
        used_ref[peer] = used + 1
        for slot in range(2):

            @pl.when(used == slot)
            def _():
                at = slice(slot * tgt_len, (slot + 1) * tgt_len)
                out_ref[peer, 0, at, :] = query_ref[target]
                out_ref[peer, 1, at, :] = grad_ref[target]


def pack(own, owners, queries, out_grads, peers):
    targets, tgt_len, width = queries.shape
    smem, vmem = pl.BlockSpec(memory_space=pltpu.SMEM), pl.BlockSpec(memory_space=pltpu.VMEM)
    return pl.pallas_call(
        pack_kernel,
        out_shape=jax.ShapeDtypeStruct((peers, 2, 2 * tgt_len, width), queries.dtype),
        in_specs=[smem, smem, vmem, vmem],
        out_specs=vmem,
        scratch_shapes=[pltpu.SMEM((peers,), jnp.int32)],
        name="pack_targets",
    )(own, owners, queries, out_grads)


def unpack_kernel(place_ref, owners_ref, back_ref, out_ref, used_ref):
    tgt_len = out_ref.shape[1]

    @pl.loop(0, back_ref.shape[0])
    def _(peer):
        used_ref[peer] = 0

    @pl.loop(0, out_ref.shape[0])
    def _(target):
        peer = slot_of(owners_ref[target], place_ref)
        used = used_ref[peer]
        used_ref[peer] = used + 1
        for slot in range(2):

            @pl.when(used == slot)
            def _():
                out_ref[target] = back_ref[peer, slot * tgt_len : (slot + 1) * tgt_len, :]


def unpack(own, owners, returned, tgt_len):
    peers, _, width = returned.shape
    smem, vmem = pl.BlockSpec(memory_space=pltpu.SMEM), pl.BlockSpec(memory_space=pltpu.VMEM)
    return pl.pallas_call(
        unpack_kernel,
        out_shape=jax.ShapeDtypeStruct((owners.shape[0], tgt_len, width), returned.dtype),
        in_specs=[smem, smem, vmem],
        out_specs=vmem,
        scratch_shapes=[pltpu.SMEM((peers,), jnp.int32)],
        name="unpack_targets",
    )(own, owners, returned)


def exchange_kernel(
    cores, ys, send_ref, states_ref, piece_ref, got_ref, all_states, all_weights, out_sem, in_sem, own_sem
):
    core, x, y, z = place()
    peers = cores * XS * ZS
    greet(core, x, y, z, cores, ys)

    own_states = pltpu.make_async_copy(states_ref, all_states.at[y], own_sem.at[0])
    own_states.start()
    own_piece = pltpu.make_async_copy(piece_ref, all_weights.at[core, x, z], own_sem.at[1])
    own_piece.start()
    own_rows = pltpu.make_async_copy(send_ref.at[0], got_ref.at[0], own_sem.at[2])
    own_rows.start()

    @pl.loop(1, ZS)
    def _(offset):
        there = (core, x * ZS + lax.rem(z + offset, ZS), y)
        send(piece_ref, all_weights.at[core, x, z], out_sem.at[0], in_sem.at[0], there)

    @pl.loop(1, peers)
    def _(offset):
        there = in_plane(core, x, y, z, offset, cores)
        send(send_ref.at[offset], got_ref.at[offset], out_sem.at[1], in_sem.at[1], there)

    @pl.loop(1, ys)
    def _(offset):
        there = (core, x * ZS + z, lax.rem(y + offset, ys))
        send(states_ref, all_states.at[y], out_sem.at[2], in_sem.at[2], there)

    own_piece.wait()
    wait_bytes(all_weights.at[0, 0, pl.ds(0, ZS - 1)], in_sem.at[0])

    @pl.loop(1, XS)
    def _(offset):
        there = (core, lax.rem(x + offset, XS) * ZS + z, y)
        rows = all_weights.at[core, x]
        send(rows, rows, out_sem.at[3], in_sem.at[3], there)

    wait_bytes(all_weights.at[0, pl.ds(0, XS - 1)], in_sem.at[3])

    @pl.loop(1, cores)
    def _(offset):
        there = (lax.rem(core + offset, cores), x * ZS + z, y)
        half = all_weights.at[core]
        send(half, half, out_sem.at[4], in_sem.at[4], there)

    own_states.wait()
    own_rows.wait()
    wait_bytes(all_weights.at[pl.ds(0, cores - 1)], in_sem.at[4])
    wait_bytes(all_states.at[pl.ds(0, ys - 1)], in_sem.at[2])
    wait_bytes(got_ref.at[pl.ds(0, peers - 1)], in_sem.at[1])
    wait_bytes(all_weights.at[0, 0, pl.ds(0, ZS - 1)], out_sem.at[0])
    wait_bytes(send_ref.at[pl.ds(0, peers - 1)], out_sem.at[1])
    wait_bytes(all_states.at[pl.ds(0, ys - 1)], out_sem.at[2])
    wait_bytes(all_weights.at[0, pl.ds(0, XS - 1)], out_sem.at[3])
    wait_bytes(all_weights.at[pl.ds(0, cores - 1)], out_sem.at[4])


def exchange(packed, states, piece, cores, ys):
    vmem, hbm = pl.BlockSpec(memory_space=pltpu.VMEM), pl.BlockSpec(memory_space=pl.ANY)
    return pl.pallas_call(
        functools.partial(exchange_kernel, cores, ys),
        out_shape=(
            jax.ShapeDtypeStruct(packed.shape, packed.dtype),
            jax.ShapeDtypeStruct((ys, *states.shape), states.dtype),
            jax.ShapeDtypeStruct((cores, XS, ZS, *piece.shape), piece.dtype),
        ),
        in_specs=[vmem, hbm, hbm],
        out_specs=(vmem, hbm, hbm),
        scratch_shapes=[
            pltpu.SemaphoreType.DMA((5,)),
            pltpu.SemaphoreType.DMA((5,)),
            pltpu.SemaphoreType.DMA((3,)),
        ],
        compiler_params=pltpu.CompilerParams(
            collective_id=1, has_side_effects=True, vmem_limit_bytes=40 << 20
        ),
        name="exchange_targets",
    )(packed, states, piece)


def attend_kernel(
    length_ref, got_ref, key_ref, value_ref, back_ref, grads_out, grads_t_out, key_t, key_sums, value_sums
):
    width = got_ref.shape[3]
    src_len = key_ref.shape[0]
    group = got_ref.shape[0] // pl.num_programs(0)
    step = pl.program_id(0)
    scale = HEAD_DIM**-0.5
    exp_scale = scale * math.log2(math.e)
    rows = group * got_ref.shape[2]
    start = step * group

    @pl.when(step == 0)
    def _():
        key_sums[...] = jnp.zeros_like(key_sums)
        value_sums[...] = jnp.zeros_like(value_sums)
        key_t[...] = jnp.transpose(key_ref[...])

    valid = lax.broadcasted_iota(jnp.int32, (src_len, rows), 0) < length_ref[0]
    lane = lax.broadcasted_iota(jnp.int32, (rows, LANES), 1)
    for pair in range(width // LANES):
        at = slice(pair * LANES, (pair + 1) * LANES)
        query = got_ref[pl.ds(start, group), 0, :, at].reshape(rows, LANES)
        grad = got_ref[pl.ds(start, group), 1, :, at].reshape(rows, LANES)
        keys = key_ref[:, at]
        values = value_ref[:, at]
        key_sum = key_sums[:, at]
        value_sum = value_sums[:, at]
        back = []
        for half in range(LANES // HEAD_DIM):
            own = (lane >= half * HEAD_DIM) & (lane < (half + 1) * HEAD_DIM)
            query_h = jnp.where(own, query, jnp.zeros_like(query))
            grad_h = jnp.where(own, grad, jnp.zeros_like(grad))
            scores = dot(keys, query_h, ((1,), (1,)))
            scores = jnp.where(valid, scores, -1e30)
            peak = jnp.max(scores, axis=0, keepdims=True)
            terms = jnp.exp2((scores - peak) * exp_scale)
            probs = terms * (1.0 / jnp.sum(terms, axis=0, keepdims=True))
            probs_b = probs.astype(jnp.bfloat16)
            prob_grad = dot(values, grad_h, ((1,), (1,)))
            delta = jnp.sum(probs_b.astype(jnp.float32) * prob_grad, axis=0, keepdims=True)
            score_grad = (probs * (prob_grad - delta)).astype(jnp.bfloat16)
            key_sum = key_sum + dot(score_grad, query_h, ((1,), (0,)))
            value_sum = value_sum + dot(probs_b, grad_h, ((1,), (0,)))
            head = pair * LANES + half * HEAD_DIM
            back.append(dot(key_t[head : head + HEAD_DIM, :], score_grad, ((1,), (0,))))
        key_sums[:, at] = key_sum
        value_sums[:, at] = value_sum
        back = jnp.concatenate(back, axis=0) * scale
        back = jnp.transpose(back).astype(jnp.bfloat16)
        back_ref[pl.ds(start, group), :, at] = back.reshape(group, rows // group, LANES)

    @pl.when(step == pl.num_programs(0) - 1)
    def _():
        grads_out[0] = (key_sums[...] * scale).astype(jnp.bfloat16)
        grads_out[1] = value_sums[...].astype(jnp.bfloat16)
        grads_t_out[0] = jnp.transpose(key_sums[...] * scale).astype(jnp.bfloat16)
        grads_t_out[1] = jnp.transpose(value_sums[...]).astype(jnp.bfloat16)


def attend(got, length, keys, values, steps=4):
    peers, _, peer_rows, width = got.shape
    src_len = keys.shape[0]
    smem, vmem = pl.BlockSpec(memory_space=pltpu.SMEM), pl.BlockSpec(memory_space=pltpu.VMEM)
    return pl.pallas_call(
        attend_kernel,
        grid=(steps,),
        out_shape=(
            jax.ShapeDtypeStruct((peers, peer_rows, width), got.dtype),
            jax.ShapeDtypeStruct((2, src_len, width), got.dtype),
            jax.ShapeDtypeStruct((2, width, src_len), got.dtype),
        ),
        in_specs=[smem, vmem, vmem, vmem],
        out_specs=(vmem, vmem, vmem),
        scratch_shapes=[
            pltpu.VMEM((width, src_len), keys.dtype),
            pltpu.VMEM((src_len, width), jnp.float32),
            pltpu.VMEM((src_len, width), jnp.float32),
        ],
        compiler_params=pltpu.CompilerParams(vmem_limit_bytes=40 << 20),
        name="attend_targets",
    )(length, got, keys, values)


def finish_kernel(
    cores,
    ys,
    back_ref,
    grads_ref,
    grads_t_ref,
    states_ref,
    weights_ref,
    returned_ref,
    state_out,
    piece_out,
    term_away,
    term_own,
    term_in,
    x_in,
    z_own,
    z_in,
    part,
    part_in,
    out_sem,
    in_sem,
    own_sem,
):
    core, x, y, z = place()
    peers = cores * XS * ZS
    unit_rows, features = term_own.shape[3:]
    width = grads_ref.shape[2]
    half_rows = ZS * unit_rows
    greet(core, x, y, z, cores, ys)

    own_rows = pltpu.make_async_copy(back_ref.at[0], returned_ref.at[0], own_sem)
    own_rows.start()

    def weight_terms(to_core, target):
        @pl.loop(0, XS)
        def _(to_x):
            block = to_core * (XS // 2) + lax.div(to_x, 2)
            first = pl.multiple_of(lax.rem(to_x, 2) * half_rows, half_rows)
            for kind in range(2):
                terms = dot(grads_t_ref[kind, pl.ds(first, half_rows), :], states_ref[block], ((1,), (0,)))
                target[to_x, :, kind] = terms.astype(jnp.bfloat16).reshape(ZS, unit_rows, features)

    sibling = lax.rem(core + 1, cores)
    weight_terms(sibling, term_away)
    send(term_away, term_in, out_sem.at[0], in_sem.at[0], (sibling, x * ZS + z, y))

    @pl.loop(1, peers)
    def _(offset):
        there = back_in_plane(core, x, y, z, offset, cores)
        send(back_ref.at[offset], returned_ref.at[offset], out_sem.at[1], in_sem.at[1], there)

    weight_terms(core, term_own)
    wait_bytes(term_in, in_sem.at[0])

    @pl.loop(0, XS)
    def _(to_x):
        both = term_own[to_x].astype(jnp.float32) + term_in[to_x].astype(jnp.float32)
        term_own[to_x] = both.astype(jnp.bfloat16)

    @pl.loop(1, XS)
    def _(offset):
        to_x = lax.rem(x + offset, XS)
        send(term_own.at[to_x], x_in.at[offset - 1], out_sem.at[2], in_sem.at[2], (core, to_x * ZS + z, y))

    def state_terms(block, target):
        for kind in range(2):
            rows = weights_ref[lax.div(block, 2), pl.ds(lax.rem(block, 2) * 2, 2), :, kind]
            terms = dot(grads_ref[kind], rows.reshape(width, features), ((1,), (0,)))
            total = terms if kind == 0 else total + terms
        target[...] = total.astype(jnp.bfloat16)

    @pl.loop(1, ys)
    def _(offset):
        to_y = lax.rem(y + offset, ys)
        state_terms(to_y, part.at[offset])
        send(part.at[offset], part_in.at[offset - 1], out_sem.at[4], in_sem.at[4], (core, x * ZS + z, to_y))

    state_terms(y, part.at[0])
    wait_bytes(x_in, in_sem.at[2])

    @pl.loop(0, ZS)
    def _(to_z):
        total = term_own[x, to_z].astype(jnp.float32)
        for other in range(XS - 1):
            total = total + x_in[other, to_z].astype(jnp.float32)
        z_own[to_z] = total.astype(jnp.bfloat16)

    @pl.loop(1, ZS)
    def _(offset):
        to_z = lax.rem(z + offset, ZS)
        send(z_own.at[to_z], z_in.at[offset - 1], out_sem.at[3], in_sem.at[3], (core, x * ZS + to_z, y))

    wait_bytes(part_in, in_sem.at[4])
    total = part[0].astype(jnp.float32)
    for other in range(ys - 1):
        total = total + part_in[other].astype(jnp.float32)
    state_out[...] = total.astype(jnp.bfloat16)

    wait_bytes(z_in, in_sem.at[3])
    total = z_own[z].astype(jnp.float32)
    for other in range(ZS - 1):
        total = total + z_in[other].astype(jnp.float32)
    piece_out[...] = total

    own_rows.wait()
    wait_bytes(returned_ref.at[pl.ds(0, peers - 1)], in_sem.at[1])
    wait_bytes(term_away, out_sem.at[0])
    wait_bytes(back_ref.at[pl.ds(0, peers - 1)], out_sem.at[1])
    wait_bytes(x_in, out_sem.at[2])
    wait_bytes(z_in, out_sem.at[3])
    wait_bytes(part_in, out_sem.at[4])


def finish(back, grads, grads_t, states_all, weights_all, cores, ys):
    vmem = pl.BlockSpec(memory_space=pltpu.VMEM)
    _, src_len, _ = grads.shape
    features = states_all.shape[2]
    piece = weights_all.shape[3:]
    wire = grads.dtype
    return pl.pallas_call(
        functools.partial(finish_kernel, cores, ys),
        out_shape=(
            jax.ShapeDtypeStruct(back.shape, wire),
            jax.ShapeDtypeStruct((src_len, features), wire),
            jax.ShapeDtypeStruct(piece, jnp.float32),
        ),
        in_specs=[vmem] * 5,
        out_specs=(vmem, vmem, vmem),
        scratch_shapes=[
            pltpu.VMEM((XS, ZS, *piece), wire),
            pltpu.VMEM((XS, ZS, *piece), wire),
            pltpu.VMEM((XS, ZS, *piece), wire),
            pltpu.VMEM((XS - 1, ZS, *piece), wire),
            pltpu.VMEM((ZS, *piece), wire),
            pltpu.VMEM((ZS - 1, *piece), wire),
            pltpu.VMEM((ys, src_len, features), wire),
            pltpu.VMEM((ys - 1, src_len, features), wire),
            pltpu.SemaphoreType.DMA((5,)),
            pltpu.SemaphoreType.DMA((5,)),
            pltpu.SemaphoreType.DMA,
        ],
        compiler_params=pltpu.CompilerParams(
            collective_id=2, has_side_effects=True, vmem_limit_bytes=48 << 20
        ),
        name="finish_gradients",
    )(back, grads, grads_t, states_all, weights_all)


def plane_moves(peers, planes):
    per_plane = peers // planes
    moves = []
    for owner in range(peers):
        plane, row = divmod(owner, per_plane)
        for part in range(planes):
            spot = part * per_plane + row
            moves.append((owner * planes + part, spot * planes + plane))
    return moves


def on_device(queries, out_grads, owners, src_keys, src_values, states, kv_weight, src_lengths):
    cores, ys = lax.axis_size("grp"), lax.axis_size("mdl")
    peers = cores * XS * ZS
    tgt_len = queries.shape[1]
    moves = plane_moves(peers, ys)
    core, x, _, z = place()
    own = jnp.stack([core, x, z, jnp.int32(cores)]).astype(jnp.int32)

    piece = lax.ppermute(jnp.transpose(kv_weight, (1, 0, 2)), ALL, moves)
    packed = pack(own, owners, queries, out_grads, peers)
    got, states_all, weights_all = exchange(packed, states[0], piece, cores, ys)
    back, grads, grads_t = attend(got, src_lengths, src_keys[0], src_values[0])
    returned, state_out, weight_sum = finish(back, grads, grads_t, states_all, weights_all, cores, ys)
    weight_out = lax.ppermute(weight_sum, ALL, [(b, a) for a, b in moves])
    query_out = unpack(own, owners, returned, tgt_len)
    return (query_out, state_out[None], jnp.transpose(weight_out, (1, 0, 2)))


def solution(mesh):
    rows = P(ROWS, None, "mdl")
    return jax.shard_map(
        on_device,
        mesh=mesh,
        in_specs=(rows, rows, P(ROWS), rows, rows, rows, rows, P(ROWS)),
        out_specs=(rows, rows, rows),
        check_vma=False,
    )
```

```python
import functools
import math

import jax
import jax.numpy as jnp
from jax import lax
from jax.experimental import pallas as pl
from jax.experimental.pallas import tpu as pltpu
from jax.sharding import PartitionSpec as P

HEAD_DIM = 64
LANES = 128
ROWS = ("grp", "seq")
MESH = pl.DeviceIdType.MESH
XS, ZS, GROUPS = 4, 8, 4


def place():
    seq = lax.axis_index("seq")
    return lax.axis_index("grp"), lax.div(seq, ZS), lax.axis_index("mdl"), lax.rem(seq, ZS)


def in_plane(core, x, y, z, offset, cores):
    to_core = lax.rem(core + lax.div(offset, XS * ZS), cores)
    to_x = lax.rem(x + lax.rem(lax.div(offset, ZS), XS), XS)
    to_z = lax.rem(z + lax.rem(offset, ZS), ZS)
    return (to_core, to_x * ZS + to_z, y)


def back_in_plane(core, x, y, z, offset, cores):
    to_core = lax.rem(core + cores - lax.div(offset, XS * ZS), cores)
    to_x = lax.rem(x + XS - lax.rem(lax.div(offset, ZS), XS), XS)
    to_z = lax.rem(z + ZS - lax.rem(offset, ZS), ZS)
    return (to_core, to_x * ZS + to_z, y)


def partner_of(core, x, y, z):
    half = XS // 2
    to_x = lax.rem(y, 2) * half + lax.rem(x, half)
    return (lax.div(y, 2), to_x * ZS + z, core * 2 + lax.div(x, half))


def greet(core, x, y, z, cores, ys, partner, away):
    barrier = pltpu.get_barrier_semaphore()
    peers = cores * XS * ZS

    @pl.loop(1, peers)
    def _(offset):
        there = in_plane(core, x, y, z, offset, cores)
        pl.semaphore_signal(barrier, inc=1, device_id=there, device_id_type=MESH)

    @pl.loop(1, ys)
    def _(offset):
        there = (core, x * ZS + z, lax.rem(y + offset, ys))
        pl.semaphore_signal(barrier, inc=1, device_id=there, device_id_type=MESH)

    @pl.when(away)
    def _():
        pl.semaphore_signal(barrier, inc=1, device_id=partner, device_id_type=MESH)

    pl.semaphore_wait(barrier, peers + ys - 2 + away.astype(jnp.int32))


def send(source, target, send_sem, recv_sem, there):
    pltpu.make_async_remote_copy(
        src_ref=source,
        dst_ref=target,
        send_sem=send_sem,
        recv_sem=recv_sem,
        device_id=there,
        device_id_type=MESH,
    ).start()


def wait_bytes(ref, sem):
    pltpu.make_async_copy(ref, ref, sem).wait()


def dot(left, right, dims):
    return lax.dot_general(left, right, (dims, ((), ())), preferred_element_type=jnp.float32)


def peer_of(owner, place_ref):
    to_core = (lax.shift_right_logical(owner, 5) - place_ref[0]) & 1
    to_x = (lax.shift_right_logical(owner, 3) - place_ref[1]) & (XS - 1)
    to_z = (owner - place_ref[2]) & (ZS - 1)
    return (to_core * XS + to_x) * ZS + to_z


def pack_kernel(place_ref, owners_ref, query_ref, grad_ref, out_ref, first_ref, second_ref):
    peers = out_ref.shape[0]

    @pl.loop(0, peers, unroll=8)
    def _(peer):
        first_ref[peer] = -1
        second_ref[peer] = -1

    @pl.loop(0, query_ref.shape[0], unroll=4)
    def _(target):
        peer = peer_of(owners_ref[target], place_ref)
        first = first_ref[peer]
        first_ref[peer] = jnp.where(first < 0, target, first)
        second_ref[peer] = jnp.where(first < 0, -1, target)

    @pl.loop(0, peers, unroll=8)
    def _(peer):
        for kind, ref in enumerate((query_ref, grad_ref)):
            rows = []
            for target in (first_ref[peer], second_ref[peer]):
                row = ref[jnp.maximum(target, 0)]
                rows.append(jnp.where(target < 0, jnp.zeros_like(row), row))
            out_ref[peer, kind] = jnp.concatenate(rows, axis=0)


def pack(own, owners, queries, out_grads, peers):
    _, tgt_len, width = queries.shape
    smem, vmem = pl.BlockSpec(memory_space=pltpu.SMEM), pl.BlockSpec(memory_space=pltpu.VMEM)
    return pl.pallas_call(
        pack_kernel,
        out_shape=jax.ShapeDtypeStruct((peers, 2, 2 * tgt_len, width), queries.dtype),
        in_specs=[smem, smem, vmem, vmem],
        out_specs=vmem,
        scratch_shapes=[pltpu.SMEM((peers,), jnp.int32), pltpu.SMEM((peers,), jnp.int32)],
        name="pack_targets",
    )(own, owners, queries, out_grads)


def unpack_kernel(place_ref, owners_ref, back_ref, out_ref, used_ref, slot_ref):
    targets, tgt_len, _ = out_ref.shape

    @pl.loop(0, back_ref.shape[0], unroll=8)
    def _(peer):
        used_ref[peer] = 0

    @pl.loop(0, targets, unroll=4)
    def _(target):
        peer = peer_of(owners_ref[target], place_ref)
        used = used_ref[peer]
        used_ref[peer] = 1
        slot_ref[target] = peer * 2 + used

    @pl.loop(0, targets, unroll=8)
    def _(target):
        slot = slot_ref[target]
        both = back_ref[lax.shift_right_logical(slot, 1)]
        out_ref[target] = jnp.where((slot & 1) == 0, both[:tgt_len], both[tgt_len:])


def unpack(own, owners, returned, tgt_len):
    peers, _, width = returned.shape
    targets = owners.shape[0]
    smem, vmem = pl.BlockSpec(memory_space=pltpu.SMEM), pl.BlockSpec(memory_space=pltpu.VMEM)
    return pl.pallas_call(
        unpack_kernel,
        out_shape=jax.ShapeDtypeStruct((targets, tgt_len, width), returned.dtype),
        in_specs=[smem, smem, vmem],
        out_specs=vmem,
        scratch_shapes=[pltpu.SMEM((peers,), jnp.int32), pltpu.SMEM((targets,), jnp.int32)],
        name="unpack_targets",
    )(own, owners, returned)


def whole_kernel(
    cores,
    ys,
    length_ref,
    send_ref,
    key_hbm,
    value_hbm,
    states_hbm,
    piece_hbm,
    returned_ref,
    state_out,
    piece_out,
    got_ref,
    back_ref,
    key_ref,
    value_ref,
    key_t,
    key_sums,
    value_sums,
    grads,
    grads_t,
    all_states,
    all_weights,
    term_away,
    term_own,
    term_in,
    x_in,
    z_own,
    z_in,
    part,
    part_in,
    piece_away,
    row_in,
    row_out,
    gather_in,
    gather_out,
    sum_in,
    sum_out,
    own_sem,
):
    core, x, y, z = place()
    peers = cores * XS * ZS
    group = peers // GROUPS
    partner = partner_of(core, x, y, z)
    away = partner[2] != y
    src_len, width = key_ref.shape
    unit_rows, features = term_own.shape[3:]
    half_rows = ZS * unit_rows
    scale = HEAD_DIM**-0.5
    exp_scale = scale * math.log2(math.e)
    rows = group * got_ref.shape[2]

    own_keys = pltpu.make_async_copy(key_hbm, key_ref, own_sem.at[0])
    own_values = pltpu.make_async_copy(value_hbm, value_ref, own_sem.at[1])
    own_states = pltpu.make_async_copy(states_hbm, all_states.at[y], own_sem.at[2])
    own_rows = pltpu.make_async_copy(send_ref.at[0], got_ref.at[0], own_sem.at[3])
    for copy in (own_keys, own_values, own_states, own_rows):
        copy.start()
    greet(core, x, y, z, cores, ys, partner, away)

    own_weight = all_weights.at[core, x, z]
    own_piece = pltpu.make_async_copy(piece_hbm, own_weight, own_sem.at[4])

    @pl.when(away)
    def _():
        there = partner_of(core, x, y, z)
        to_core, to_seq = there[0], there[1]
        target = all_weights.at[to_core, lax.div(to_seq, ZS), lax.rem(to_seq, ZS)]
        send(piece_hbm, target, gather_out.at[0], gather_in.at[0], there)

    @pl.when(jnp.logical_not(away))
    def _():
        own_piece.start()

    def dispatch(first, last):
        @pl.loop(first, last)
        def _(offset):
            there = in_plane(core, x, y, z, offset, cores)
            at = lax.div(offset, group)
            send(send_ref.at[offset], got_ref.at[offset], row_out.at[0], row_in.at[at], there)

    dispatch(1, group)

    @pl.loop(1, ys)
    def _(offset):
        there = (core, x * ZS + z, lax.rem(y + offset, ys))
        send(states_hbm, all_states.at[y], gather_out.at[1], gather_in.at[1], there)

    @pl.when(away)
    def _():
        wait_bytes(own_weight, gather_in.at[0])
        wait_bytes(own_weight, gather_out.at[0])

    @pl.when(jnp.logical_not(away))
    def _():
        own_piece.wait()

    @pl.loop(1, ZS)
    def _(offset):
        there = (core, x * ZS + lax.rem(z + offset, ZS), y)
        send(own_weight, own_weight, gather_out.at[2], gather_in.at[2], there)

    dispatch(group, 2 * group)
    key_sums[...] = jnp.zeros_like(key_sums)
    value_sums[...] = jnp.zeros_like(value_sums)
    own_keys.wait()
    own_values.wait()
    key_t[...] = jnp.transpose(key_ref[...])
    own_rows.wait()
    wait_bytes(all_weights.at[0, 0, pl.ds(0, ZS - 1)], gather_in.at[2])

    @pl.loop(1, XS)
    def _(offset):
        there = (core, lax.rem(x + offset, XS) * ZS + z, y)
        line = all_weights.at[core, x]
        send(line, line, gather_out.at[3], gather_in.at[3], there)

    def give_back(first, last):
        @pl.loop(first, last)
        def _(offset):
            there = back_in_plane(core, x, y, z, offset, cores)
            send(back_ref.at[offset], returned_ref.at[offset], row_out.at[1], row_in.at[GROUPS], there)

    @pl.loop(0, GROUPS)
    def _(step):
        start = step * group

        @pl.when(step == 0)
        def _():
            wait_bytes(got_ref.at[pl.ds(1, group - 1)], row_in.at[0])

        @pl.when(step > 0)
        def _():
            wait_bytes(got_ref.at[pl.ds(start, group)], row_in.at[step])

        @pl.when(step < GROUPS - 2)
        def _():
            dispatch((step + 2) * group, (step + 3) * group)

        @pl.when(step == GROUPS - 2)
        def _():
            wait_bytes(all_weights.at[0, pl.ds(0, XS - 1)], gather_in.at[3])

            @pl.loop(1, cores)
            def _(offset):
                there = (lax.rem(core + offset, cores), x * ZS + z, y)
                half = all_weights.at[core]
                send(half, half, gather_out.at[4], gather_in.at[4], there)

        @pl.when(step == GROUPS - 1)
        def _():
            give_back(1, (GROUPS - 1) * group)

        valid = lax.broadcasted_iota(jnp.int32, (src_len, rows), 0) < length_ref[0]
        lane = lax.broadcasted_iota(jnp.int32, (rows, LANES), 1)
        for pair in range(width // LANES):
            at = slice(pair * LANES, (pair + 1) * LANES)
            query = got_ref[pl.ds(start, group), 0, :, at].reshape(rows, LANES)
            grad = got_ref[pl.ds(start, group), 1, :, at].reshape(rows, LANES)
            keys = key_ref[:, at]
            values = value_ref[:, at]
            key_sum = key_sums[:, at]
            value_sum = value_sums[:, at]
            back = []
            for half in range(LANES // HEAD_DIM):
                own = (lane >= half * HEAD_DIM) & (lane < (half + 1) * HEAD_DIM)
                query_h = jnp.where(own, query, jnp.zeros_like(query))
                grad_h = jnp.where(own, grad, jnp.zeros_like(grad))
                scores = dot(keys, query_h, ((1,), (1,)))
                scores = jnp.where(valid, scores, -1e30)
                peak = jnp.max(scores, axis=0, keepdims=True)
                terms = jnp.exp2((scores - peak) * exp_scale)
                probs = terms * (1.0 / jnp.sum(terms, axis=0, keepdims=True))
                probs_b = probs.astype(jnp.bfloat16)
                prob_grad = dot(values, grad_h, ((1,), (1,)))
                delta = jnp.sum(probs_b.astype(jnp.float32) * prob_grad, axis=0, keepdims=True)
                score_grad = (probs * (prob_grad - delta)).astype(jnp.bfloat16)
                key_sum = key_sum + dot(score_grad, query_h, ((1,), (0,)))
                value_sum = value_sum + dot(probs_b, grad_h, ((1,), (0,)))
                head = pair * LANES + half * HEAD_DIM
                back.append(dot(key_t[head : head + HEAD_DIM, :], score_grad, ((1,), (0,))))
            key_sums[:, at] = key_sum
            value_sums[:, at] = value_sum
            back = jnp.concatenate(back, axis=0) * scale
            back = jnp.transpose(back).astype(jnp.bfloat16)
            back_ref[pl.ds(start, group), :, at] = back.reshape(group, rows // group, LANES)

    def weight_terms(kind, to_core, target):
        @pl.loop(0, XS)
        def _(to_x):
            block = to_core * (XS // 2) + lax.div(to_x, 2)
            first = pl.multiple_of(lax.rem(to_x, 2) * half_rows, half_rows)
            terms = dot(grads_t[kind, pl.ds(first, half_rows), :], all_states[block], ((1,), (0,)))
            target[kind, to_x] = terms.astype(jnp.bfloat16).reshape(ZS, unit_rows, features)

    own_states.wait()
    wait_bytes(all_states.at[pl.ds(0, ys - 1)], gather_in.at[1])
    sibling = lax.rem(core + 1, cores)
    for kind in range(2):
        sums = key_sums[...] * scale if kind == 0 else value_sums[...]
        grads_t[kind] = jnp.transpose(sums).astype(jnp.bfloat16)
        weight_terms(kind, sibling, term_away)
        there = (sibling, x * ZS + z, y)
        send(term_away.at[kind], term_in.at[kind], sum_out.at[kind], sum_in.at[kind], there)
    for kind in range(2):
        weight_terms(kind, core, term_own)
        wait_bytes(term_in.at[kind], sum_in.at[kind])

        @pl.loop(0, XS)
        def _(to_x):
            both = term_own[kind, to_x].astype(jnp.float32) + term_in[kind, to_x].astype(jnp.float32)
            term_own[kind, to_x] = both.astype(jnp.bfloat16)

        @pl.loop(1, XS)
        def _(offset):
            to_x = lax.rem(x + offset, XS)
            there = (core, to_x * ZS + z, y)
            rows_x = term_own.at[kind, to_x]
            send(rows_x, x_in.at[kind, offset - 1], sum_out.at[2 + kind], sum_in.at[2 + kind], there)

    give_back((GROUPS - 1) * group, peers)
    returned_ref[0] = back_ref[0]

    grads[0] = (key_sums[...] * scale).astype(jnp.bfloat16)
    grads[1] = value_sums[...].astype(jnp.bfloat16)
    wait_bytes(all_weights.at[pl.ds(0, cores - 1)], gather_in.at[4])

    def state_terms(block, target):
        for kind in range(2):
            lines = all_weights[lax.div(block, 2), pl.ds(lax.rem(block, 2) * 2, 2), :, kind]
            terms = dot(grads[kind], lines.reshape(width, features), ((1,), (0,)))
            total = terms if kind == 0 else total + terms
        target[...] = total.astype(jnp.bfloat16)

    @pl.loop(1, ys)
    def _(offset):
        to_y = lax.rem(y + offset, ys)
        state_terms(to_y, part.at[offset])
        there = (core, x * ZS + z, to_y)
        send(part.at[offset], part_in.at[offset - 1], sum_out.at[6], sum_in.at[6], there)

    state_terms(y, part.at[0])
    for kind in range(2):
        wait_bytes(x_in.at[kind], sum_in.at[2 + kind])

        @pl.loop(0, ZS)
        def _(to_z):
            total = term_own[kind, x, to_z].astype(jnp.float32)
            for other in range(XS - 1):
                total = total + x_in[kind, other, to_z].astype(jnp.float32)
            z_own[kind, to_z] = total.astype(jnp.bfloat16)

        @pl.loop(1, ZS)
        def _(offset):
            to_z = lax.rem(z + offset, ZS)
            there = (core, x * ZS + to_z, y)
            piece = z_own.at[kind, to_z]
            send(piece, z_in.at[kind, offset - 1], sum_out.at[4 + kind], sum_in.at[4 + kind], there)

    wait_bytes(part_in, sum_in.at[6])
    total = part[0].astype(jnp.float32)
    for other in range(ys - 1):
        total = total + part_in[other].astype(jnp.float32)
    state_out[...] = total.astype(jnp.bfloat16)

    for kind in range(2):
        wait_bytes(z_in.at[kind], sum_in.at[4 + kind])
        total = z_own[kind, z].astype(jnp.float32)
        for other in range(ZS - 1):
            total = total + z_in[kind, other].astype(jnp.float32)
        piece_away[kind] = total

    @pl.when(away)
    def _():
        send(piece_away, piece_out, sum_out.at[7], sum_in.at[7], partner_of(core, x, y, z))
        wait_bytes(piece_out, sum_in.at[7])
        wait_bytes(piece_away, sum_out.at[7])

    @pl.when(jnp.logical_not(away))
    def _():
        piece_out[...] = piece_away[...]

    wait_bytes(returned_ref.at[pl.ds(1, peers - 1)], row_in.at[GROUPS])
    wait_bytes(send_ref.at[pl.ds(1, peers - 1)], row_out.at[0])
    wait_bytes(back_ref.at[pl.ds(1, peers - 1)], row_out.at[1])
    wait_bytes(all_states.at[pl.ds(0, ys - 1)], gather_out.at[1])
    wait_bytes(all_weights.at[0, 0, pl.ds(0, ZS - 1)], gather_out.at[2])
    wait_bytes(all_weights.at[0, pl.ds(0, XS - 1)], gather_out.at[3])
    wait_bytes(all_weights.at[pl.ds(0, cores - 1)], gather_out.at[4])
    for kind in range(2):
        wait_bytes(term_away.at[kind], sum_out.at[kind])
        wait_bytes(x_in.at[kind], sum_out.at[2 + kind])
        wait_bytes(z_in.at[kind], sum_out.at[4 + kind])
    wait_bytes(part_in, sum_out.at[6])


def whole(length, packed, keys, values, states, piece, cores, ys):
    smem, vmem = pl.BlockSpec(memory_space=pltpu.SMEM), pl.BlockSpec(memory_space=pltpu.VMEM)
    hbm = pl.BlockSpec(memory_space=pl.ANY)
    wire = packed.dtype
    peers, _, peer_rows, width = packed.shape
    src_len, features = states.shape
    unit_rows = piece.shape[1]
    terms = (2, XS, ZS, unit_rows, features)
    return pl.pallas_call(
        functools.partial(whole_kernel, cores, ys),
        out_shape=(
            jax.ShapeDtypeStruct((peers, peer_rows, width), wire),
            jax.ShapeDtypeStruct((src_len, features), wire),
            jax.ShapeDtypeStruct(piece.shape, jnp.float32),
        ),
        in_specs=[smem, vmem, hbm, hbm, hbm, hbm],
        out_specs=(vmem, vmem, vmem),
        scratch_shapes=[
            pltpu.VMEM(packed.shape, wire),
            pltpu.VMEM((peers, peer_rows, width), wire),
            pltpu.VMEM((src_len, width), wire),
            pltpu.VMEM((src_len, width), wire),
            pltpu.VMEM((width, src_len), wire),
            pltpu.VMEM((src_len, width), jnp.float32),
            pltpu.VMEM((src_len, width), jnp.float32),
            pltpu.VMEM((2, src_len, width), wire),
            pltpu.VMEM((2, width, src_len), wire),
            pltpu.VMEM((ys, src_len, features), wire),
            pltpu.VMEM((cores, XS, ZS, *piece.shape), wire),
            pltpu.VMEM(terms, wire),
            pltpu.VMEM(terms, wire),
            pltpu.VMEM(terms, wire),
            pltpu.VMEM((2, XS - 1, *terms[2:]), wire),
            pltpu.VMEM((2, *terms[2:]), wire),
            pltpu.VMEM((2, ZS - 1, *terms[3:]), wire),
            pltpu.VMEM((ys, src_len, features), wire),
            pltpu.VMEM((ys - 1, src_len, features), wire),
            pltpu.VMEM(piece.shape, jnp.float32),
            pltpu.SemaphoreType.DMA((GROUPS + 1,)),
            pltpu.SemaphoreType.DMA((2,)),
            pltpu.SemaphoreType.DMA((5,)),
            pltpu.SemaphoreType.DMA((5,)),
            pltpu.SemaphoreType.DMA((8,)),
            pltpu.SemaphoreType.DMA((8,)),
            pltpu.SemaphoreType.DMA((5,)),
        ],
        compiler_params=pltpu.CompilerParams(
            collective_id=1, has_side_effects=True, vmem_limit_bytes=56 << 20
        ),
        name="exchange_attend_reduce",
    )(length, packed, keys, values, states, piece)


def on_device(queries, out_grads, owners, src_keys, src_values, states, kv_weight, src_lengths):
    cores, ys = lax.axis_size("grp"), lax.axis_size("mdl")
    peers = cores * XS * ZS
    tgt_len = queries.shape[1]
    core, x, _, z = place()
    own = jnp.stack([core, x, z]).astype(jnp.int32)
    packed = pack(own, owners, queries, out_grads, peers)
    piece = jnp.transpose(kv_weight, (1, 0, 2))
    returned, state_out, weight_out = whole(
        src_lengths, packed, src_keys[0], src_values[0], states[0], piece, cores, ys
    )
    query_out = unpack(own, owners, returned, tgt_len)
    return (query_out, state_out[None], jnp.transpose(weight_out, (1, 0, 2)))


def solution(mesh):
    rows = P(ROWS, None, "mdl")
    return jax.shard_map(
        on_device,
        mesh=mesh,
        in_specs=(rows, rows, P(ROWS), rows, rows, rows, rows, P(ROWS)),
        out_specs=(rows, rows, rows),
        check_vma=False,
    )
```

```python
import functools
import math

import jax
import jax.numpy as jnp
from jax import lax
from jax.experimental import pallas as pl
from jax.experimental.pallas import tpu as pltpu
from jax.sharding import PartitionSpec as P

HEAD_DIM = 64
LANES = 128
ROWS = ("grp", "seq")
MESH = pl.DeviceIdType.MESH
XS, ZS, GROUPS = 4, 8, 4


def place():
    seq = lax.axis_index("seq")
    return lax.axis_index("grp"), lax.div(seq, ZS), lax.axis_index("mdl"), lax.rem(seq, ZS)


def in_plane(core, x, y, z, offset, cores):
    to_core = lax.rem(core + lax.div(offset, XS * ZS), cores)
    to_x = lax.rem(x + lax.rem(lax.div(offset, ZS), XS), XS)
    to_z = lax.rem(z + lax.rem(offset, ZS), ZS)
    return (to_core, to_x * ZS + to_z, y)


def back_in_plane(core, x, y, z, offset, cores):
    to_core = lax.rem(core + cores - lax.div(offset, XS * ZS), cores)
    to_x = lax.rem(x + XS - lax.rem(lax.div(offset, ZS), XS), XS)
    to_z = lax.rem(z + ZS - lax.rem(offset, ZS), ZS)
    return (to_core, to_x * ZS + to_z, y)


def partner_of(core, x, y, z):
    half = XS // 2
    to_x = lax.rem(y, 2) * half + lax.rem(x, half)
    return (lax.div(y, 2), to_x * ZS + z, core * 2 + lax.div(x, half))


def in_column(partner, z, offset):
    return (partner[0], lax.div(partner[1], ZS) * ZS + lax.rem(z + offset, ZS), partner[2])


def greet(core, x, y, z, cores, ys, partner, away):
    barrier = pltpu.get_barrier_semaphore()
    peers = cores * XS * ZS

    @pl.loop(1, peers)
    def _(offset):
        there = in_plane(core, x, y, z, offset, cores)
        pl.semaphore_signal(barrier, inc=1, device_id=there, device_id_type=MESH)

    @pl.loop(1, ys)
    def _(offset):
        there = (core, x * ZS + z, lax.rem(y + offset, ys))
        pl.semaphore_signal(barrier, inc=1, device_id=there, device_id_type=MESH)

    @pl.when(away)
    def _():
        @pl.loop(0, ZS)
        def _(offset):
            there = in_column(partner, z, offset)
            pl.semaphore_signal(barrier, inc=1, device_id=there, device_id_type=MESH)

    pl.semaphore_wait(barrier, peers + ys - 2 + ZS * away.astype(jnp.int32))


def send(source, target, send_sem, recv_sem, there):
    pltpu.make_async_remote_copy(
        src_ref=source,
        dst_ref=target,
        send_sem=send_sem,
        recv_sem=recv_sem,
        device_id=there,
        device_id_type=MESH,
    ).start()


def wait_bytes(ref, sem):
    pltpu.make_async_copy(ref, ref, sem).wait()


def dot(left, right, dims):
    return lax.dot_general(left, right, (dims, ((), ())), preferred_element_type=jnp.float32)


def peer_of(owner, core, x, z):
    to_core = (lax.shift_right_logical(owner, 5) - core) & 1
    to_x = (lax.shift_right_logical(owner, 3) - x) & (XS - 1)
    to_z = (owner - z) & (ZS - 1)
    return (to_core * XS + to_x) * ZS + to_z


def pack_kernel(owners_ref, query_ref, grad_ref, out_ref, first_ref, second_ref):
    peers = out_ref.shape[0]
    core, x, _, z = place()

    @pl.loop(0, peers, unroll=8)
    def _(peer):
        first_ref[peer] = -1
        second_ref[peer] = -1

    @pl.loop(0, query_ref.shape[0], unroll=4)
    def _(target):
        peer = peer_of(owners_ref[target], core, x, z)
        first = first_ref[peer]
        first_ref[peer] = jnp.where(first < 0, target, first)
        second_ref[peer] = jnp.where(first < 0, -1, target)

    @pl.loop(0, peers, unroll=8)
    def _(peer):
        for kind, ref in enumerate((query_ref, grad_ref)):
            rows = []
            for target in (first_ref[peer], second_ref[peer]):
                row = ref[jnp.maximum(target, 0)]
                rows.append(jnp.where(target < 0, jnp.zeros_like(row), row))
            out_ref[peer, kind] = jnp.concatenate(rows, axis=0)


def pack(owners, queries, out_grads, peers):
    _, tgt_len, width = queries.shape
    smem, vmem = pl.BlockSpec(memory_space=pltpu.SMEM), pl.BlockSpec(memory_space=pltpu.VMEM)
    return pl.pallas_call(
        pack_kernel,
        out_shape=jax.ShapeDtypeStruct((peers, 2, 2 * tgt_len, width), queries.dtype),
        in_specs=[smem, vmem, vmem],
        out_specs=vmem,
        scratch_shapes=[pltpu.SMEM((peers,), jnp.int32), pltpu.SMEM((peers,), jnp.int32)],
        name="pack_targets",
    )(owners, queries, out_grads)


def unpack_kernel(
    owners_ref, back_ref, state_ref, weight_ref, out_ref, state_out, weight_out, used_ref, slot_ref
):
    targets, tgt_len, _ = out_ref.shape
    core, x, _, z = place()

    @pl.loop(0, back_ref.shape[0], unroll=8)
    def _(peer):
        used_ref[peer] = 0

    @pl.loop(0, targets, unroll=4)
    def _(target):
        peer = peer_of(owners_ref[target], core, x, z)
        used = used_ref[peer]
        used_ref[peer] = 1
        slot_ref[target] = peer * 2 + used

    @pl.loop(0, targets, unroll=8)
    def _(target):
        slot = slot_ref[target]
        both = back_ref[lax.shift_right_logical(slot, 1)]
        out_ref[target] = jnp.where((slot & 1) == 0, both[:tgt_len], both[tgt_len:])

    state_out[0] = state_ref[...]
    for kind in range(2):
        weight_out[:, kind, :] = weight_ref[kind]


def unpack(owners, returned, state, weight, tgt_len):
    peers, _, width = returned.shape
    targets = owners.shape[0]
    kinds, unit_rows, features = weight.shape
    smem, vmem = pl.BlockSpec(memory_space=pltpu.SMEM), pl.BlockSpec(memory_space=pltpu.VMEM)
    return pl.pallas_call(
        unpack_kernel,
        out_shape=(
            jax.ShapeDtypeStruct((targets, tgt_len, width), returned.dtype),
            jax.ShapeDtypeStruct((1, *state.shape), state.dtype),
            jax.ShapeDtypeStruct((unit_rows, kinds, features), weight.dtype),
        ),
        in_specs=[smem, vmem, vmem, vmem],
        out_specs=(vmem, vmem, vmem),
        scratch_shapes=[pltpu.SMEM((peers,), jnp.int32), pltpu.SMEM((targets,), jnp.int32)],
        name="unpack_targets",
    )(owners, returned, state, weight)


def whole_kernel(
    cores,
    ys,
    length_ref,
    send_ref,
    key_hbm,
    value_hbm,
    states_hbm,
    weight_ref,
    returned_ref,
    state_out,
    piece_out,
    got_ref,
    back_ref,
    key_ref,
    value_ref,
    key_t,
    key_sums,
    value_sums,
    grads,
    grads_t,
    all_states,
    all_weights,
    term_away,
    term_own,
    term_in,
    x_in,
    z_own,
    z_in,
    part,
    part_in,
    piece_away,
    piece_ref,
    row_in,
    row_out,
    gather_in,
    gather_out,
    sum_in,
    sum_out,
    own_sem,
):
    core, x, y, z = place()
    peers = cores * XS * ZS
    group = peers // GROUPS
    partner = partner_of(core, x, y, z)
    away = partner[2] != y
    src_len, width = key_ref.shape
    unit_rows, features = term_own.shape[3:]
    half_rows = ZS * unit_rows
    scale = HEAD_DIM**-0.5
    exp_scale = scale * math.log2(math.e)
    rows = group * got_ref.shape[2]

    own_keys = pltpu.make_async_copy(key_hbm, key_ref, own_sem.at[0])
    own_values = pltpu.make_async_copy(value_hbm, value_ref, own_sem.at[1])
    own_states = pltpu.make_async_copy(states_hbm, all_states.at[y], own_sem.at[2])
    own_rows = pltpu.make_async_copy(send_ref.at[0], got_ref.at[0], own_sem.at[3])
    for copy in (own_keys, own_values, own_states, own_rows):
        copy.start()
    for kind in range(2):
        piece_ref[kind] = weight_ref[:, kind, :]
    greet(core, x, y, z, cores, ys, partner, away)

    to_core, to_x = partner[0], lax.div(partner[1], ZS)
    own_piece = pltpu.make_async_copy(piece_ref, all_weights.at[core, x, z], own_sem.at[4])

    @pl.loop(1, ZS)
    def _(offset):
        there = in_column(partner, z, offset)
        send(piece_ref, all_weights.at[to_core, to_x, z], gather_out.at[2], gather_in.at[2], there)

    @pl.when(away)
    def _():
        there = partner_of(core, x, y, z)
        send(piece_ref, all_weights.at[to_core, to_x, z], gather_out.at[0], gather_in.at[0], there)

    @pl.when(jnp.logical_not(away))
    def _():
        own_piece.start()

    @pl.loop(1, ys)
    def _(offset):
        there = (core, x * ZS + z, lax.rem(y + offset, ys))
        send(states_hbm, all_states.at[y], gather_out.at[1], gather_in.at[1], there)

    def dispatch(first, last):
        @pl.loop(first, last)
        def _(offset):
            there = in_plane(core, x, y, z, offset, cores)
            at = lax.div(offset, group)
            send(send_ref.at[offset], got_ref.at[offset], row_out.at[0], row_in.at[at], there)

    dispatch(1, 2 * group)
    key_sums[...] = jnp.zeros_like(key_sums)
    value_sums[...] = jnp.zeros_like(value_sums)
    own_keys.wait()
    own_values.wait()
    key_t[...] = jnp.transpose(key_ref[...])
    own_rows.wait()

    @pl.when(away)
    def _():
        wait_bytes(piece_ref, gather_in.at[0])
        wait_bytes(piece_ref, gather_out.at[0])

    @pl.when(jnp.logical_not(away))
    def _():
        own_piece.wait()

    wait_bytes(all_weights.at[0, 0, pl.ds(0, ZS - 1)], gather_in.at[2])

    @pl.loop(1, XS)
    def _(offset):
        there = (core, lax.rem(x + offset, XS) * ZS + z, y)
        line = all_weights.at[core, x]
        send(line, line, gather_out.at[3], gather_in.at[3], there)

    def give_back(first, last):
        @pl.loop(first, last)
        def _(offset):
            there = back_in_plane(core, x, y, z, offset, cores)
            send(back_ref.at[offset], returned_ref.at[offset], row_out.at[1], row_in.at[GROUPS], there)

    @pl.loop(0, GROUPS)
    def _(step):
        start = step * group

        @pl.when(step == 0)
        def _():
            wait_bytes(got_ref.at[pl.ds(1, group - 1)], row_in.at[0])

        @pl.when(step > 0)
        def _():
            wait_bytes(got_ref.at[pl.ds(start, group)], row_in.at[step])

        @pl.when(step < GROUPS - 2)
        def _():
            dispatch((step + 2) * group, (step + 3) * group)

        @pl.when(step == GROUPS - 2)
        def _():
            wait_bytes(all_weights.at[0, pl.ds(0, XS - 1)], gather_in.at[3])

            @pl.loop(1, cores)
            def _(offset):
                there = (lax.rem(core + offset, cores), x * ZS + z, y)
                half = all_weights.at[core]
                send(half, half, gather_out.at[4], gather_in.at[4], there)

        @pl.when(step == GROUPS - 1)
        def _():
            give_back(1, (GROUPS - 1) * group)

        valid = lax.broadcasted_iota(jnp.int32, (src_len, rows), 0) < length_ref[0]
        lane = lax.broadcasted_iota(jnp.int32, (rows, LANES), 1)
        for pair in range(width // LANES):
            at = slice(pair * LANES, (pair + 1) * LANES)
            query = got_ref[pl.ds(start, group), 0, :, at].reshape(rows, LANES)
            grad = got_ref[pl.ds(start, group), 1, :, at].reshape(rows, LANES)
            keys = key_ref[:, at]
            values = value_ref[:, at]
            key_sum = key_sums[:, at]
            value_sum = value_sums[:, at]
            back = []
            for half in range(LANES // HEAD_DIM):
                own = (lane >= half * HEAD_DIM) & (lane < (half + 1) * HEAD_DIM)
                query_h = jnp.where(own, query, jnp.zeros_like(query))
                grad_h = jnp.where(own, grad, jnp.zeros_like(grad))
                scores = dot(keys, query_h, ((1,), (1,)))
                scores = jnp.where(valid, scores, -1e30)
                peak = jnp.max(scores, axis=0, keepdims=True)
                terms = jnp.exp2((scores - peak) * exp_scale)
                probs = terms * (1.0 / jnp.sum(terms, axis=0, keepdims=True))
                probs_b = probs.astype(jnp.bfloat16)
                prob_grad = dot(values, grad_h, ((1,), (1,)))
                delta = jnp.sum(probs_b.astype(jnp.float32) * prob_grad, axis=0, keepdims=True)
                score_grad = (probs * (prob_grad - delta)).astype(jnp.bfloat16)
                key_sum = key_sum + dot(score_grad, query_h, ((1,), (0,)))
                value_sum = value_sum + dot(probs_b, grad_h, ((1,), (0,)))
                head = pair * LANES + half * HEAD_DIM
                back.append(dot(key_t[head : head + HEAD_DIM, :], score_grad, ((1,), (0,))))
            key_sums[:, at] = key_sum
            value_sums[:, at] = value_sum
            back = jnp.concatenate(back, axis=0) * scale
            back = jnp.transpose(back).astype(jnp.bfloat16)
            back_ref[pl.ds(start, group), :, at] = back.reshape(group, rows // group, LANES)

    def weight_terms(kind, to_core, target, added):
        @pl.loop(0, XS)
        def _(to_x):
            block = to_core * (XS // 2) + lax.div(to_x, 2)
            first = pl.multiple_of(lax.rem(to_x, 2) * half_rows, half_rows)
            terms = dot(grads_t[kind, pl.ds(first, half_rows), :], all_states[block], ((1,), (0,)))
            if added is not None:
                terms = terms + added[kind, to_x].reshape(half_rows, features).astype(jnp.float32)
            target[kind, to_x] = terms.astype(jnp.bfloat16).reshape(ZS, unit_rows, features)

    own_states.wait()
    wait_bytes(all_states.at[pl.ds(0, ys - 1)], gather_in.at[1])
    sibling = lax.rem(core + 1, cores)
    for kind in range(2):
        sums = key_sums[...] * scale if kind == 0 else value_sums[...]
        grads[kind] = sums.astype(jnp.bfloat16)
        grads_t[kind] = jnp.transpose(grads[kind])
        weight_terms(kind, sibling, term_away, None)
        there = (sibling, x * ZS + z, y)
        send(term_away.at[kind], term_in.at[kind], sum_out.at[kind], sum_in.at[kind], there)

    wait_bytes(all_weights.at[pl.ds(0, cores - 1)], gather_in.at[4])

    def state_terms(block, target):
        for kind in range(2):
            lines = all_weights[lax.div(block, 2), pl.ds(lax.rem(block, 2) * 2, 2), :, kind]
            terms = dot(grads[kind], lines.reshape(width, features), ((1,), (0,)))
            total = terms if kind == 0 else total + terms
        target[...] = total.astype(jnp.bfloat16)

    def state_send(offset):
        to_y = lax.rem(y + offset, ys)
        state_terms(to_y, part.at[offset])
        there = (core, x * ZS + z, to_y)
        send(part.at[offset], part_in.at[offset - 1], sum_out.at[6], sum_in.at[6], there)

    pl.loop(1, ys)(state_send)

    for kind in range(2):
        wait_bytes(term_in.at[kind], sum_in.at[kind])
        weight_terms(kind, core, term_own, term_in)

        @pl.loop(1, XS)
        def _(offset):
            to_x = lax.rem(x + offset, XS)
            there = (core, to_x * ZS + z, y)
            rows_x = term_own.at[kind, to_x]
            send(rows_x, x_in.at[kind, offset - 1], sum_out.at[2 + kind], sum_in.at[2 + kind], there)

    give_back((GROUPS - 1) * group, peers)
    returned_ref[0] = back_ref[0]
    state_terms(y, part.at[0])
    for kind in range(2):
        wait_bytes(x_in.at[kind], sum_in.at[2 + kind])

        @pl.loop(0, ZS)
        def _(to_z):
            total = term_own[kind, x, to_z].astype(jnp.float32)
            for other in range(XS - 1):
                total = total + x_in[kind, other, to_z].astype(jnp.float32)
            z_own[kind, to_z] = total.astype(jnp.bfloat16)

        @pl.loop(1, ZS)
        def _(offset):
            to_z = lax.rem(z + offset, ZS)
            there = (core, x * ZS + to_z, y)
            piece = z_own.at[kind, to_z]
            send(piece, z_in.at[kind, offset - 1], sum_out.at[4 + kind], sum_in.at[4 + kind], there)

    wait_bytes(part_in, sum_in.at[6])
    total = part[0].astype(jnp.float32)
    for other in range(ys - 1):
        total = total + part_in[other].astype(jnp.float32)
    state_out[...] = total.astype(jnp.bfloat16)

    for kind in range(2):
        wait_bytes(z_in.at[kind], sum_in.at[4 + kind])
        total = z_own[kind, z].astype(jnp.float32)
        for other in range(ZS - 1):
            total = total + z_in[kind, other].astype(jnp.float32)
        piece_away[kind] = total

    @pl.when(away)
    def _():
        send(piece_away, piece_out, sum_out.at[7], sum_in.at[7], partner_of(core, x, y, z))
        wait_bytes(piece_out, sum_in.at[7])
        wait_bytes(piece_away, sum_out.at[7])

    @pl.when(jnp.logical_not(away))
    def _():
        piece_out[...] = piece_away[...]

    wait_bytes(returned_ref.at[pl.ds(1, peers - 1)], row_in.at[GROUPS])
    wait_bytes(send_ref.at[pl.ds(1, peers - 1)], row_out.at[0])
    wait_bytes(back_ref.at[pl.ds(1, peers - 1)], row_out.at[1])
    wait_bytes(all_states.at[pl.ds(0, ys - 1)], gather_out.at[1])
    wait_bytes(all_weights.at[0, 0, pl.ds(0, ZS - 1)], gather_out.at[2])
    wait_bytes(all_weights.at[0, pl.ds(0, XS - 1)], gather_out.at[3])
    wait_bytes(all_weights.at[pl.ds(0, cores - 1)], gather_out.at[4])
    for kind in range(2):
        wait_bytes(term_away.at[kind], sum_out.at[kind])
        wait_bytes(x_in.at[kind], sum_out.at[2 + kind])
        wait_bytes(z_in.at[kind], sum_out.at[4 + kind])
    wait_bytes(part_in, sum_out.at[6])


def whole(length, packed, keys, values, states, weights, cores, ys):
    smem, vmem = pl.BlockSpec(memory_space=pltpu.SMEM), pl.BlockSpec(memory_space=pltpu.VMEM)
    hbm = pl.BlockSpec(memory_space=pl.ANY)
    wire = packed.dtype
    peers, _, peer_rows, width = packed.shape
    src_len, features = states.shape
    unit_rows = weights.shape[0]
    piece = (2, unit_rows, features)
    terms = (2, XS, ZS, unit_rows, features)
    return pl.pallas_call(
        functools.partial(whole_kernel, cores, ys),
        out_shape=(
            jax.ShapeDtypeStruct((peers, peer_rows, width), wire),
            jax.ShapeDtypeStruct((src_len, features), wire),
            jax.ShapeDtypeStruct(piece, jnp.float32),
        ),
        in_specs=[smem, vmem, hbm, hbm, hbm, vmem],
        out_specs=(vmem, vmem, vmem),
        scratch_shapes=[
            pltpu.VMEM(packed.shape, wire),
            pltpu.VMEM((peers, peer_rows, width), wire),
            pltpu.VMEM((src_len, width), wire),
            pltpu.VMEM((src_len, width), wire),
            pltpu.VMEM((width, src_len), wire),
            pltpu.VMEM((src_len, width), jnp.float32),
            pltpu.VMEM((src_len, width), jnp.float32),
            pltpu.VMEM((2, src_len, width), wire),
            pltpu.VMEM((2, width, src_len), wire),
            pltpu.VMEM((ys, src_len, features), wire),
            pltpu.VMEM((cores, XS, ZS, *piece), wire),
            pltpu.VMEM(terms, wire),
            pltpu.VMEM(terms, wire),
            pltpu.VMEM(terms, wire),
            pltpu.VMEM((2, XS - 1, *terms[2:]), wire),
            pltpu.VMEM((2, *terms[2:]), wire),
            pltpu.VMEM((2, ZS - 1, *terms[3:]), wire),
            pltpu.VMEM((ys, src_len, features), wire),
            pltpu.VMEM((ys - 1, src_len, features), wire),
            pltpu.VMEM(piece, jnp.float32),
            pltpu.VMEM(piece, wire),
            pltpu.SemaphoreType.DMA((GROUPS + 1,)),
            pltpu.SemaphoreType.DMA((2,)),
            pltpu.SemaphoreType.DMA((5,)),
            pltpu.SemaphoreType.DMA((5,)),
            pltpu.SemaphoreType.DMA((8,)),
            pltpu.SemaphoreType.DMA((8,)),
            pltpu.SemaphoreType.DMA((5,)),
        ],
        compiler_params=pltpu.CompilerParams(
            collective_id=1, has_side_effects=True, vmem_limit_bytes=56 << 20
        ),
        name="exchange_attend_reduce",
    )(length, packed, keys, values, states, weights)


def on_device(queries, out_grads, owners, src_keys, src_values, states, kv_weight, src_lengths):
    cores, ys = lax.axis_size("grp"), lax.axis_size("mdl")
    peers = cores * XS * ZS
    tgt_len = queries.shape[1]
    packed = pack(owners, queries, out_grads, peers)
    returned, state_sum, weight_sum = whole(
        src_lengths, packed, src_keys[0], src_values[0], states[0], kv_weight, cores, ys
    )
    return unpack(owners, returned, state_sum, weight_sum, tgt_len)


def solution(mesh):
    rows = P(ROWS, None, "mdl")
    return jax.shard_map(
        on_device,
        mesh=mesh,
        in_specs=(rows, rows, P(ROWS), rows, rows, rows, rows, P(ROWS)),
        out_specs=(rows, rows, rows),
        check_vma=False,
    )
```

```python
import functools
import math

import jax
import jax.numpy as jnp
from jax import lax
from jax.experimental import pallas as pl
from jax.experimental.pallas import tpu as pltpu
from jax.sharding import PartitionSpec as P

HEAD_DIM = 64
LANES = 128
ROWS = ("grp", "seq")
MESH = pl.DeviceIdType.MESH
XS, ZS, GROUPS = 4, 8, 4


def place():
    seq = lax.axis_index("seq")
    return lax.axis_index("grp"), lax.div(seq, ZS), lax.axis_index("mdl"), lax.rem(seq, ZS)


def in_plane(core, x, y, z, offset, cores):
    to_core = lax.rem(core + lax.div(offset, XS * ZS), cores)
    to_x = lax.rem(x + lax.rem(lax.div(offset, ZS), XS), XS)
    to_z = lax.rem(z + lax.rem(offset, ZS), ZS)
    return (to_core, to_x * ZS + to_z, y)


def back_in_plane(core, x, y, z, offset, cores):
    to_core = lax.rem(core + cores - lax.div(offset, XS * ZS), cores)
    to_x = lax.rem(x + XS - lax.rem(lax.div(offset, ZS), XS), XS)
    to_z = lax.rem(z + ZS - lax.rem(offset, ZS), ZS)
    return (to_core, to_x * ZS + to_z, y)


def partner_of(core, x, y, z):
    half = XS // 2
    to_x = lax.rem(y, 2) * half + lax.rem(x, half)
    return (lax.div(y, 2), to_x * ZS + z, core * 2 + lax.div(x, half))


def in_column(partner, z, offset):
    return (partner[0], lax.div(partner[1], ZS) * ZS + lax.rem(z + offset, ZS), partner[2])


def greet(core, x, y, z, cores, ys, partner, away):
    barrier = pltpu.get_barrier_semaphore()
    peers = cores * XS * ZS

    @pl.loop(1, peers)
    def _(offset):
        there = in_plane(core, x, y, z, offset, cores)
        pl.semaphore_signal(barrier, inc=1, device_id=there, device_id_type=MESH)

    @pl.loop(1, ys)
    def _(offset):
        there = (core, x * ZS + z, lax.rem(y + offset, ys))
        pl.semaphore_signal(barrier, inc=1, device_id=there, device_id_type=MESH)

    @pl.when(away)
    def _():
        @pl.loop(0, ZS)
        def _(offset):
            there = in_column(partner, z, offset)
            pl.semaphore_signal(barrier, inc=1, device_id=there, device_id_type=MESH)

    pl.semaphore_wait(barrier, peers + ys - 2 + ZS * away.astype(jnp.int32))


def send(source, target, send_sem, recv_sem, there):
    pltpu.make_async_remote_copy(
        src_ref=source,
        dst_ref=target,
        send_sem=send_sem,
        recv_sem=recv_sem,
        device_id=there,
        device_id_type=MESH,
    ).start()


def wait_bytes(ref, sem):
    pltpu.make_async_copy(ref, ref, sem).wait()


def dot(left, right, dims):
    return lax.dot_general(left, right, (dims, ((), ())), preferred_element_type=jnp.float32)


def peer_of(owner, core, x, z):
    to_core = (lax.shift_right_logical(owner, 5) - core) & 1
    to_x = (lax.shift_right_logical(owner, 3) - x) & (XS - 1)
    to_z = (owner - z) & (ZS - 1)
    return (to_core * XS + to_x) * ZS + to_z


def pack_kernel(owners_ref, query_ref, grad_ref, out_ref, first_ref, second_ref):
    peers = out_ref.shape[0]
    core, x, _, z = place()

    @pl.loop(0, peers, unroll=8)
    def _(peer):
        first_ref[peer] = -1
        second_ref[peer] = -1

    @pl.loop(0, query_ref.shape[0], unroll=4)
    def _(target):
        peer = peer_of(owners_ref[target], core, x, z)
        first = first_ref[peer]
        first_ref[peer] = jnp.where(first < 0, target, first)
        second_ref[peer] = jnp.where(first < 0, -1, target)

    @pl.loop(0, peers, unroll=8)
    def _(peer):
        for kind, ref in enumerate((query_ref, grad_ref)):
            rows = []
            for target in (first_ref[peer], second_ref[peer]):
                row = ref[jnp.maximum(target, 0)]
                rows.append(jnp.where(target < 0, jnp.zeros_like(row), row))
            out_ref[peer, kind] = jnp.concatenate(rows, axis=0)


def pack(owners, queries, out_grads, peers):
    _, tgt_len, width = queries.shape
    smem, vmem = pl.BlockSpec(memory_space=pltpu.SMEM), pl.BlockSpec(memory_space=pltpu.VMEM)
    return pl.pallas_call(
        pack_kernel,
        out_shape=jax.ShapeDtypeStruct((peers, 2, 2 * tgt_len, width), queries.dtype),
        in_specs=[smem, vmem, vmem],
        out_specs=vmem,
        scratch_shapes=[pltpu.SMEM((peers,), jnp.int32), pltpu.SMEM((peers,), jnp.int32)],
        name="pack_targets",
    )(owners, queries, out_grads)


def unpack_kernel(
    owners_ref, back_ref, state_ref, weight_ref, out_ref, state_out, weight_out, used_ref, slot_ref
):
    targets, tgt_len, _ = out_ref.shape
    core, x, _, z = place()

    @pl.loop(0, back_ref.shape[0], unroll=8)
    def _(peer):
        used_ref[peer] = 0

    @pl.loop(0, targets, unroll=4)
    def _(target):
        peer = peer_of(owners_ref[target], core, x, z)
        used = used_ref[peer]
        used_ref[peer] = 1
        slot_ref[target] = peer * 2 + used

    @pl.loop(0, targets, unroll=8)
    def _(target):
        slot = slot_ref[target]
        both = back_ref[lax.shift_right_logical(slot, 1)]
        out_ref[target] = jnp.where((slot & 1) == 0, both[:tgt_len], both[tgt_len:])

    state_out[0] = state_ref[...]
    for kind in range(2):
        weight_out[:, kind, :] = weight_ref[kind]


def unpack(owners, returned, state, weight, tgt_len):
    peers, _, width = returned.shape
    targets = owners.shape[0]
    kinds, unit_rows, features = weight.shape
    smem, vmem = pl.BlockSpec(memory_space=pltpu.SMEM), pl.BlockSpec(memory_space=pltpu.VMEM)
    return pl.pallas_call(
        unpack_kernel,
        out_shape=(
            jax.ShapeDtypeStruct((targets, tgt_len, width), returned.dtype),
            jax.ShapeDtypeStruct((1, *state.shape), state.dtype),
            jax.ShapeDtypeStruct((unit_rows, kinds, features), weight.dtype),
        ),
        in_specs=[smem, vmem, vmem, vmem],
        out_specs=(vmem, vmem, vmem),
        scratch_shapes=[pltpu.SMEM((peers,), jnp.int32), pltpu.SMEM((targets,), jnp.int32)],
        name="unpack_targets",
    )(owners, returned, state, weight)


def whole_kernel(
    cores,
    ys,
    length_ref,
    send_ref,
    key_hbm,
    value_hbm,
    states_hbm,
    weight_ref,
    returned_ref,
    state_out,
    piece_out,
    got_ref,
    back_ref,
    key_ref,
    value_ref,
    key_t,
    key_sums,
    value_sums,
    grads,
    grads_t,
    all_states,
    all_weights,
    term_away,
    term_own,
    term_in,
    far_in,
    x_in,
    z_own,
    z_in,
    part,
    part_in,
    piece_away,
    piece_ref,
    row_in,
    row_out,
    gather_in,
    gather_out,
    sum_in,
    sum_out,
    own_sem,
):
    core, x, y, z = place()
    peers = cores * XS * ZS
    group = peers // GROUPS
    partner = partner_of(core, x, y, z)
    away = partner[2] != y
    src_len, width = key_ref.shape
    unit_rows, features = term_own.shape[3:]
    half_rows = ZS * unit_rows
    scale = HEAD_DIM**-0.5
    exp_scale = scale * math.log2(math.e)
    rows = group * got_ref.shape[2]

    own_keys = pltpu.make_async_copy(key_hbm, key_ref, own_sem.at[0])
    own_values = pltpu.make_async_copy(value_hbm, value_ref, own_sem.at[1])
    own_states = pltpu.make_async_copy(states_hbm, all_states.at[y], own_sem.at[2])
    own_rows = pltpu.make_async_copy(send_ref.at[0], got_ref.at[0], own_sem.at[3])
    for copy in (own_keys, own_values, own_states, own_rows):
        copy.start()
    for kind in range(2):
        piece_ref[kind] = weight_ref[:, kind, :]
    greet(core, x, y, z, cores, ys, partner, away)

    to_core, to_x = partner[0], lax.div(partner[1], ZS)
    own_piece = pltpu.make_async_copy(piece_ref, all_weights.at[core, x, z], own_sem.at[4])

    @pl.loop(1, ZS)
    def _(offset):
        there = in_column(partner, z, offset)
        send(piece_ref, all_weights.at[to_core, to_x, z], gather_out.at[2], gather_in.at[2], there)

    @pl.when(away)
    def _():
        there = partner_of(core, x, y, z)
        send(piece_ref, all_weights.at[to_core, to_x, z], gather_out.at[0], gather_in.at[0], there)

    @pl.when(jnp.logical_not(away))
    def _():
        own_piece.start()

    @pl.loop(1, ys)
    def _(offset):
        there = (core, x * ZS + z, lax.rem(y + offset, ys))
        send(states_hbm, all_states.at[y], gather_out.at[1], gather_in.at[1], there)

    def dispatch(first, last):
        @pl.loop(first, last)
        def _(offset):
            there = in_plane(core, x, y, z, offset, cores)
            at = lax.div(offset, group)
            send(send_ref.at[offset], got_ref.at[offset], row_out.at[0], row_in.at[at], there)

    dispatch(1, 2 * group)
    key_sums[...] = jnp.zeros_like(key_sums)
    value_sums[...] = jnp.zeros_like(value_sums)
    own_keys.wait()
    own_values.wait()
    key_t[...] = jnp.transpose(key_ref[...])
    own_rows.wait()

    @pl.when(away)
    def _():
        wait_bytes(piece_ref, gather_in.at[0])
        wait_bytes(piece_ref, gather_out.at[0])

    @pl.when(jnp.logical_not(away))
    def _():
        own_piece.wait()

    wait_bytes(all_weights.at[0, 0, pl.ds(0, ZS - 1)], gather_in.at[2])

    @pl.loop(1, XS)
    def _(offset):
        there = (core, lax.rem(x + offset, XS) * ZS + z, y)
        line = all_weights.at[core, x]
        send(line, line, gather_out.at[3], gather_in.at[3], there)

    def give_back(first, last):
        @pl.loop(first, last)
        def _(offset):
            there = back_in_plane(core, x, y, z, offset, cores)
            send(back_ref.at[offset], returned_ref.at[offset], row_out.at[1], row_in.at[GROUPS], there)

    @pl.loop(0, GROUPS)
    def _(step):
        start = step * group

        @pl.when(step == 0)
        def _():
            wait_bytes(got_ref.at[pl.ds(1, group - 1)], row_in.at[0])

        @pl.when(step > 0)
        def _():
            wait_bytes(got_ref.at[pl.ds(start, group)], row_in.at[step])

        @pl.when(step < GROUPS - 2)
        def _():
            dispatch((step + 2) * group, (step + 3) * group)

        @pl.when(step == GROUPS - 2)
        def _():
            wait_bytes(all_weights.at[0, pl.ds(0, XS - 1)], gather_in.at[3])

            @pl.loop(1, cores)
            def _(offset):
                there = (lax.rem(core + offset, cores), x * ZS + z, y)
                half = all_weights.at[core]
                send(half, half, gather_out.at[4], gather_in.at[4], there)

        @pl.when(step == GROUPS - 1)
        def _():
            give_back(1, (GROUPS - 1) * group)

        valid = lax.broadcasted_iota(jnp.int32, (src_len, rows), 0) < length_ref[0]
        lane = lax.broadcasted_iota(jnp.int32, (rows, LANES), 1)
        for pair in range(width // LANES):
            at = slice(pair * LANES, (pair + 1) * LANES)
            query = got_ref[pl.ds(start, group), 0, :, at].reshape(rows, LANES)
            grad = got_ref[pl.ds(start, group), 1, :, at].reshape(rows, LANES)
            keys = key_ref[:, at]
            values = value_ref[:, at]
            key_sum = key_sums[:, at]
            value_sum = value_sums[:, at]
            back = []
            for half in range(LANES // HEAD_DIM):
                own = (lane >= half * HEAD_DIM) & (lane < (half + 1) * HEAD_DIM)
                query_h = jnp.where(own, query, jnp.zeros_like(query))
                grad_h = jnp.where(own, grad, jnp.zeros_like(grad))
                scores = dot(keys, query_h, ((1,), (1,)))
                scores = jnp.where(valid, scores, -1e30)
                peak = jnp.max(scores, axis=0, keepdims=True)
                terms = jnp.exp2((scores - peak) * exp_scale)
                probs = terms * (1.0 / jnp.sum(terms, axis=0, keepdims=True))
                probs_b = probs.astype(jnp.bfloat16)
                prob_grad = dot(values, grad_h, ((1,), (1,)))
                delta = jnp.sum(probs_b.astype(jnp.float32) * prob_grad, axis=0, keepdims=True)
                score_grad = (probs * (prob_grad - delta)).astype(jnp.bfloat16)
                key_sum = key_sum + dot(score_grad, query_h, ((1,), (0,)))
                value_sum = value_sum + dot(probs_b, grad_h, ((1,), (0,)))
                head = pair * LANES + half * HEAD_DIM
                back.append(dot(key_t[head : head + HEAD_DIM, :], score_grad, ((1,), (0,))))
            key_sums[:, at] = key_sum
            value_sums[:, at] = value_sum
            back = jnp.concatenate(back, axis=0) * scale
            back = jnp.transpose(back).astype(jnp.bfloat16)
            back_ref[pl.ds(start, group), :, at] = back.reshape(group, rows // group, LANES)

    def weight_terms(kind, to_core, target, added, first_x, last_x):
        @pl.loop(first_x, last_x)
        def _(step_x):
            to_x = lax.rem(x + XS // 2 + step_x, XS)
            block = to_core * (XS // 2) + lax.div(to_x, 2)
            first = pl.multiple_of(lax.rem(to_x, 2) * half_rows, half_rows)
            terms = dot(grads_t[kind, pl.ds(first, half_rows), :], all_states[block], ((1,), (0,)))
            if added is not None:
                terms = terms + added[kind, to_x].reshape(half_rows, features).astype(jnp.float32)
            target[kind, to_x] = terms.astype(jnp.bfloat16).reshape(ZS, unit_rows, features)

    own_states.wait()
    wait_bytes(all_states.at[pl.ds(0, ys - 1)], gather_in.at[1])
    sibling = lax.rem(core + 1, cores)
    for kind in range(2):
        sums = key_sums[...] * scale if kind == 0 else value_sums[...]
        grads[kind] = sums.astype(jnp.bfloat16)
        grads_t[kind] = jnp.transpose(grads[kind])
        weight_terms(kind, sibling, term_away, None, 0, XS)
        there = (sibling, x * ZS + z, y)
        send(term_away.at[kind], term_in.at[kind], sum_out.at[kind], sum_in.at[kind], there)

    wait_bytes(all_weights.at[pl.ds(0, cores - 1)], gather_in.at[4])

    def state_terms(block, target):
        for kind in range(2):
            lines = all_weights[lax.div(block, 2), pl.ds(lax.rem(block, 2) * 2, 2), :, kind]
            terms = dot(grads[kind], lines.reshape(width, features), ((1,), (0,)))
            total = terms if kind == 0 else total + terms
        target[...] = total.astype(jnp.bfloat16)

    def state_send(offset):
        to_y = lax.rem(y + offset, ys)
        state_terms(to_y, part.at[offset])
        there = (core, x * ZS + z, to_y)
        send(part.at[offset], part_in.at[offset - 1], sum_out.at[6], sum_in.at[6], there)

    pl.loop(1, ys)(state_send)

    low, high = pl.ds(0, ZS // 2), pl.ds(ZS // 2, ZS // 2)
    right_x, far_x, left_x = (lax.rem(x + offset, XS) for offset in range(1, XS))

    def x_send(source, target, sem, to_x):
        send(source, target, sum_out.at[sem], sum_in.at[sem], (core, to_x * ZS + z, y))

    for kind in range(2):
        wait_bytes(term_in.at[kind], sum_in.at[kind])
        weight_terms(kind, core, term_own, term_in, 0, 1)
        x_send(term_own.at[kind, far_x, low], far_in.at[kind, 0], 2 + kind, right_x)
        x_send(term_own.at[kind, far_x, high], far_in.at[kind, 1], 2 + kind, left_x)
        weight_terms(kind, core, term_own, term_in, 1, XS)
        x_send(term_own.at[kind, right_x, high], x_in.at[kind, 0, high], 8 + kind, right_x)
        x_send(term_own.at[kind, left_x, low], x_in.at[kind, 1, low], 8 + kind, left_x)

    give_back((GROUPS - 1) * group, peers)
    returned_ref[0] = back_ref[0]
    state_terms(y, part.at[0])
    for kind in range(2):
        wait_bytes(far_in.at[kind], sum_in.at[2 + kind])
        for side, (to_x, half) in enumerate(((right_x, low), (left_x, high))):
            both = term_own[kind, to_x, half].astype(jnp.float32)
            both = both + far_in[kind, side].astype(jnp.float32)
            term_own[kind, to_x, half] = both.astype(jnp.bfloat16)
            x_send(term_own.at[kind, to_x, half], x_in.at[kind, side, half], 10 + kind, to_x)

    for kind in range(2):
        wait_bytes(far_in.at[kind], sum_in.at[8 + kind])
        wait_bytes(far_in.at[kind], sum_in.at[10 + kind])

        @pl.loop(0, ZS)
        def _(to_z):
            total = term_own[kind, x, to_z].astype(jnp.float32)
            for other in range(2):
                total = total + x_in[kind, other, to_z].astype(jnp.float32)
            z_own[kind, to_z] = total.astype(jnp.bfloat16)

        @pl.loop(1, ZS)
        def _(offset):
            to_z = lax.rem(z + offset, ZS)
            there = (core, x * ZS + to_z, y)
            piece = z_own.at[kind, to_z]
            send(piece, z_in.at[kind, offset - 1], sum_out.at[4 + kind], sum_in.at[4 + kind], there)

    wait_bytes(part_in, sum_in.at[6])
    total = part[0].astype(jnp.float32)
    for other in range(ys - 1):
        total = total + part_in[other].astype(jnp.float32)
    state_out[...] = total.astype(jnp.bfloat16)

    for kind in range(2):
        wait_bytes(z_in.at[kind], sum_in.at[4 + kind])
        total = z_own[kind, z].astype(jnp.float32)
        for other in range(ZS - 1):
            total = total + z_in[kind, other].astype(jnp.float32)
        piece_away[kind] = total

    @pl.when(away)
    def _():
        send(piece_away, piece_out, sum_out.at[7], sum_in.at[7], partner_of(core, x, y, z))
        wait_bytes(piece_out, sum_in.at[7])
        wait_bytes(piece_away, sum_out.at[7])

    @pl.when(jnp.logical_not(away))
    def _():
        piece_out[...] = piece_away[...]

    wait_bytes(returned_ref.at[pl.ds(1, peers - 1)], row_in.at[GROUPS])
    wait_bytes(send_ref.at[pl.ds(1, peers - 1)], row_out.at[0])
    wait_bytes(back_ref.at[pl.ds(1, peers - 1)], row_out.at[1])
    wait_bytes(all_states.at[pl.ds(0, ys - 1)], gather_out.at[1])
    wait_bytes(all_weights.at[0, 0, pl.ds(0, ZS - 1)], gather_out.at[2])
    wait_bytes(all_weights.at[0, pl.ds(0, XS - 1)], gather_out.at[3])
    wait_bytes(all_weights.at[pl.ds(0, cores - 1)], gather_out.at[4])
    for kind in range(2):
        wait_bytes(term_away.at[kind], sum_out.at[kind])
        for sem in (2, 8, 10):
            wait_bytes(far_in.at[kind], sum_out.at[sem + kind])
        wait_bytes(z_in.at[kind], sum_out.at[4 + kind])
    wait_bytes(part_in, sum_out.at[6])


def whole(length, packed, keys, values, states, weights, cores, ys):
    smem, vmem = pl.BlockSpec(memory_space=pltpu.SMEM), pl.BlockSpec(memory_space=pltpu.VMEM)
    hbm = pl.BlockSpec(memory_space=pl.ANY)
    wire = packed.dtype
    peers, _, peer_rows, width = packed.shape
    src_len, features = states.shape
    unit_rows = weights.shape[0]
    piece = (2, unit_rows, features)
    terms = (2, XS, ZS, unit_rows, features)
    return pl.pallas_call(
        functools.partial(whole_kernel, cores, ys),
        out_shape=(
            jax.ShapeDtypeStruct((peers, peer_rows, width), wire),
            jax.ShapeDtypeStruct((src_len, features), wire),
            jax.ShapeDtypeStruct(piece, jnp.float32),
        ),
        in_specs=[smem, vmem, hbm, hbm, hbm, vmem],
        out_specs=(vmem, vmem, vmem),
        scratch_shapes=[
            pltpu.VMEM(packed.shape, wire),
            pltpu.VMEM((peers, peer_rows, width), wire),
            pltpu.VMEM((src_len, width), wire),
            pltpu.VMEM((src_len, width), wire),
            pltpu.VMEM((width, src_len), wire),
            pltpu.VMEM((src_len, width), jnp.float32),
            pltpu.VMEM((src_len, width), jnp.float32),
            pltpu.VMEM((2, src_len, width), wire),
            pltpu.VMEM((2, width, src_len), wire),
            pltpu.VMEM((ys, src_len, features), wire),
            pltpu.VMEM((cores, XS, ZS, *piece), wire),
            pltpu.VMEM(terms, wire),
            pltpu.VMEM(terms, wire),
            pltpu.VMEM(terms, wire),
            pltpu.VMEM((2, 2, ZS // 2, *terms[3:]), wire),
            pltpu.VMEM((2, 2, *terms[2:]), wire),
            pltpu.VMEM((2, *terms[2:]), wire),
            pltpu.VMEM((2, ZS - 1, *terms[3:]), wire),
            pltpu.VMEM((ys, src_len, features), wire),
            pltpu.VMEM((ys - 1, src_len, features), wire),
            pltpu.VMEM(piece, jnp.float32),
            pltpu.VMEM(piece, wire),
            pltpu.SemaphoreType.DMA((GROUPS + 1,)),
            pltpu.SemaphoreType.DMA((2,)),
            pltpu.SemaphoreType.DMA((5,)),
            pltpu.SemaphoreType.DMA((5,)),
            pltpu.SemaphoreType.DMA((12,)),
            pltpu.SemaphoreType.DMA((12,)),
            pltpu.SemaphoreType.DMA((5,)),
        ],
        compiler_params=pltpu.CompilerParams(
            collective_id=1, has_side_effects=True, vmem_limit_bytes=56 << 20
        ),
        name="exchange_attend_reduce",
    )(length, packed, keys, values, states, weights)


def on_device(queries, out_grads, owners, src_keys, src_values, states, kv_weight, src_lengths):
    cores, ys = lax.axis_size("grp"), lax.axis_size("mdl")
    peers = cores * XS * ZS
    tgt_len = queries.shape[1]
    packed = pack(owners, queries, out_grads, peers)
    returned, state_sum, weight_sum = whole(
        src_lengths, packed, src_keys[0], src_values[0], states[0], kv_weight, cores, ys
    )
    return unpack(owners, returned, state_sum, weight_sum, tgt_len)


def solution(mesh):
    rows = P(ROWS, None, "mdl")
    return jax.shard_map(
        on_device,
        mesh=mesh,
        in_specs=(rows, rows, P(ROWS), rows, rows, rows, rows, P(ROWS)),
        out_specs=(rows, rows, rows),
        check_vma=False,
    )
```

```python
import functools
import math

import jax
import jax.numpy as jnp
from jax import lax
from jax.experimental import pallas as pl
from jax.experimental.pallas import tpu as pltpu
from jax.sharding import PartitionSpec as P

HEAD_DIM = 64
LANES = 128
ROWS = ("grp", "seq")
MESH = pl.DeviceIdType.MESH
XS, ZS, GROUPS, CHUNKS = 4, 8, 4, 4


def place():
    seq = lax.axis_index("seq")
    return lax.axis_index("grp"), lax.div(seq, ZS), lax.axis_index("mdl"), lax.rem(seq, ZS)


def in_plane(core, x, y, z, offset, cores):
    to_core = lax.rem(core + lax.div(offset, XS * ZS), cores)
    to_x = lax.rem(x + lax.rem(lax.div(offset, ZS), XS), XS)
    to_z = lax.rem(z + lax.rem(offset, ZS), ZS)
    return (to_core, to_x * ZS + to_z, y)


def back_in_plane(core, x, y, z, offset, cores):
    to_core = lax.rem(core + cores - lax.div(offset, XS * ZS), cores)
    to_x = lax.rem(x + XS - lax.rem(lax.div(offset, ZS), XS), XS)
    to_z = lax.rem(z + ZS - lax.rem(offset, ZS), ZS)
    return (to_core, to_x * ZS + to_z, y)


def partner_of(core, x, y, z):
    half = XS // 2
    to_x = lax.rem(y, 2) * half + lax.rem(x, half)
    return (lax.div(y, 2), to_x * ZS + z, core * 2 + lax.div(x, half))


def in_column(partner, z, offset):
    return (partner[0], lax.div(partner[1], ZS) * ZS + lax.rem(z + offset, ZS), partner[2])


def greet(core, x, y, z, cores, ys, partner, away):
    barrier = pltpu.get_barrier_semaphore()
    peers = cores * XS * ZS

    @pl.loop(1, peers)
    def _(offset):
        there = in_plane(core, x, y, z, offset, cores)
        pl.semaphore_signal(barrier, inc=1, device_id=there, device_id_type=MESH)

    @pl.loop(1, ys)
    def _(offset):
        there = (core, x * ZS + z, lax.rem(y + offset, ys))
        pl.semaphore_signal(barrier, inc=1, device_id=there, device_id_type=MESH)

    @pl.when(away)
    def _():
        @pl.loop(0, ZS)
        def _(offset):
            there = in_column(partner, z, offset)
            pl.semaphore_signal(barrier, inc=1, device_id=there, device_id_type=MESH)

    pl.semaphore_wait(barrier, peers + ys - 2 + ZS * away.astype(jnp.int32))


def send(source, target, send_sem, recv_sem, there):
    pltpu.make_async_remote_copy(
        src_ref=source,
        dst_ref=target,
        send_sem=send_sem,
        recv_sem=recv_sem,
        device_id=there,
        device_id_type=MESH,
    ).start()


def wait_bytes(ref, sem):
    pltpu.make_async_copy(ref, ref, sem).wait()


def dot(left, right, dims):
    return lax.dot_general(left, right, (dims, ((), ())), preferred_element_type=jnp.float32)


def peer_of(owner, core, x, z):
    to_core = (lax.shift_right_logical(owner, 5) - core) & 1
    to_x = (lax.shift_right_logical(owner, 3) - x) & (XS - 1)
    to_z = (owner - z) & (ZS - 1)
    return (to_core * XS + to_x) * ZS + to_z


def pack_kernel(owners_ref, query_ref, grad_ref, out_ref, first_ref, second_ref):
    peers = out_ref.shape[0]
    core, x, _, z = place()

    @pl.loop(0, peers, unroll=8)
    def _(peer):
        first_ref[peer] = -1
        second_ref[peer] = -1

    @pl.loop(0, query_ref.shape[0], unroll=4)
    def _(target):
        peer = peer_of(owners_ref[target], core, x, z)
        first = first_ref[peer]
        first_ref[peer] = jnp.where(first < 0, target, first)
        second_ref[peer] = jnp.where(first < 0, -1, target)

    @pl.loop(0, peers, unroll=8)
    def _(peer):
        for kind, ref in enumerate((query_ref, grad_ref)):
            rows = []
            for target in (first_ref[peer], second_ref[peer]):
                row = ref[jnp.maximum(target, 0)]
                rows.append(jnp.where(target < 0, jnp.zeros_like(row), row))
            out_ref[peer, kind] = jnp.concatenate(rows, axis=0)


def pack(owners, queries, out_grads, peers):
    _, tgt_len, width = queries.shape
    smem, vmem = pl.BlockSpec(memory_space=pltpu.SMEM), pl.BlockSpec(memory_space=pltpu.VMEM)
    return pl.pallas_call(
        pack_kernel,
        out_shape=jax.ShapeDtypeStruct((peers, 2, 2 * tgt_len, width), queries.dtype),
        in_specs=[smem, vmem, vmem],
        out_specs=vmem,
        scratch_shapes=[pltpu.SMEM((peers,), jnp.int32), pltpu.SMEM((peers,), jnp.int32)],
        name="pack_targets",
    )(owners, queries, out_grads)


def unpack_kernel(
    owners_ref, back_ref, state_ref, weight_ref, out_ref, state_out, weight_out, used_ref, slot_ref
):
    targets, tgt_len, _ = out_ref.shape
    core, x, _, z = place()

    @pl.loop(0, back_ref.shape[0], unroll=8)
    def _(peer):
        used_ref[peer] = 0

    @pl.loop(0, targets, unroll=4)
    def _(target):
        peer = peer_of(owners_ref[target], core, x, z)
        used = used_ref[peer]
        used_ref[peer] = 1
        slot_ref[target] = peer * 2 + used

    @pl.loop(0, targets, unroll=8)
    def _(target):
        slot = slot_ref[target]
        both = back_ref[lax.shift_right_logical(slot, 1)]
        out_ref[target] = jnp.where((slot & 1) == 0, both[:tgt_len], both[tgt_len:])

    state_out[0] = state_ref[...]
    for kind in range(2):
        weight_out[:, kind, :] = weight_ref[kind].astype(jnp.float32)


def unpack(owners, returned, state, weight, tgt_len):
    peers, _, width = returned.shape
    targets = owners.shape[0]
    kinds, unit_rows, features = weight.shape
    smem, vmem = pl.BlockSpec(memory_space=pltpu.SMEM), pl.BlockSpec(memory_space=pltpu.VMEM)
    return pl.pallas_call(
        unpack_kernel,
        out_shape=(
            jax.ShapeDtypeStruct((targets, tgt_len, width), returned.dtype),
            jax.ShapeDtypeStruct((1, *state.shape), state.dtype),
            jax.ShapeDtypeStruct((unit_rows, kinds, features), jnp.float32),
        ),
        in_specs=[smem, vmem, vmem, vmem],
        out_specs=(vmem, vmem, vmem),
        scratch_shapes=[pltpu.SMEM((peers,), jnp.int32), pltpu.SMEM((targets,), jnp.int32)],
        name="unpack_targets",
    )(owners, returned, state, weight)


def whole_kernel(
    cores,
    ys,
    length_ref,
    send_ref,
    key_hbm,
    value_hbm,
    states_hbm,
    weight_ref,
    returned_ref,
    state_out,
    piece_out,
    got_ref,
    back_ref,
    key_ref,
    value_ref,
    key_t,
    key_sums,
    value_sums,
    grads,
    grads_t,
    all_states,
    all_weights,
    term_away,
    term_own,
    term_in,
    far_in,
    x_in,
    z_own,
    z_in,
    part,
    part_in,
    piece_away,
    piece_ref,
    row_in,
    row_out,
    gather_in,
    gather_out,
    sum_in,
    sum_out,
    state_sem,
    own_sem,
):
    core, x, y, z = place()
    peers = cores * XS * ZS
    group = peers // GROUPS
    partner = partner_of(core, x, y, z)
    away = partner[2] != y
    src_len, width = key_ref.shape
    unit_rows, chunk_width = term_own.shape[3:]
    features = all_states.shape[2]
    halves = CHUNKS // 2
    half_rows = ZS * unit_rows
    scale = HEAD_DIM**-0.5
    exp_scale = scale * math.log2(math.e)
    rows = group * got_ref.shape[2]

    own_keys = pltpu.make_async_copy(key_hbm, key_ref, own_sem.at[0])
    own_values = pltpu.make_async_copy(value_hbm, value_ref, own_sem.at[1])
    own_states = pltpu.make_async_copy(states_hbm, all_states.at[y], own_sem.at[2])
    own_rows = pltpu.make_async_copy(send_ref.at[0], got_ref.at[0], own_sem.at[3])
    for copy in (own_keys, own_values, own_states, own_rows):
        copy.start()
    for kind in range(2):
        piece_ref[kind] = weight_ref[:, kind, :]
    greet(core, x, y, z, cores, ys, partner, away)

    to_core, to_x = partner[0], lax.div(partner[1], ZS)
    own_piece = pltpu.make_async_copy(piece_ref, all_weights.at[core, x, z], own_sem.at[4])

    @pl.loop(1, ZS)
    def _(offset):
        there = in_column(partner, z, offset)
        send(piece_ref, all_weights.at[to_core, to_x, z], gather_out.at[2], gather_in.at[2], there)

    @pl.when(away)
    def _():
        there = partner_of(core, x, y, z)
        send(piece_ref, all_weights.at[to_core, to_x, z], gather_out.at[0], gather_in.at[0], there)

    @pl.when(jnp.logical_not(away))
    def _():
        own_piece.start()

    @pl.loop(1, ys)
    def _(offset):
        there = (core, x * ZS + z, lax.rem(y + offset, ys))
        send(states_hbm, all_states.at[y], gather_out.at[1], gather_in.at[1], there)

    def dispatch(first, last):
        @pl.loop(first, last)
        def _(offset):
            there = in_plane(core, x, y, z, offset, cores)
            at = lax.div(offset, group)
            send(send_ref.at[offset], got_ref.at[offset], row_out.at[0], row_in.at[at], there)

    dispatch(1, 2 * group)
    key_sums[...] = jnp.zeros_like(key_sums)
    value_sums[...] = jnp.zeros_like(value_sums)
    own_keys.wait()
    own_values.wait()
    key_t[...] = jnp.transpose(key_ref[...])
    own_rows.wait()

    @pl.when(away)
    def _():
        wait_bytes(piece_ref, gather_in.at[0])
        wait_bytes(piece_ref, gather_out.at[0])

    @pl.when(jnp.logical_not(away))
    def _():
        own_piece.wait()

    wait_bytes(all_weights.at[0, 0, pl.ds(0, ZS - 1)], gather_in.at[2])

    @pl.loop(1, XS)
    def _(offset):
        there = (core, lax.rem(x + offset, XS) * ZS + z, y)
        line = all_weights.at[core, x]
        send(line, line, gather_out.at[3], gather_in.at[3], there)

    def give_back(first, last):
        @pl.loop(first, last)
        def _(offset):
            there = back_in_plane(core, x, y, z, offset, cores)
            send(back_ref.at[offset], returned_ref.at[offset], row_out.at[1], row_in.at[GROUPS], there)

    @pl.loop(0, GROUPS)
    def _(step):
        start = step * group

        @pl.when(step == 0)
        def _():
            wait_bytes(got_ref.at[pl.ds(1, group - 1)], row_in.at[0])

        @pl.when(step > 0)
        def _():
            wait_bytes(got_ref.at[pl.ds(start, group)], row_in.at[step])

        @pl.when(step < GROUPS - 2)
        def _():
            dispatch((step + 2) * group, (step + 3) * group)

        @pl.when(step == GROUPS - 2)
        def _():
            wait_bytes(all_weights.at[0, pl.ds(0, XS - 1)], gather_in.at[3])

            @pl.loop(1, cores)
            def _(offset):
                there = (lax.rem(core + offset, cores), x * ZS + z, y)
                half = all_weights.at[core]
                send(half, half, gather_out.at[4], gather_in.at[4], there)

        @pl.when(step == GROUPS - 1)
        def _():
            give_back(1, (GROUPS - 1) * group)

        valid = lax.broadcasted_iota(jnp.int32, (src_len, rows), 0) < length_ref[0]
        lane = lax.broadcasted_iota(jnp.int32, (rows, LANES), 1)
        for pair in range(width // LANES):
            at = slice(pair * LANES, (pair + 1) * LANES)
            query = got_ref[pl.ds(start, group), 0, :, at].reshape(rows, LANES)
            grad = got_ref[pl.ds(start, group), 1, :, at].reshape(rows, LANES)
            keys = key_ref[:, at]
            values = value_ref[:, at]
            key_sum = key_sums[:, at]
            value_sum = value_sums[:, at]
            back = []
            for half in range(LANES // HEAD_DIM):
                own = (lane >= half * HEAD_DIM) & (lane < (half + 1) * HEAD_DIM)
                query_h = jnp.where(own, query, jnp.zeros_like(query))
                grad_h = jnp.where(own, grad, jnp.zeros_like(grad))
                scores = dot(keys, query_h, ((1,), (1,)))
                scores = jnp.where(valid, scores, -1e30)
                peak = jnp.max(scores, axis=0, keepdims=True)
                terms = jnp.exp2((scores - peak) * exp_scale)
                probs = terms * (1.0 / jnp.sum(terms, axis=0, keepdims=True))
                probs_b = probs.astype(jnp.bfloat16)
                prob_grad = dot(values, grad_h, ((1,), (1,)))
                delta = jnp.sum(probs_b.astype(jnp.float32) * prob_grad, axis=0, keepdims=True)
                score_grad = (probs * (prob_grad - delta)).astype(jnp.bfloat16)
                key_sum = key_sum + dot(score_grad, query_h, ((1,), (0,)))
                value_sum = value_sum + dot(probs_b, grad_h, ((1,), (0,)))
                head = pair * LANES + half * HEAD_DIM
                back.append(dot(key_t[head : head + HEAD_DIM, :], score_grad, ((1,), (0,))))
            key_sums[:, at] = key_sum
            value_sums[:, at] = value_sum
            back = jnp.concatenate(back, axis=0) * scale
            back = jnp.transpose(back).astype(jnp.bfloat16)
            back_ref[pl.ds(start, group), :, at] = back.reshape(group, rows // group, LANES)

    def weight_terms(chunk, to_core, target, added, first_x, last_x):
        columns = slice(chunk % halves * chunk_width, (chunk % halves + 1) * chunk_width)

        @pl.loop(first_x, last_x)
        def _(step_x):
            to_x = lax.rem(x + XS // 2 + step_x, XS)
            block = to_core * (XS // 2) + lax.div(to_x, 2)
            first = pl.multiple_of(lax.rem(to_x, 2) * half_rows, half_rows)
            left = grads_t[chunk // halves, pl.ds(first, half_rows), :]
            terms = dot(left, all_states[block, :, columns], ((1,), (0,)))
            if added is not None:
                terms = terms + added[chunk, to_x].reshape(half_rows, chunk_width).astype(jnp.float32)
            target[chunk, to_x] = terms.astype(jnp.bfloat16).reshape(ZS, unit_rows, chunk_width)

    CORE, FAR, NEAR, MERGED, ALONG_Z = (CHUNKS * stage for stage in range(5))
    own_states.wait()
    wait_bytes(all_states.at[pl.ds(0, ys - 1)], gather_in.at[1])
    sibling = lax.rem(core + 1, cores)
    for chunk in range(CHUNKS):
        kind = chunk // halves
        if chunk % halves == 0:
            sums = key_sums[...] * scale if kind == 0 else value_sums[...]
            grads[kind] = sums.astype(jnp.bfloat16)
            grads_t[kind] = jnp.transpose(grads[kind])
        weight_terms(chunk, sibling, term_away, None, 0, XS)
        there = (sibling, x * ZS + z, y)
        at = CORE + chunk
        send(term_away.at[chunk], term_in.at[chunk], sum_out.at[at], sum_in.at[at], there)


    def state_terms(block, target):
        for kind in range(2):
            lines = all_weights[lax.div(block, 2), pl.ds(lax.rem(block, 2) * 2, 2), :, kind]
            terms = dot(grads[kind], lines.reshape(width, features), ((1,), (0,)))
            total = terms if kind == 0 else total + terms
        target[...] = total.astype(jnp.bfloat16)

    def state_send(offset):
        to_y = lax.rem(y + offset, ys)
        state_terms(to_y, part.at[offset])
        there = (core, x * ZS + z, to_y)
        send(part.at[offset], part_in.at[offset - 1], state_sem.at[0], state_sem.at[1], there)

    low, high = pl.ds(0, ZS // 2), pl.ds(ZS // 2, ZS // 2)
    right_x, far_x, left_x = (lax.rem(x + offset, XS) for offset in range(1, XS))

    def x_send(source, target, sem, to_x):
        send(source, target, sum_out.at[sem], sum_in.at[sem], (core, to_x * ZS + z, y))

    for chunk in range(CHUNKS):
        wait_bytes(term_in.at[chunk], sum_in.at[CORE + chunk])
        weight_terms(chunk, core, term_own, term_in, 0, 1)
        x_send(term_own.at[chunk, far_x, low], far_in.at[chunk, 0], FAR + chunk, right_x)
        x_send(term_own.at[chunk, far_x, high], far_in.at[chunk, 1], FAR + chunk, left_x)
        weight_terms(chunk, core, term_own, term_in, 1, XS)
        x_send(term_own.at[chunk, right_x, high], x_in.at[chunk, 0, high], NEAR + chunk, right_x)
        x_send(term_own.at[chunk, left_x, low], x_in.at[chunk, 1, low], NEAR + chunk, left_x)
        if chunk == halves - 1:
            wait_bytes(all_weights.at[pl.ds(0, cores - 1)], gather_in.at[4])
        if chunk % halves == halves - 1:
            state_send(chunk // halves + 1)

    give_back((GROUPS - 1) * group, peers)
    returned_ref[0] = back_ref[0]

    def merge(chunk):
        wait_bytes(far_in.at[chunk], sum_in.at[FAR + chunk])
        for side, (to_x, half) in enumerate(((right_x, low), (left_x, high))):
            both = term_own[chunk, to_x, half].astype(jnp.float32)
            both = both + far_in[chunk, side].astype(jnp.float32)
            term_own[chunk, to_x, half] = both.astype(jnp.bfloat16)
            x_send(term_own.at[chunk, to_x, half], x_in.at[chunk, side, half], MERGED + chunk, to_x)

    for chunk in range(CHUNKS):
        merge(chunk)
        if chunk == 1:
            state_send(3)
    state_terms(y, part.at[0])

    for chunk in range(CHUNKS):
        wait_bytes(far_in.at[chunk], sum_in.at[NEAR + chunk])
        wait_bytes(far_in.at[chunk], sum_in.at[MERGED + chunk])

        @pl.loop(0, ZS)
        def _(to_z):
            total = term_own[chunk, x, to_z].astype(jnp.float32)
            for other in range(2):
                total = total + x_in[chunk, other, to_z].astype(jnp.float32)
            z_own[chunk, to_z] = total.astype(jnp.bfloat16)

        @pl.loop(1, ZS)
        def _(offset):
            to_z = lax.rem(z + offset, ZS)
            there = (core, x * ZS + to_z, y)
            piece = z_own.at[chunk, to_z]
            at = ALONG_Z + chunk
            send(piece, z_in.at[chunk, offset - 1], sum_out.at[at], sum_in.at[at], there)

    wait_bytes(part_in, state_sem.at[1])
    total = part[0].astype(jnp.float32)
    for other in range(ys - 1):
        total = total + part_in[other].astype(jnp.float32)
    state_out[...] = total.astype(jnp.bfloat16)

    for chunk in range(CHUNKS):
        columns = slice(chunk % halves * chunk_width, (chunk % halves + 1) * chunk_width)
        wait_bytes(z_in.at[chunk], sum_in.at[ALONG_Z + chunk])
        total = z_own[chunk, z].astype(jnp.float32)
        for other in range(ZS - 1):
            total = total + z_in[chunk, other].astype(jnp.float32)
        piece_away[chunk // halves, :, columns] = total.astype(jnp.bfloat16)

    @pl.when(away)
    def _():
        send(piece_away, piece_out, state_sem.at[2], state_sem.at[3], partner_of(core, x, y, z))
        wait_bytes(piece_out, state_sem.at[3])
        wait_bytes(piece_away, state_sem.at[2])

    @pl.when(jnp.logical_not(away))
    def _():
        piece_out[...] = piece_away[...]

    wait_bytes(returned_ref.at[pl.ds(1, peers - 1)], row_in.at[GROUPS])
    wait_bytes(send_ref.at[pl.ds(1, peers - 1)], row_out.at[0])
    wait_bytes(back_ref.at[pl.ds(1, peers - 1)], row_out.at[1])
    wait_bytes(all_states.at[pl.ds(0, ys - 1)], gather_out.at[1])
    wait_bytes(all_weights.at[0, 0, pl.ds(0, ZS - 1)], gather_out.at[2])
    wait_bytes(all_weights.at[0, pl.ds(0, XS - 1)], gather_out.at[3])
    wait_bytes(all_weights.at[pl.ds(0, cores - 1)], gather_out.at[4])
    for chunk in range(CHUNKS):
        wait_bytes(term_away.at[chunk], sum_out.at[CORE + chunk])
        for stage in (FAR, NEAR, MERGED):
            wait_bytes(far_in.at[chunk], sum_out.at[stage + chunk])
        wait_bytes(z_in.at[chunk], sum_out.at[ALONG_Z + chunk])
    wait_bytes(part_in, state_sem.at[0])


def whole(length, packed, keys, values, states, weights, cores, ys):
    smem, vmem = pl.BlockSpec(memory_space=pltpu.SMEM), pl.BlockSpec(memory_space=pltpu.VMEM)
    hbm = pl.BlockSpec(memory_space=pl.ANY)
    wire = packed.dtype
    peers, _, peer_rows, width = packed.shape
    src_len, features = states.shape
    unit_rows = weights.shape[0]
    piece = (2, unit_rows, features)
    chunk_width = features * 2 // CHUNKS
    terms = (CHUNKS, XS, ZS, unit_rows, chunk_width)
    return pl.pallas_call(
        functools.partial(whole_kernel, cores, ys),
        out_shape=(
            jax.ShapeDtypeStruct((peers, peer_rows, width), wire),
            jax.ShapeDtypeStruct((src_len, features), wire),
            jax.ShapeDtypeStruct(piece, wire),
        ),
        in_specs=[smem, vmem, hbm, hbm, hbm, vmem],
        out_specs=(vmem, vmem, vmem),
        scratch_shapes=[
            pltpu.VMEM(packed.shape, wire),
            pltpu.VMEM((peers, peer_rows, width), wire),
            pltpu.VMEM((src_len, width), wire),
            pltpu.VMEM((src_len, width), wire),
            pltpu.VMEM((width, src_len), wire),
            pltpu.VMEM((src_len, width), jnp.float32),
            pltpu.VMEM((src_len, width), jnp.float32),
            pltpu.VMEM((2, src_len, width), wire),
            pltpu.VMEM((2, width, src_len), wire),
            pltpu.VMEM((ys, src_len, features), wire),
            pltpu.VMEM((cores, XS, ZS, *piece), wire),
            pltpu.VMEM(terms, wire),
            pltpu.VMEM(terms, wire),
            pltpu.VMEM(terms, wire),
            pltpu.VMEM((CHUNKS, 2, ZS // 2, *terms[3:]), wire),
            pltpu.VMEM((CHUNKS, 2, *terms[2:]), wire),
            pltpu.VMEM((CHUNKS, *terms[2:]), wire),
            pltpu.VMEM((CHUNKS, ZS - 1, *terms[3:]), wire),
            pltpu.VMEM((ys, src_len, features), wire),
            pltpu.VMEM((ys - 1, src_len, features), wire),
            pltpu.VMEM(piece, wire),
            pltpu.VMEM(piece, wire),
            pltpu.SemaphoreType.DMA((GROUPS + 1,)),
            pltpu.SemaphoreType.DMA((2,)),
            pltpu.SemaphoreType.DMA((5,)),
            pltpu.SemaphoreType.DMA((5,)),
            pltpu.SemaphoreType.DMA((5 * CHUNKS,)),
            pltpu.SemaphoreType.DMA((5 * CHUNKS,)),
            pltpu.SemaphoreType.DMA((4,)),
            pltpu.SemaphoreType.DMA((5,)),
        ],
        compiler_params=pltpu.CompilerParams(
            collective_id=1, has_side_effects=True, vmem_limit_bytes=56 << 20
        ),
        name="exchange_attend_reduce",
    )(length, packed, keys, values, states, weights)


def on_device(queries, out_grads, owners, src_keys, src_values, states, kv_weight, src_lengths):
    cores, ys = lax.axis_size("grp"), lax.axis_size("mdl")
    peers = cores * XS * ZS
    tgt_len = queries.shape[1]
    packed = pack(owners, queries, out_grads, peers)
    returned, state_sum, weight_sum = whole(
        src_lengths, packed, src_keys[0], src_values[0], states[0], kv_weight, cores, ys
    )
    return unpack(owners, returned, state_sum, weight_sum, tgt_len)


def solution(mesh):
    rows = P(ROWS, None, "mdl")
    return jax.shard_map(
        on_device,
        mesh=mesh,
        in_specs=(rows, rows, P(ROWS), rows, rows, rows, rows, P(ROWS)),
        out_specs=(rows, rows, rows),
        check_vma=False,
    )
```

```python
import functools
import math

import jax
import jax.numpy as jnp
from jax import lax
from jax.experimental import pallas as pl
from jax.experimental.pallas import tpu as pltpu
from jax.sharding import PartitionSpec as P

HEAD_DIM = 64
LANES = 128
ROWS = ("grp", "seq")
MESH = pl.DeviceIdType.MESH
XS, ZS, GROUPS, CHUNKS = 4, 8, 4, 4


def place():
    seq = lax.axis_index("seq")
    return lax.axis_index("grp"), lax.div(seq, ZS), lax.axis_index("mdl"), lax.rem(seq, ZS)


def in_plane(core, x, y, z, offset, cores):
    to_core = lax.rem(core + lax.div(offset, XS * ZS), cores)
    to_x = lax.rem(x + lax.rem(lax.div(offset, ZS), XS), XS)
    to_z = lax.rem(z + lax.rem(offset, ZS), ZS)
    return (to_core, to_x * ZS + to_z, y)


def back_in_plane(core, x, y, z, offset, cores):
    to_core = lax.rem(core + cores - lax.div(offset, XS * ZS), cores)
    to_x = lax.rem(x + XS - lax.rem(lax.div(offset, ZS), XS), XS)
    to_z = lax.rem(z + ZS - lax.rem(offset, ZS), ZS)
    return (to_core, to_x * ZS + to_z, y)


def partner_of(core, x, y, z):
    half = XS // 2
    to_x = lax.rem(y, 2) * half + lax.rem(x, half)
    return (lax.div(y, 2), to_x * ZS + z, core * 2 + lax.div(x, half))


def in_column(partner, z, offset):
    return (partner[0], lax.div(partner[1], ZS) * ZS + lax.rem(z + offset, ZS), partner[2])


def greet(core, x, y, z, cores, ys, partner, away):
    barrier = pltpu.get_barrier_semaphore()
    peers = cores * XS * ZS

    @pl.loop(1, peers)
    def _(offset):
        there = in_plane(core, x, y, z, offset, cores)
        pl.semaphore_signal(barrier, inc=1, device_id=there, device_id_type=MESH)

    @pl.loop(1, ys)
    def _(offset):
        there = (core, x * ZS + z, lax.rem(y + offset, ys))
        pl.semaphore_signal(barrier, inc=1, device_id=there, device_id_type=MESH)

    @pl.when(away)
    def _():
        @pl.loop(0, ZS)
        def _(offset):
            there = in_column(partner, z, offset)
            pl.semaphore_signal(barrier, inc=1, device_id=there, device_id_type=MESH)

    pl.semaphore_wait(barrier, peers + ys - 2 + ZS * away.astype(jnp.int32))


def send(source, target, send_sem, recv_sem, there):
    pltpu.make_async_remote_copy(
        src_ref=source,
        dst_ref=target,
        send_sem=send_sem,
        recv_sem=recv_sem,
        device_id=there,
        device_id_type=MESH,
    ).start()


def wait_bytes(ref, sem):
    pltpu.make_async_copy(ref, ref, sem).wait()


def dot(left, right, dims):
    return lax.dot_general(left, right, (dims, ((), ())), preferred_element_type=jnp.float32)


def peer_of(owner, core, x, z):
    to_core = (lax.shift_right_logical(owner, 5) - core) & 1
    to_x = (lax.shift_right_logical(owner, 3) - x) & (XS - 1)
    to_z = (owner - z) & (ZS - 1)
    return (to_core * XS + to_x) * ZS + to_z


def pack_kernel(owners_ref, query_ref, grad_ref, out_ref, first_ref, second_ref):
    peers = out_ref.shape[0]
    core, x, _, z = place()

    @pl.loop(0, peers, unroll=8)
    def _(peer):
        first_ref[peer] = -1
        second_ref[peer] = -1

    @pl.loop(0, query_ref.shape[0], unroll=4)
    def _(target):
        peer = peer_of(owners_ref[target], core, x, z)
        first = first_ref[peer]
        first_ref[peer] = jnp.where(first < 0, target, first)
        second_ref[peer] = jnp.where(first < 0, -1, target)

    @pl.loop(0, peers, unroll=8)
    def _(peer):
        for kind, ref in enumerate((query_ref, grad_ref)):
            rows = []
            for target in (first_ref[peer], second_ref[peer]):
                row = ref[jnp.maximum(target, 0)]
                rows.append(jnp.where(target < 0, jnp.zeros_like(row), row))
            out_ref[peer, kind] = jnp.concatenate(rows, axis=0)


def pack(owners, queries, out_grads, peers):
    _, tgt_len, width = queries.shape
    smem, vmem = pl.BlockSpec(memory_space=pltpu.SMEM), pl.BlockSpec(memory_space=pltpu.VMEM)
    return pl.pallas_call(
        pack_kernel,
        out_shape=jax.ShapeDtypeStruct((peers, 2, 2 * tgt_len, width), queries.dtype),
        in_specs=[smem, vmem, vmem],
        out_specs=vmem,
        scratch_shapes=[pltpu.SMEM((peers,), jnp.int32), pltpu.SMEM((peers,), jnp.int32)],
        name="pack_targets",
    )(owners, queries, out_grads)


def unpack_kernel(
    owners_ref, back_ref, state_ref, weight_ref, out_ref, state_out, weight_out, used_ref, slot_ref
):
    targets, tgt_len, _ = out_ref.shape
    core, x, _, z = place()

    @pl.loop(0, back_ref.shape[0], unroll=8)
    def _(peer):
        used_ref[peer] = 0

    @pl.loop(0, targets, unroll=4)
    def _(target):
        peer = peer_of(owners_ref[target], core, x, z)
        used = used_ref[peer]
        used_ref[peer] = 1
        slot_ref[target] = peer * 2 + used

    @pl.loop(0, targets, unroll=8)
    def _(target):
        slot = slot_ref[target]
        both = back_ref[lax.shift_right_logical(slot, 1)]
        out_ref[target] = jnp.where((slot & 1) == 0, both[:tgt_len], both[tgt_len:])

    state_out[0] = state_ref[...]
    for kind in range(2):
        weight_out[:, kind, :] = weight_ref[kind].astype(jnp.float32)


def unpack(owners, returned, state, weight, tgt_len):
    peers, _, width = returned.shape
    targets = owners.shape[0]
    kinds, unit_rows, features = weight.shape
    smem, vmem = pl.BlockSpec(memory_space=pltpu.SMEM), pl.BlockSpec(memory_space=pltpu.VMEM)
    return pl.pallas_call(
        unpack_kernel,
        out_shape=(
            jax.ShapeDtypeStruct((targets, tgt_len, width), returned.dtype),
            jax.ShapeDtypeStruct((1, *state.shape), state.dtype),
            jax.ShapeDtypeStruct((unit_rows, kinds, features), jnp.float32),
        ),
        in_specs=[smem, vmem, vmem, vmem],
        out_specs=(vmem, vmem, vmem),
        scratch_shapes=[pltpu.SMEM((peers,), jnp.int32), pltpu.SMEM((targets,), jnp.int32)],
        name="unpack_targets",
    )(owners, returned, state, weight)


def whole_kernel(
    cores,
    ys,
    length_ref,
    send_ref,
    key_hbm,
    value_hbm,
    states_hbm,
    weight_ref,
    returned_ref,
    state_out,
    piece_out,
    got_ref,
    back_ref,
    key_ref,
    value_ref,
    key_t,
    key_sums,
    value_sums,
    grads,
    grads_t,
    all_states,
    all_weights,
    term_away,
    term_own,
    term_in,
    far_in,
    x_in,
    z_own,
    z_in,
    part,
    part_in,
    piece_away,
    piece_ref,
    row_in,
    row_out,
    gather_in,
    gather_out,
    sum_in,
    sum_out,
    state_sem,
    own_sem,
):
    core, x, y, z = place()
    peers = cores * XS * ZS
    group = peers // GROUPS
    partner = partner_of(core, x, y, z)
    away = partner[2] != y
    src_len, width = key_ref.shape
    unit_rows, chunk_width = term_own.shape[3:]
    features = all_states.shape[2]
    halves = CHUNKS // 2
    half_rows = ZS * unit_rows
    scale = HEAD_DIM**-0.5
    exp_scale = scale * math.log2(math.e)
    rows = group * got_ref.shape[2]

    own_keys = pltpu.make_async_copy(key_hbm, key_ref, own_sem.at[0])
    own_values = pltpu.make_async_copy(value_hbm, value_ref, own_sem.at[1])
    own_states = pltpu.make_async_copy(states_hbm, all_states.at[y], own_sem.at[2])
    own_rows = pltpu.make_async_copy(send_ref.at[0], got_ref.at[0], own_sem.at[3])
    for copy in (own_keys, own_values, own_states, own_rows):
        copy.start()
    for kind in range(2):
        piece_ref[kind] = weight_ref[:, kind, :]
    greet(core, x, y, z, cores, ys, partner, away)

    to_core, to_x = partner[0], lax.div(partner[1], ZS)
    own_piece = pltpu.make_async_copy(piece_ref, all_weights.at[core, x, z], own_sem.at[4])

    for offset in (1, ZS - 1):
        there = in_column(partner, z, offset)
        send(piece_ref, all_weights.at[to_core, to_x, z], gather_out.at[2], gather_in.at[2], there)

    @pl.when(away)
    def _():
        there = partner_of(core, x, y, z)
        send(piece_ref, all_weights.at[to_core, to_x, z], gather_out.at[0], gather_in.at[0], there)

    @pl.when(jnp.logical_not(away))
    def _():
        own_piece.start()

    @pl.loop(1, ys)
    def _(offset):
        there = (core, x * ZS + z, lax.rem(y + offset, ys))
        send(states_hbm, all_states.at[y], gather_out.at[1], gather_in.at[1], there)

    def dispatch(first, last):
        @pl.loop(first, last)
        def _(offset):
            there = in_plane(core, x, y, z, offset, cores)
            at = lax.div(offset, group)
            send(send_ref.at[offset], got_ref.at[offset], row_out.at[0], row_in.at[at], there)

    dispatch(1, 2 * group)
    key_sums[...] = jnp.zeros_like(key_sums)
    value_sums[...] = jnp.zeros_like(value_sums)
    own_keys.wait()
    own_values.wait()
    key_t[...] = jnp.transpose(key_ref[...])
    own_rows.wait()

    @pl.when(away)
    def _():
        wait_bytes(piece_ref, gather_in.at[0])
        wait_bytes(piece_ref, gather_out.at[0])

    @pl.when(jnp.logical_not(away))
    def _():
        own_piece.wait()

    wait_bytes(all_weights.at[0, 0, pl.ds(0, 2)], gather_in.at[2])
    up = (core, x * ZS + lax.rem(z + 1, ZS), y)
    down = (core, x * ZS + lax.rem(z + ZS - 1, ZS), y)
    for hop in range(1, ZS // 2):
        from_down = all_weights.at[core, x, lax.rem(z + ZS - hop, ZS)]
        from_up = all_weights.at[core, x, lax.rem(z + hop, ZS)]
        at = 4 + hop
        if hop < ZS // 2 - 1:
            send(from_down, from_down, gather_out.at[at], gather_in.at[at], up)
            send(from_up, from_up, gather_out.at[at], gather_in.at[at], down)
            wait_bytes(all_weights.at[0, 0, pl.ds(0, 2)], gather_in.at[at])
        else:
            send(from_down.at[0], from_down.at[0], gather_out.at[at], gather_in.at[at], up)
            send(from_up.at[1], from_up.at[1], gather_out.at[at], gather_in.at[at], down)
            wait_bytes(all_weights.at[0, 0, 0], gather_in.at[at])

    @pl.loop(1, XS)
    def _(offset):
        there = (core, lax.rem(x + offset, XS) * ZS + z, y)
        line = all_weights.at[core, x]
        send(line, line, gather_out.at[3], gather_in.at[3], there)

    def give_back(first, last):
        @pl.loop(first, last)
        def _(offset):
            there = back_in_plane(core, x, y, z, offset, cores)
            send(back_ref.at[offset], returned_ref.at[offset], row_out.at[1], row_in.at[GROUPS], there)

    @pl.loop(0, GROUPS)
    def _(step):
        start = step * group

        @pl.when(step == 0)
        def _():
            wait_bytes(got_ref.at[pl.ds(1, group - 1)], row_in.at[0])

        @pl.when(step > 0)
        def _():
            wait_bytes(got_ref.at[pl.ds(start, group)], row_in.at[step])

        @pl.when(step < GROUPS - 2)
        def _():
            dispatch((step + 2) * group, (step + 3) * group)

        @pl.when(step == GROUPS - 2)
        def _():
            wait_bytes(all_weights.at[0, pl.ds(0, XS - 1)], gather_in.at[3])

            @pl.loop(1, cores)
            def _(offset):
                there = (lax.rem(core + offset, cores), x * ZS + z, y)
                half = all_weights.at[core]
                send(half, half, gather_out.at[4], gather_in.at[4], there)

        @pl.when(step == GROUPS - 1)
        def _():
            give_back(1, (GROUPS - 1) * group)

        valid = lax.broadcasted_iota(jnp.int32, (src_len, rows), 0) < length_ref[0]
        lane = lax.broadcasted_iota(jnp.int32, (rows, LANES), 1)
        for pair in range(width // LANES):
            at = slice(pair * LANES, (pair + 1) * LANES)
            query = got_ref[pl.ds(start, group), 0, :, at].reshape(rows, LANES)
            grad = got_ref[pl.ds(start, group), 1, :, at].reshape(rows, LANES)
            keys = key_ref[:, at]
            values = value_ref[:, at]
            key_sum = key_sums[:, at]
            value_sum = value_sums[:, at]
            back = []
            for half in range(LANES // HEAD_DIM):
                own = (lane >= half * HEAD_DIM) & (lane < (half + 1) * HEAD_DIM)
                query_h = jnp.where(own, query, jnp.zeros_like(query))
                grad_h = jnp.where(own, grad, jnp.zeros_like(grad))
                scores = dot(keys, query_h, ((1,), (1,)))
                scores = jnp.where(valid, scores, -1e30)
                peak = jnp.max(scores, axis=0, keepdims=True)
                terms = jnp.exp2((scores - peak) * exp_scale)
                probs = terms * (1.0 / jnp.sum(terms, axis=0, keepdims=True))
                probs_b = probs.astype(jnp.bfloat16)
                prob_grad = dot(values, grad_h, ((1,), (1,)))
                delta = jnp.sum(probs_b.astype(jnp.float32) * prob_grad, axis=0, keepdims=True)
                score_grad = (probs * (prob_grad - delta)).astype(jnp.bfloat16)
                key_sum = key_sum + dot(score_grad, query_h, ((1,), (0,)))
                value_sum = value_sum + dot(probs_b, grad_h, ((1,), (0,)))
                head = pair * LANES + half * HEAD_DIM
                back.append(dot(key_t[head : head + HEAD_DIM, :], score_grad, ((1,), (0,))))
            key_sums[:, at] = key_sum
            value_sums[:, at] = value_sum
            back = jnp.concatenate(back, axis=0) * scale
            back = jnp.transpose(back).astype(jnp.bfloat16)
            back_ref[pl.ds(start, group), :, at] = back.reshape(group, rows // group, LANES)

    def weight_terms(chunk, to_core, target, added, first_x, last_x):
        columns = slice(chunk % halves * chunk_width, (chunk % halves + 1) * chunk_width)

        @pl.loop(first_x, last_x)
        def _(step_x):
            to_x = lax.rem(x + XS // 2 + step_x, XS)
            block = to_core * (XS // 2) + lax.div(to_x, 2)
            first = pl.multiple_of(lax.rem(to_x, 2) * half_rows, half_rows)
            left = grads_t[chunk // halves, pl.ds(first, half_rows), :]
            terms = dot(left, all_states[block, :, columns], ((1,), (0,)))
            if added is not None:
                terms = terms + added[chunk, to_x].reshape(half_rows, chunk_width).astype(jnp.float32)
            target[chunk, to_x] = terms.astype(jnp.bfloat16).reshape(ZS, unit_rows, chunk_width)

    CORE, FAR, NEAR, MERGED, ALONG_Z = (CHUNKS * stage for stage in range(5))
    own_states.wait()
    wait_bytes(all_states.at[pl.ds(0, ys - 1)], gather_in.at[1])
    sibling = lax.rem(core + 1, cores)
    for chunk in range(CHUNKS):
        kind = chunk // halves
        if chunk % halves == 0:
            sums = key_sums[...] * scale if kind == 0 else value_sums[...]
            grads[kind] = sums.astype(jnp.bfloat16)
            grads_t[kind] = jnp.transpose(grads[kind])
        weight_terms(chunk, sibling, term_away, None, 0, XS)
        there = (sibling, x * ZS + z, y)
        at = CORE + chunk
        send(term_away.at[chunk], term_in.at[chunk], sum_out.at[at], sum_in.at[at], there)


    def state_terms(block, target):
        for kind in range(2):
            lines = all_weights[lax.div(block, 2), pl.ds(lax.rem(block, 2) * 2, 2), :, kind]
            terms = dot(grads[kind], lines.reshape(width, features), ((1,), (0,)))
            total = terms if kind == 0 else total + terms
        target[...] = total.astype(jnp.bfloat16)

    def state_send(offset):
        to_y = lax.rem(y + offset, ys)
        state_terms(to_y, part.at[offset])
        there = (core, x * ZS + z, to_y)
        send(part.at[offset], part_in.at[offset - 1], state_sem.at[0], state_sem.at[1], there)

    low, high = pl.ds(0, ZS // 2), pl.ds(ZS // 2, ZS // 2)
    right_x, far_x, left_x = (lax.rem(x + offset, XS) for offset in range(1, XS))

    def x_send(source, target, sem, to_x):
        send(source, target, sum_out.at[sem], sum_in.at[sem], (core, to_x * ZS + z, y))

    for chunk in range(CHUNKS):
        wait_bytes(term_in.at[chunk], sum_in.at[CORE + chunk])
        weight_terms(chunk, core, term_own, term_in, 0, 1)
        x_send(term_own.at[chunk, far_x, low], far_in.at[chunk, 0], FAR + chunk, right_x)
        x_send(term_own.at[chunk, far_x, high], far_in.at[chunk, 1], FAR + chunk, left_x)
        weight_terms(chunk, core, term_own, term_in, 1, XS)
        x_send(term_own.at[chunk, right_x, high], x_in.at[chunk, 0, high], NEAR + chunk, right_x)
        x_send(term_own.at[chunk, left_x, low], x_in.at[chunk, 1, low], NEAR + chunk, left_x)
        if chunk == halves - 1:
            wait_bytes(all_weights.at[pl.ds(0, cores - 1)], gather_in.at[4])
        if chunk % halves == halves - 1:
            state_send(chunk // halves + 1)

    give_back((GROUPS - 1) * group, peers)
    returned_ref[0] = back_ref[0]

    def merge(chunk):
        wait_bytes(far_in.at[chunk], sum_in.at[FAR + chunk])
        for side, (to_x, half) in enumerate(((right_x, low), (left_x, high))):
            both = term_own[chunk, to_x, half].astype(jnp.float32)
            both = both + far_in[chunk, side].astype(jnp.float32)
            term_own[chunk, to_x, half] = both.astype(jnp.bfloat16)
            x_send(term_own.at[chunk, to_x, half], x_in.at[chunk, side, half], MERGED + chunk, to_x)

    for chunk in range(CHUNKS):
        merge(chunk)
        if chunk == 1:
            state_send(3)
    state_terms(y, part.at[0])

    for chunk in range(CHUNKS):
        wait_bytes(far_in.at[chunk], sum_in.at[NEAR + chunk])
        wait_bytes(far_in.at[chunk], sum_in.at[MERGED + chunk])

        @pl.loop(0, ZS)
        def _(to_z):
            total = term_own[chunk, x, to_z].astype(jnp.float32)
            for other in range(2):
                total = total + x_in[chunk, other, to_z].astype(jnp.float32)
            z_own[chunk, to_z] = total.astype(jnp.bfloat16)

        @pl.loop(1, ZS)
        def _(offset):
            to_z = lax.rem(z + offset, ZS)
            there = (core, x * ZS + to_z, y)
            piece = z_own.at[chunk, to_z]
            at = ALONG_Z + chunk
            send(piece, z_in.at[chunk, offset - 1], sum_out.at[at], sum_in.at[at], there)

    wait_bytes(part_in, state_sem.at[1])
    total = part[0].astype(jnp.float32)
    for other in range(ys - 1):
        total = total + part_in[other].astype(jnp.float32)
    state_out[...] = total.astype(jnp.bfloat16)

    for chunk in range(CHUNKS):
        columns = slice(chunk % halves * chunk_width, (chunk % halves + 1) * chunk_width)
        wait_bytes(z_in.at[chunk], sum_in.at[ALONG_Z + chunk])
        total = z_own[chunk, z].astype(jnp.float32)
        for other in range(ZS - 1):
            total = total + z_in[chunk, other].astype(jnp.float32)
        piece_away[chunk // halves, :, columns] = total.astype(jnp.bfloat16)

    @pl.when(away)
    def _():
        send(piece_away, piece_out, state_sem.at[2], state_sem.at[3], partner_of(core, x, y, z))
        wait_bytes(piece_out, state_sem.at[3])
        wait_bytes(piece_away, state_sem.at[2])

    @pl.when(jnp.logical_not(away))
    def _():
        piece_out[...] = piece_away[...]

    wait_bytes(returned_ref.at[pl.ds(1, peers - 1)], row_in.at[GROUPS])
    wait_bytes(send_ref.at[pl.ds(1, peers - 1)], row_out.at[0])
    wait_bytes(back_ref.at[pl.ds(1, peers - 1)], row_out.at[1])
    wait_bytes(all_states.at[pl.ds(0, ys - 1)], gather_out.at[1])
    wait_bytes(all_weights.at[0, 0, pl.ds(0, 2)], gather_out.at[2])
    for hop in range(1, ZS // 2):
        last = hop == ZS // 2 - 1
        wait_bytes(all_weights.at[0, 0, 0 if last else pl.ds(0, 2)], gather_out.at[4 + hop])
    wait_bytes(all_weights.at[0, pl.ds(0, XS - 1)], gather_out.at[3])
    wait_bytes(all_weights.at[pl.ds(0, cores - 1)], gather_out.at[4])
    for chunk in range(CHUNKS):
        wait_bytes(term_away.at[chunk], sum_out.at[CORE + chunk])
        for stage in (FAR, NEAR, MERGED):
            wait_bytes(far_in.at[chunk], sum_out.at[stage + chunk])
        wait_bytes(z_in.at[chunk], sum_out.at[ALONG_Z + chunk])
    wait_bytes(part_in, state_sem.at[0])


def whole(length, packed, keys, values, states, weights, cores, ys):
    smem, vmem = pl.BlockSpec(memory_space=pltpu.SMEM), pl.BlockSpec(memory_space=pltpu.VMEM)
    hbm = pl.BlockSpec(memory_space=pl.ANY)
    wire = packed.dtype
    peers, _, peer_rows, width = packed.shape
    src_len, features = states.shape
    unit_rows = weights.shape[0]
    piece = (2, unit_rows, features)
    chunk_width = features * 2 // CHUNKS
    terms = (CHUNKS, XS, ZS, unit_rows, chunk_width)
    return pl.pallas_call(
        functools.partial(whole_kernel, cores, ys),
        out_shape=(
            jax.ShapeDtypeStruct((peers, peer_rows, width), wire),
            jax.ShapeDtypeStruct((src_len, features), wire),
            jax.ShapeDtypeStruct(piece, wire),
        ),
        in_specs=[smem, vmem, hbm, hbm, hbm, vmem],
        out_specs=(vmem, vmem, vmem),
        scratch_shapes=[
            pltpu.VMEM(packed.shape, wire),
            pltpu.VMEM((peers, peer_rows, width), wire),
            pltpu.VMEM((src_len, width), wire),
            pltpu.VMEM((src_len, width), wire),
            pltpu.VMEM((width, src_len), wire),
            pltpu.VMEM((src_len, width), jnp.float32),
            pltpu.VMEM((src_len, width), jnp.float32),
            pltpu.VMEM((2, src_len, width), wire),
            pltpu.VMEM((2, width, src_len), wire),
            pltpu.VMEM((ys, src_len, features), wire),
            pltpu.VMEM((cores, XS, ZS, *piece), wire),
            pltpu.VMEM(terms, wire),
            pltpu.VMEM(terms, wire),
            pltpu.VMEM(terms, wire),
            pltpu.VMEM((CHUNKS, 2, ZS // 2, *terms[3:]), wire),
            pltpu.VMEM((CHUNKS, 2, *terms[2:]), wire),
            pltpu.VMEM((CHUNKS, *terms[2:]), wire),
            pltpu.VMEM((CHUNKS, ZS - 1, *terms[3:]), wire),
            pltpu.VMEM((ys, src_len, features), wire),
            pltpu.VMEM((ys - 1, src_len, features), wire),
            pltpu.VMEM(piece, wire),
            pltpu.VMEM(piece, wire),
            pltpu.SemaphoreType.DMA((GROUPS + 1,)),
            pltpu.SemaphoreType.DMA((2,)),
            pltpu.SemaphoreType.DMA((8,)),
            pltpu.SemaphoreType.DMA((8,)),
            pltpu.SemaphoreType.DMA((5 * CHUNKS,)),
            pltpu.SemaphoreType.DMA((5 * CHUNKS,)),
            pltpu.SemaphoreType.DMA((4,)),
            pltpu.SemaphoreType.DMA((5,)),
        ],
        compiler_params=pltpu.CompilerParams(
            collective_id=1, has_side_effects=True, vmem_limit_bytes=56 << 20
        ),
        name="exchange_attend_reduce",
    )(length, packed, keys, values, states, weights)


def on_device(queries, out_grads, owners, src_keys, src_values, states, kv_weight, src_lengths):
    cores, ys = lax.axis_size("grp"), lax.axis_size("mdl")
    peers = cores * XS * ZS
    tgt_len = queries.shape[1]
    packed = pack(owners, queries, out_grads, peers)
    returned, state_sum, weight_sum = whole(
        src_lengths, packed, src_keys[0], src_values[0], states[0], kv_weight, cores, ys
    )
    return unpack(owners, returned, state_sum, weight_sum, tgt_len)


def solution(mesh):
    rows = P(ROWS, None, "mdl")
    return jax.shard_map(
        on_device,
        mesh=mesh,
        in_specs=(rows, rows, P(ROWS), rows, rows, rows, rows, P(ROWS)),
        out_specs=(rows, rows, rows),
        check_vma=False,
    )
```

```python
import functools
import math

import jax
import jax.numpy as jnp
from jax import lax
from jax.experimental import pallas as pl
from jax.experimental.pallas import tpu as pltpu
from jax.sharding import PartitionSpec as P

HEAD_DIM = 64
LANES = 128
ROWS = ("grp", "seq")
MESH = pl.DeviceIdType.MESH
XS, ZS, GROUPS, CHUNKS = 4, 8, 4, 4


def place():
    seq = lax.axis_index("seq")
    return lax.axis_index("grp"), lax.div(seq, ZS), lax.axis_index("mdl"), lax.rem(seq, ZS)


def in_plane(core, x, y, z, offset, cores):
    to_core = lax.rem(core + lax.div(offset, XS * ZS), cores)
    to_x = lax.rem(x + lax.rem(lax.div(offset, ZS), XS), XS)
    to_z = lax.rem(z + lax.rem(offset, ZS), ZS)
    return (to_core, to_x * ZS + to_z, y)


def back_in_plane(core, x, y, z, offset, cores):
    to_core = lax.rem(core + cores - lax.div(offset, XS * ZS), cores)
    to_x = lax.rem(x + XS - lax.rem(lax.div(offset, ZS), XS), XS)
    to_z = lax.rem(z + ZS - lax.rem(offset, ZS), ZS)
    return (to_core, to_x * ZS + to_z, y)


def partner_of(core, x, y, z):
    half = XS // 2
    to_x = lax.rem(y, 2) * half + lax.rem(x, half)
    return (lax.div(y, 2), to_x * ZS + z, core * 2 + lax.div(x, half))


def in_column(partner, z, offset):
    return (partner[0], lax.div(partner[1], ZS) * ZS + lax.rem(z + offset, ZS), partner[2])


def greet(core, x, y, z, cores, ys, partner, away):
    barrier = pltpu.get_barrier_semaphore()
    peers = cores * XS * ZS

    @pl.loop(1, peers)
    def _(offset):
        there = in_plane(core, x, y, z, offset, cores)
        pl.semaphore_signal(barrier, inc=1, device_id=there, device_id_type=MESH)

    @pl.loop(1, ys)
    def _(offset):
        there = (core, x * ZS + z, lax.rem(y + offset, ys))
        pl.semaphore_signal(barrier, inc=1, device_id=there, device_id_type=MESH)

    @pl.when(away)
    def _():
        @pl.loop(0, ZS)
        def _(offset):
            there = in_column(partner, z, offset)
            pl.semaphore_signal(barrier, inc=1, device_id=there, device_id_type=MESH)

    pl.semaphore_wait(barrier, peers + ys - 2 + ZS * away.astype(jnp.int32))


def send(source, target, send_sem, recv_sem, there):
    pltpu.make_async_remote_copy(
        src_ref=source,
        dst_ref=target,
        send_sem=send_sem,
        recv_sem=recv_sem,
        device_id=there,
        device_id_type=MESH,
    ).start()


def wait_bytes(ref, sem):
    pltpu.make_async_copy(ref, ref, sem).wait()


def dot(left, right, dims):
    return lax.dot_general(left, right, (dims, ((), ())), preferred_element_type=jnp.float32)


def peer_of(owner, core, x, z):
    to_core = (lax.shift_right_logical(owner, 5) - core) & 1
    to_x = (lax.shift_right_logical(owner, 3) - x) & (XS - 1)
    to_z = (owner - z) & (ZS - 1)
    return (to_core * XS + to_x) * ZS + to_z


def pack_kernel(owners_ref, query_ref, grad_ref, out_ref, first_ref, second_ref):
    peers = out_ref.shape[0]
    core, x, _, z = place()

    @pl.loop(0, peers, unroll=8)
    def _(peer):
        first_ref[peer] = -1
        second_ref[peer] = -1

    @pl.loop(0, query_ref.shape[0], unroll=4)
    def _(target):
        peer = peer_of(owners_ref[target], core, x, z)
        first = first_ref[peer]
        first_ref[peer] = jnp.where(first < 0, target, first)
        second_ref[peer] = jnp.where(first < 0, -1, target)

    @pl.loop(0, peers, unroll=8)
    def _(peer):
        for kind, ref in enumerate((query_ref, grad_ref)):
            rows = []
            for target in (first_ref[peer], second_ref[peer]):
                row = ref[jnp.maximum(target, 0)]
                rows.append(jnp.where(target < 0, jnp.zeros_like(row), row))
            out_ref[peer, kind] = jnp.concatenate(rows, axis=0)


def pack(owners, queries, out_grads, peers):
    _, tgt_len, width = queries.shape
    smem, vmem = pl.BlockSpec(memory_space=pltpu.SMEM), pl.BlockSpec(memory_space=pltpu.VMEM)
    return pl.pallas_call(
        pack_kernel,
        out_shape=jax.ShapeDtypeStruct((peers, 2, 2 * tgt_len, width), queries.dtype),
        in_specs=[smem, vmem, vmem],
        out_specs=vmem,
        scratch_shapes=[pltpu.SMEM((peers,), jnp.int32), pltpu.SMEM((peers,), jnp.int32)],
        name="pack_targets",
    )(owners, queries, out_grads)


def unpack_kernel(
    owners_ref, back_ref, state_ref, weight_ref, out_ref, state_out, weight_out, used_ref, slot_ref
):
    targets, tgt_len, _ = out_ref.shape
    core, x, _, z = place()

    @pl.loop(0, back_ref.shape[0], unroll=8)
    def _(peer):
        used_ref[peer] = 0

    @pl.loop(0, targets, unroll=4)
    def _(target):
        peer = peer_of(owners_ref[target], core, x, z)
        used = used_ref[peer]
        used_ref[peer] = 1
        slot_ref[target] = peer * 2 + used

    @pl.loop(0, targets, unroll=8)
    def _(target):
        slot = slot_ref[target]
        both = back_ref[lax.shift_right_logical(slot, 1)]
        out_ref[target] = jnp.where((slot & 1) == 0, both[:tgt_len], both[tgt_len:])

    state_out[0] = state_ref[...]
    for kind in range(2):
        weight_out[:, kind, :] = weight_ref[kind].astype(jnp.float32)


def unpack(owners, returned, state, weight, tgt_len):
    peers, _, width = returned.shape
    targets = owners.shape[0]
    kinds, unit_rows, features = weight.shape
    smem, vmem = pl.BlockSpec(memory_space=pltpu.SMEM), pl.BlockSpec(memory_space=pltpu.VMEM)
    return pl.pallas_call(
        unpack_kernel,
        out_shape=(
            jax.ShapeDtypeStruct((targets, tgt_len, width), returned.dtype),
            jax.ShapeDtypeStruct((1, *state.shape), state.dtype),
            jax.ShapeDtypeStruct((unit_rows, kinds, features), jnp.float32),
        ),
        in_specs=[smem, vmem, vmem, vmem],
        out_specs=(vmem, vmem, vmem),
        scratch_shapes=[pltpu.SMEM((peers,), jnp.int32), pltpu.SMEM((targets,), jnp.int32)],
        name="unpack_targets",
    )(owners, returned, state, weight)


def whole_kernel(
    cores,
    ys,
    length_ref,
    send_ref,
    key_hbm,
    value_hbm,
    states_hbm,
    weight_ref,
    returned_ref,
    state_out,
    piece_out,
    got_ref,
    back_ref,
    key_ref,
    value_ref,
    key_t,
    key_sums,
    value_sums,
    grads,
    grads_t,
    all_states,
    all_weights,
    term_away,
    term_own,
    term_in,
    far_in,
    x_in,
    z_own,
    z_in,
    part,
    part_in,
    piece_away,
    piece_ref,
    row_in,
    row_out,
    gather_in,
    gather_out,
    sum_in,
    sum_out,
    state_sem,
    own_sem,
):
    core, x, y, z = place()
    peers = cores * XS * ZS
    group = peers // GROUPS
    partner = partner_of(core, x, y, z)
    away = partner[2] != y
    src_len, width = key_ref.shape
    unit_rows, chunk_width = term_own.shape[3:]
    features = all_states.shape[2]
    halves = CHUNKS // 2
    half_rows = ZS * unit_rows
    scale = HEAD_DIM**-0.5
    exp_scale = scale * math.log2(math.e)
    rows = group * got_ref.shape[2]

    own_keys = pltpu.make_async_copy(key_hbm, key_ref, own_sem.at[0])
    own_values = pltpu.make_async_copy(value_hbm, value_ref, own_sem.at[1])
    own_states = pltpu.make_async_copy(states_hbm, all_states.at[y], own_sem.at[2])
    own_rows = pltpu.make_async_copy(send_ref.at[0], got_ref.at[0], own_sem.at[3])
    for copy in (own_keys, own_values, own_states, own_rows):
        copy.start()
    for kind in range(2):
        piece_ref[kind] = weight_ref[:, kind, :]
    greet(core, x, y, z, cores, ys, partner, away)

    to_core, to_x = partner[0], lax.div(partner[1], ZS)
    own_piece = pltpu.make_async_copy(piece_ref, all_weights.at[core, x, z], own_sem.at[4])

    for offset in (1, ZS - 1):
        there = in_column(partner, z, offset)
        send(piece_ref, all_weights.at[to_core, to_x, z], gather_out.at[2], gather_in.at[2], there)

    @pl.when(away)
    def _():
        there = partner_of(core, x, y, z)
        send(piece_ref, all_weights.at[to_core, to_x, z], gather_out.at[0], gather_in.at[0], there)

    @pl.when(jnp.logical_not(away))
    def _():
        own_piece.start()

    @pl.loop(1, ys)
    def _(offset):
        there = (core, x * ZS + z, lax.rem(y + offset, ys))
        send(states_hbm, all_states.at[y], gather_out.at[1], gather_in.at[1], there)

    def dispatch(first, last):
        @pl.loop(first, last)
        def _(offset):
            there = in_plane(core, x, y, z, offset, cores)
            at = lax.div(offset, group)
            send(send_ref.at[offset], got_ref.at[offset], row_out.at[0], row_in.at[at], there)

    dispatch(1, 2 * group)
    key_sums[...] = jnp.zeros_like(key_sums)
    value_sums[...] = jnp.zeros_like(value_sums)
    own_keys.wait()
    own_values.wait()
    key_t[...] = jnp.transpose(key_ref[...])
    own_rows.wait()

    @pl.when(away)
    def _():
        wait_bytes(piece_ref, gather_in.at[0])
        wait_bytes(piece_ref, gather_out.at[0])

    @pl.when(jnp.logical_not(away))
    def _():
        own_piece.wait()

    def hand_on(hop):
        up = (core, x * ZS + lax.rem(z + 1, ZS), y)
        down = (core, x * ZS + lax.rem(z + ZS - 1, ZS), y)
        from_down = all_weights.at[core, x, lax.rem(z + ZS - hop, ZS)]
        from_up = all_weights.at[core, x, lax.rem(z + hop, ZS)]
        at = 4 + hop
        wait_bytes(all_weights.at[0, 0, pl.ds(0, 2)], gather_in.at[2 if hop == 1 else at - 1])
        if hop < ZS // 2 - 1:
            send(from_down, from_down, gather_out.at[at], gather_in.at[at], up)
            send(from_up, from_up, gather_out.at[at], gather_in.at[at], down)
        else:
            send(from_down.at[0], from_down.at[0], gather_out.at[at], gather_in.at[at], up)
            send(from_up.at[1], from_up.at[1], gather_out.at[at], gather_in.at[at], down)

    hand_on(1)

    def give_back(first, last):
        @pl.loop(first, last)
        def _(offset):
            there = back_in_plane(core, x, y, z, offset, cores)
            send(back_ref.at[offset], returned_ref.at[offset], row_out.at[1], row_in.at[GROUPS], there)

    @pl.loop(0, GROUPS)
    def _(step):
        start = step * group

        @pl.when(step == 0)
        def _():
            wait_bytes(got_ref.at[pl.ds(1, group - 1)], row_in.at[0])

        @pl.when(step > 0)
        def _():
            wait_bytes(got_ref.at[pl.ds(start, group)], row_in.at[step])

        @pl.when(step < GROUPS - 2)
        def _():
            dispatch((step + 2) * group, (step + 3) * group)

        @pl.when(step == 0)
        def _():
            hand_on(2)

        @pl.when(step == 1)
        def _():
            wait_bytes(all_weights.at[0, 0, 0], gather_in.at[7])

            @pl.loop(1, XS)
            def _(offset):
                there = (core, lax.rem(x + offset, XS) * ZS + z, y)
                line = all_weights.at[core, x]
                send(line, line, gather_out.at[3], gather_in.at[3], there)

        @pl.when(step == GROUPS - 1)
        def _():
            wait_bytes(all_weights.at[0, pl.ds(0, XS - 1)], gather_in.at[3])

            @pl.loop(1, cores)
            def _(offset):
                there = (lax.rem(core + offset, cores), x * ZS + z, y)
                half = all_weights.at[core]
                send(half, half, gather_out.at[4], gather_in.at[4], there)

        @pl.when(step == GROUPS - 1)
        def _():
            give_back(1, (GROUPS - 1) * group)

        valid = lax.broadcasted_iota(jnp.int32, (src_len, rows), 0) < length_ref[0]
        lane = lax.broadcasted_iota(jnp.int32, (rows, LANES), 1)
        for pair in range(width // LANES):
            at = slice(pair * LANES, (pair + 1) * LANES)
            query = got_ref[pl.ds(start, group), 0, :, at].reshape(rows, LANES)
            grad = got_ref[pl.ds(start, group), 1, :, at].reshape(rows, LANES)
            keys = key_ref[:, at]
            values = value_ref[:, at]
            key_sum = key_sums[:, at]
            value_sum = value_sums[:, at]
            back = []
            for half in range(LANES // HEAD_DIM):
                own = (lane >= half * HEAD_DIM) & (lane < (half + 1) * HEAD_DIM)
                query_h = jnp.where(own, query, jnp.zeros_like(query))
                grad_h = jnp.where(own, grad, jnp.zeros_like(grad))
                scores = dot(keys, query_h, ((1,), (1,)))
                scores = jnp.where(valid, scores, -1e30)
                peak = jnp.max(scores, axis=0, keepdims=True)
                terms = jnp.exp2((scores - peak) * exp_scale)
                probs = terms * (1.0 / jnp.sum(terms, axis=0, keepdims=True))
                probs_b = probs.astype(jnp.bfloat16)
                prob_grad = dot(values, grad_h, ((1,), (1,)))
                delta = jnp.sum(probs_b.astype(jnp.float32) * prob_grad, axis=0, keepdims=True)
                score_grad = (probs * (prob_grad - delta)).astype(jnp.bfloat16)
                key_sum = key_sum + dot(score_grad, query_h, ((1,), (0,)))
                value_sum = value_sum + dot(probs_b, grad_h, ((1,), (0,)))
                head = pair * LANES + half * HEAD_DIM
                back.append(dot(key_t[head : head + HEAD_DIM, :], score_grad, ((1,), (0,))))
            key_sums[:, at] = key_sum
            value_sums[:, at] = value_sum
            back = jnp.concatenate(back, axis=0) * scale
            back = jnp.transpose(back).astype(jnp.bfloat16)
            back_ref[pl.ds(start, group), :, at] = back.reshape(group, rows // group, LANES)

        @pl.when(step == 0)
        def _():
            hand_on(3)

    def weight_terms(chunk, to_core, target, added, first_x, last_x):
        columns = slice(chunk % halves * chunk_width, (chunk % halves + 1) * chunk_width)

        @pl.loop(first_x, last_x)
        def _(step_x):
            to_x = lax.rem(x + XS // 2 + step_x, XS)
            block = to_core * (XS // 2) + lax.div(to_x, 2)
            first = pl.multiple_of(lax.rem(to_x, 2) * half_rows, half_rows)
            left = grads_t[chunk // halves, pl.ds(first, half_rows), :]
            terms = dot(left, all_states[block, :, columns], ((1,), (0,)))
            if added is not None:
                terms = terms + added[chunk, to_x].reshape(half_rows, chunk_width).astype(jnp.float32)
            target[chunk, to_x] = terms.astype(jnp.bfloat16).reshape(ZS, unit_rows, chunk_width)

    CORE, FAR, NEAR, MERGED, ALONG_Z = (CHUNKS * stage for stage in range(5))
    own_states.wait()
    wait_bytes(all_states.at[pl.ds(0, ys - 1)], gather_in.at[1])
    sibling = lax.rem(core + 1, cores)
    for chunk in range(CHUNKS):
        kind = chunk // halves
        if chunk % halves == 0:
            sums = key_sums[...] * scale if kind == 0 else value_sums[...]
            grads[kind] = sums.astype(jnp.bfloat16)
            grads_t[kind] = jnp.transpose(grads[kind])
        weight_terms(chunk, sibling, term_away, None, 0, XS)
        there = (sibling, x * ZS + z, y)
        at = CORE + chunk
        send(term_away.at[chunk], term_in.at[chunk], sum_out.at[at], sum_in.at[at], there)


    def state_terms(block, target):
        for kind in range(2):
            lines = all_weights[lax.div(block, 2), pl.ds(lax.rem(block, 2) * 2, 2), :, kind]
            terms = dot(grads[kind], lines.reshape(width, features), ((1,), (0,)))
            total = terms if kind == 0 else total + terms
        target[...] = total.astype(jnp.bfloat16)

    def state_send(offset):
        to_y = lax.rem(y + offset, ys)
        state_terms(to_y, part.at[offset])
        there = (core, x * ZS + z, to_y)
        send(part.at[offset], part_in.at[offset - 1], state_sem.at[0], state_sem.at[1], there)

    low, high = pl.ds(0, ZS // 2), pl.ds(ZS // 2, ZS // 2)
    right_x, far_x, left_x = (lax.rem(x + offset, XS) for offset in range(1, XS))

    def x_send(source, target, sem, to_x):
        send(source, target, sum_out.at[sem], sum_in.at[sem], (core, to_x * ZS + z, y))

    for chunk in range(CHUNKS):
        wait_bytes(term_in.at[chunk], sum_in.at[CORE + chunk])
        weight_terms(chunk, core, term_own, term_in, 0, 1)
        x_send(term_own.at[chunk, far_x, low], far_in.at[chunk, 0], FAR + chunk, right_x)
        x_send(term_own.at[chunk, far_x, high], far_in.at[chunk, 1], FAR + chunk, left_x)
        weight_terms(chunk, core, term_own, term_in, 1, XS)
        x_send(term_own.at[chunk, right_x, high], x_in.at[chunk, 0, high], NEAR + chunk, right_x)
        x_send(term_own.at[chunk, left_x, low], x_in.at[chunk, 1, low], NEAR + chunk, left_x)
        if chunk == halves - 1:
            wait_bytes(all_weights.at[pl.ds(0, cores - 1)], gather_in.at[4])
        if chunk % halves == halves - 1:
            state_send(chunk // halves + 1)

    give_back((GROUPS - 1) * group, peers)
    returned_ref[0] = back_ref[0]

    def merge(chunk):
        wait_bytes(far_in.at[chunk], sum_in.at[FAR + chunk])
        for side, (to_x, half) in enumerate(((right_x, low), (left_x, high))):
            both = term_own[chunk, to_x, half].astype(jnp.float32)
            both = both + far_in[chunk, side].astype(jnp.float32)
            term_own[chunk, to_x, half] = both.astype(jnp.bfloat16)
            x_send(term_own.at[chunk, to_x, half], x_in.at[chunk, side, half], MERGED + chunk, to_x)

    for chunk in range(CHUNKS):
        merge(chunk)
        if chunk == 1:
            state_send(3)
    state_terms(y, part.at[0])

    for chunk in range(CHUNKS):
        wait_bytes(far_in.at[chunk], sum_in.at[NEAR + chunk])
        wait_bytes(far_in.at[chunk], sum_in.at[MERGED + chunk])

        @pl.loop(0, ZS)
        def _(to_z):
            total = term_own[chunk, x, to_z].astype(jnp.float32)
            for other in range(2):
                total = total + x_in[chunk, other, to_z].astype(jnp.float32)
            z_own[chunk, to_z] = total.astype(jnp.bfloat16)

        @pl.loop(1, ZS)
        def _(offset):
            to_z = lax.rem(z + offset, ZS)
            there = (core, x * ZS + to_z, y)
            piece = z_own.at[chunk, to_z]
            at = ALONG_Z + chunk
            send(piece, z_in.at[chunk, offset - 1], sum_out.at[at], sum_in.at[at], there)

    wait_bytes(part_in, state_sem.at[1])
    total = part[0].astype(jnp.float32)
    for other in range(ys - 1):
        total = total + part_in[other].astype(jnp.float32)
    state_out[...] = total.astype(jnp.bfloat16)

    for chunk in range(CHUNKS):
        columns = slice(chunk % halves * chunk_width, (chunk % halves + 1) * chunk_width)
        wait_bytes(z_in.at[chunk], sum_in.at[ALONG_Z + chunk])
        total = z_own[chunk, z].astype(jnp.float32)
        for other in range(ZS - 1):
            total = total + z_in[chunk, other].astype(jnp.float32)
        piece_away[chunk // halves, :, columns] = total.astype(jnp.bfloat16)

    @pl.when(away)
    def _():
        send(piece_away, piece_out, state_sem.at[2], state_sem.at[3], partner_of(core, x, y, z))
        wait_bytes(piece_out, state_sem.at[3])
        wait_bytes(piece_away, state_sem.at[2])

    @pl.when(jnp.logical_not(away))
    def _():
        piece_out[...] = piece_away[...]

    wait_bytes(returned_ref.at[pl.ds(1, peers - 1)], row_in.at[GROUPS])
    wait_bytes(send_ref.at[pl.ds(1, peers - 1)], row_out.at[0])
    wait_bytes(back_ref.at[pl.ds(1, peers - 1)], row_out.at[1])
    wait_bytes(all_states.at[pl.ds(0, ys - 1)], gather_out.at[1])
    wait_bytes(all_weights.at[0, 0, pl.ds(0, 2)], gather_out.at[2])
    for hop in range(1, ZS // 2):
        last = hop == ZS // 2 - 1
        wait_bytes(all_weights.at[0, 0, 0 if last else pl.ds(0, 2)], gather_out.at[4 + hop])
    wait_bytes(all_weights.at[0, pl.ds(0, XS - 1)], gather_out.at[3])
    wait_bytes(all_weights.at[pl.ds(0, cores - 1)], gather_out.at[4])
    for chunk in range(CHUNKS):
        wait_bytes(term_away.at[chunk], sum_out.at[CORE + chunk])
        for stage in (FAR, NEAR, MERGED):
            wait_bytes(far_in.at[chunk], sum_out.at[stage + chunk])
        wait_bytes(z_in.at[chunk], sum_out.at[ALONG_Z + chunk])
    wait_bytes(part_in, state_sem.at[0])


def whole(length, packed, keys, values, states, weights, cores, ys):
    smem, vmem = pl.BlockSpec(memory_space=pltpu.SMEM), pl.BlockSpec(memory_space=pltpu.VMEM)
    hbm = pl.BlockSpec(memory_space=pl.ANY)
    wire = packed.dtype
    peers, _, peer_rows, width = packed.shape
    src_len, features = states.shape
    unit_rows = weights.shape[0]
    piece = (2, unit_rows, features)
    chunk_width = features * 2 // CHUNKS
    terms = (CHUNKS, XS, ZS, unit_rows, chunk_width)
    return pl.pallas_call(
        functools.partial(whole_kernel, cores, ys),
        out_shape=(
            jax.ShapeDtypeStruct((peers, peer_rows, width), wire),
            jax.ShapeDtypeStruct((src_len, features), wire),
            jax.ShapeDtypeStruct(piece, wire),
        ),
        in_specs=[smem, vmem, hbm, hbm, hbm, vmem],
        out_specs=(vmem, vmem, vmem),
        scratch_shapes=[
            pltpu.VMEM(packed.shape, wire),
            pltpu.VMEM((peers, peer_rows, width), wire),
            pltpu.VMEM((src_len, width), wire),
            pltpu.VMEM((src_len, width), wire),
            pltpu.VMEM((width, src_len), wire),
            pltpu.VMEM((src_len, width), jnp.float32),
            pltpu.VMEM((src_len, width), jnp.float32),
            pltpu.VMEM((2, src_len, width), wire),
            pltpu.VMEM((2, width, src_len), wire),
            pltpu.VMEM((ys, src_len, features), wire),
            pltpu.VMEM((cores, XS, ZS, *piece), wire),
            pltpu.VMEM(terms, wire),
            pltpu.VMEM(terms, wire),
            pltpu.VMEM(terms, wire),
            pltpu.VMEM((CHUNKS, 2, ZS // 2, *terms[3:]), wire),
            pltpu.VMEM((CHUNKS, 2, *terms[2:]), wire),
            pltpu.VMEM((CHUNKS, *terms[2:]), wire),
            pltpu.VMEM((CHUNKS, ZS - 1, *terms[3:]), wire),
            pltpu.VMEM((ys, src_len, features), wire),
            pltpu.VMEM((ys - 1, src_len, features), wire),
            pltpu.VMEM(piece, wire),
            pltpu.VMEM(piece, wire),
            pltpu.SemaphoreType.DMA((GROUPS + 1,)),
            pltpu.SemaphoreType.DMA((2,)),
            pltpu.SemaphoreType.DMA((8,)),
            pltpu.SemaphoreType.DMA((8,)),
            pltpu.SemaphoreType.DMA((5 * CHUNKS,)),
            pltpu.SemaphoreType.DMA((5 * CHUNKS,)),
            pltpu.SemaphoreType.DMA((4,)),
            pltpu.SemaphoreType.DMA((5,)),
        ],
        compiler_params=pltpu.CompilerParams(
            collective_id=1, has_side_effects=True, vmem_limit_bytes=56 << 20
        ),
        name="exchange_attend_reduce",
    )(length, packed, keys, values, states, weights)


def on_device(queries, out_grads, owners, src_keys, src_values, states, kv_weight, src_lengths):
    cores, ys = lax.axis_size("grp"), lax.axis_size("mdl")
    peers = cores * XS * ZS
    tgt_len = queries.shape[1]
    packed = pack(owners, queries, out_grads, peers)
    returned, state_sum, weight_sum = whole(
        src_lengths, packed, src_keys[0], src_values[0], states[0], kv_weight, cores, ys
    )
    return unpack(owners, returned, state_sum, weight_sum, tgt_len)


def solution(mesh):
    rows = P(ROWS, None, "mdl")
    return jax.shard_map(
        on_device,
        mesh=mesh,
        in_specs=(rows, rows, P(ROWS), rows, rows, rows, rows, P(ROWS)),
        out_specs=(rows, rows, rows),
        check_vma=False,
    )
```

```python
import functools
import math

import jax
import jax.numpy as jnp
from jax import lax
from jax.experimental import pallas as pl
from jax.experimental.pallas import tpu as pltpu
from jax.sharding import PartitionSpec as P

HEAD_DIM = 64
LANES = 128
ROWS = ("grp", "seq")
MESH = pl.DeviceIdType.MESH
XS, ZS, GROUPS, CHUNKS = 4, 8, 4, 4


def place():
    seq = lax.axis_index("seq")
    return lax.axis_index("grp"), lax.div(seq, ZS), lax.axis_index("mdl"), lax.rem(seq, ZS)


def in_plane(core, x, y, z, offset, cores):
    to_core = lax.rem(core + lax.div(offset, XS * ZS), cores)
    to_x = lax.rem(x + lax.rem(lax.div(offset, ZS), XS), XS)
    to_z = lax.rem(z + lax.rem(offset, ZS), ZS)
    return (to_core, to_x * ZS + to_z, y)


def back_in_plane(core, x, y, z, offset, cores):
    to_core = lax.rem(core + cores - lax.div(offset, XS * ZS), cores)
    to_x = lax.rem(x + XS - lax.rem(lax.div(offset, ZS), XS), XS)
    to_z = lax.rem(z + ZS - lax.rem(offset, ZS), ZS)
    return (to_core, to_x * ZS + to_z, y)


def partner_of(core, x, y, z):
    half = XS // 2
    to_x = lax.rem(y, 2) * half + lax.rem(x, half)
    return (lax.div(y, 2), to_x * ZS + z, core * 2 + lax.div(x, half))


def in_column(partner, z, offset):
    return (partner[0], lax.div(partner[1], ZS) * ZS + lax.rem(z + offset, ZS), partner[2])


def greet(core, x, y, z, cores, ys, partner, away):
    barrier = pltpu.get_barrier_semaphore()
    peers = cores * XS * ZS

    @pl.loop(1, peers)
    def _(offset):
        there = in_plane(core, x, y, z, offset, cores)
        pl.semaphore_signal(barrier, inc=1, device_id=there, device_id_type=MESH)

    @pl.loop(1, ys)
    def _(offset):
        there = (core, x * ZS + z, lax.rem(y + offset, ys))
        pl.semaphore_signal(barrier, inc=1, device_id=there, device_id_type=MESH)

    @pl.when(away)
    def _():
        @pl.loop(0, ZS)
        def _(offset):
            there = in_column(partner, z, offset)
            pl.semaphore_signal(barrier, inc=1, device_id=there, device_id_type=MESH)

    pl.semaphore_wait(barrier, peers + ys - 2 + ZS * away.astype(jnp.int32))


def send(source, target, send_sem, recv_sem, there):
    pltpu.make_async_remote_copy(
        src_ref=source,
        dst_ref=target,
        send_sem=send_sem,
        recv_sem=recv_sem,
        device_id=there,
        device_id_type=MESH,
    ).start()


def wait_bytes(ref, sem):
    pltpu.make_async_copy(ref, ref, sem).wait()


def dot(left, right, dims):
    return lax.dot_general(left, right, (dims, ((), ())), preferred_element_type=jnp.float32)


def peer_of(owner, core, x, z):
    to_core = (lax.shift_right_logical(owner, 5) - core) & 1
    to_x = (lax.shift_right_logical(owner, 3) - x) & (XS - 1)
    to_z = (owner - z) & (ZS - 1)
    return (to_core * XS + to_x) * ZS + to_z


def row_slots(owners_ref, core, x, z, tgt_len):
    targets = owners_ref.shape[1]
    peer_row = jnp.broadcast_to(peer_of(owners_ref[...], core, x, z), (targets, targets))
    down = lax.broadcasted_iota(jnp.int32, (targets, targets), 0)
    across = lax.broadcasted_iota(jnp.int32, (targets, targets), 1)
    peer = jnp.sum(jnp.where(down == across, peer_row, 0), axis=1, keepdims=True)
    earlier = (peer_row == peer) & (across < down)
    slot = peer * 2 + jnp.sum(jnp.where(earlier, 1, 0), axis=1, keepdims=True)
    shape = (targets, targets * tgt_len)
    token = lax.broadcasted_iota(jnp.int32, shape, 1)
    first = lax.broadcasted_iota(jnp.int32, shape, 0) * tgt_len
    here = (token >= first) & (token < first + tgt_len)
    return jnp.sum(jnp.where(here, slot * tgt_len + token - first, 0), axis=0, keepdims=True)


def unpack_kernel(
    owners_ref, back_ref, state_ref, weight_ref, out_ref, state_out, weight_out, used_ref, slot_ref
):
    targets, tgt_len, _ = out_ref.shape
    core, x, _, z = place()

    @pl.loop(0, back_ref.shape[0], unroll=8)
    def _(peer):
        used_ref[peer] = 0

    @pl.loop(0, targets, unroll=4)
    def _(target):
        peer = peer_of(owners_ref[target], core, x, z)
        used = used_ref[peer]
        used_ref[peer] = 1
        slot_ref[target] = peer * 2 + used

    @pl.loop(0, targets, unroll=8)
    def _(target):
        slot = slot_ref[target]
        both = back_ref[lax.shift_right_logical(slot, 1)]
        out_ref[target] = jnp.where((slot & 1) == 0, both[:tgt_len], both[tgt_len:])

    state_out[0] = state_ref[...]
    for kind in range(2):
        weight_out[:, kind, :] = weight_ref[kind].astype(jnp.float32)


def unpack(owners, returned, state, weight, tgt_len):
    peers, _, width = returned.shape
    targets = owners.shape[0]
    kinds, unit_rows, features = weight.shape
    smem, vmem = pl.BlockSpec(memory_space=pltpu.SMEM), pl.BlockSpec(memory_space=pltpu.VMEM)
    return pl.pallas_call(
        unpack_kernel,
        out_shape=(
            jax.ShapeDtypeStruct((targets, tgt_len, width), returned.dtype),
            jax.ShapeDtypeStruct((1, *state.shape), state.dtype),
            jax.ShapeDtypeStruct((unit_rows, kinds, features), jnp.float32),
        ),
        in_specs=[smem, vmem, vmem, vmem],
        out_specs=(vmem, vmem, vmem),
        scratch_shapes=[pltpu.SMEM((peers,), jnp.int32), pltpu.SMEM((targets,), jnp.int32)],
        name="unpack_targets",
    )(owners, returned, state, weight)


def whole_kernel(
    cores,
    ys,
    length_ref,
    owners_ref,
    query_hbm,
    grad_hbm,
    key_hbm,
    value_hbm,
    states_hbm,
    weight_ref,
    returned_ref,
    state_out,
    piece_out,
    query_ref,
    grad_ref,
    send_ref,
    got_ref,
    back_ref,
    key_ref,
    value_ref,
    key_t,
    key_sums,
    value_sums,
    grads,
    grads_t,
    all_states,
    all_weights,
    term_away,
    term_own,
    term_in,
    far_in,
    x_in,
    z_own,
    z_in,
    part,
    part_in,
    piece_away,
    piece_ref,
    row_in,
    row_out,
    gather_in,
    gather_out,
    sum_in,
    sum_out,
    state_sem,
    own_sem,
):
    core, x, y, z = place()
    peers = cores * XS * ZS
    group = peers // GROUPS
    partner = partner_of(core, x, y, z)
    away = partner[2] != y
    src_len, width = key_ref.shape
    unit_rows, chunk_width = term_own.shape[3:]
    features = all_states.shape[2]
    halves = CHUNKS // 2
    half_rows = ZS * unit_rows
    scale = HEAD_DIM**-0.5
    exp_scale = scale * math.log2(math.e)
    rows = group * got_ref.shape[2]

    own_keys = pltpu.make_async_copy(key_hbm, key_ref, own_sem.at[0])
    own_values = pltpu.make_async_copy(value_hbm, value_ref, own_sem.at[1])
    own_states = pltpu.make_async_copy(states_hbm, all_states.at[y], own_sem.at[2])
    own_queries = pltpu.make_async_copy(query_hbm, query_ref, own_sem.at[3])
    own_grads = pltpu.make_async_copy(grad_hbm, grad_ref, own_sem.at[5])
    for copy in (own_queries, own_grads, own_keys, own_values, own_states):
        copy.start()
    for kind in range(2):
        piece_ref[kind] = weight_ref[:, kind, :]
    greet(core, x, y, z, cores, ys, partner, away)

    to_core, to_x = partner[0], lax.div(partner[1], ZS)
    own_piece = pltpu.make_async_copy(piece_ref, all_weights.at[core, x, z], own_sem.at[4])

    @pl.loop(1, ZS)
    def _(offset):
        there = in_column(partner, z, offset)
        send(piece_ref, all_weights.at[to_core, to_x, z], gather_out.at[2], gather_in.at[2], there)

    @pl.when(away)
    def _():
        there = partner_of(core, x, y, z)
        send(piece_ref, all_weights.at[to_core, to_x, z], gather_out.at[0], gather_in.at[0], there)

    @pl.when(jnp.logical_not(away))
    def _():
        own_piece.start()

    @pl.loop(1, ys)
    def _(offset):
        there = (core, x * ZS + z, lax.rem(y + offset, ys))
        send(states_hbm, all_states.at[y], gather_out.at[1], gather_in.at[1], there)

    def dispatch(first, last):
        @pl.loop(first, last)
        def _(offset):
            there = in_plane(core, x, y, z, offset, cores)
            at = lax.div(offset, group)
            send(send_ref.at[offset], got_ref.at[offset], row_out.at[0], row_in.at[at], there)

    tgt_len = got_ref.shape[2] // 2
    taken = row_slots(owners_ref, core, x, z, tgt_len)
    own_queries.wait()
    own_grads.wait()

    def pack(at):
        slot_row = lax.broadcasted_iota(jnp.int32, (rows, taken.shape[1]), 0) + at * rows
        chosen = jnp.where(slot_row == taken, 1.0, 0.0).astype(jnp.bfloat16)
        for kind, ref in enumerate((query_ref, grad_ref)):
            filled = dot(chosen, ref[...], ((1,), (0,))).astype(jnp.bfloat16)
            send_ref[at * group : (at + 1) * group, kind] = filled.reshape(group, rows // group, width)

    pack(0)
    dispatch(1, group)
    pack(1)
    dispatch(group, 2 * group)
    got_ref[0] = send_ref[0]
    for at in range(2, GROUPS):
        pack(at)
    key_sums[...] = jnp.zeros_like(key_sums)
    value_sums[...] = jnp.zeros_like(value_sums)
    own_keys.wait()
    own_values.wait()
    key_t[...] = jnp.transpose(key_ref[...])

    @pl.when(away)
    def _():
        wait_bytes(piece_ref, gather_in.at[0])
        wait_bytes(piece_ref, gather_out.at[0])

    @pl.when(jnp.logical_not(away))
    def _():
        own_piece.wait()

    wait_bytes(all_weights.at[0, 0, pl.ds(0, ZS - 1)], gather_in.at[2])

    @pl.loop(1, XS)
    def _(offset):
        there = (core, lax.rem(x + offset, XS) * ZS + z, y)
        line = all_weights.at[core, x]
        send(line, line, gather_out.at[3], gather_in.at[3], there)

    def give_back(first, last):
        @pl.loop(first, last)
        def _(offset):
            there = back_in_plane(core, x, y, z, offset, cores)
            send(back_ref.at[offset], returned_ref.at[offset], row_out.at[1], row_in.at[GROUPS], there)

    @pl.loop(0, GROUPS)
    def _(step):
        start = step * group

        @pl.when(step == 0)
        def _():
            wait_bytes(got_ref.at[pl.ds(1, group - 1)], row_in.at[0])

        @pl.when(step > 0)
        def _():
            wait_bytes(got_ref.at[pl.ds(start, group)], row_in.at[step])

        @pl.when(step < GROUPS - 2)
        def _():
            dispatch((step + 2) * group, (step + 3) * group)

        @pl.when(step == GROUPS - 1)
        def _():
            wait_bytes(all_weights.at[0, pl.ds(0, XS - 1)], gather_in.at[3])

            @pl.loop(1, cores)
            def _(offset):
                there = (lax.rem(core + offset, cores), x * ZS + z, y)
                half = all_weights.at[core]
                send(half, half, gather_out.at[4], gather_in.at[4], there)

        @pl.when(step == GROUPS - 1)
        def _():
            give_back(1, (GROUPS - 1) * group)

        valid = lax.broadcasted_iota(jnp.int32, (src_len, rows), 0) < length_ref[0]
        lane = lax.broadcasted_iota(jnp.int32, (rows, LANES), 1)
        for pair in range(width // LANES):
            at = slice(pair * LANES, (pair + 1) * LANES)
            query = got_ref[pl.ds(start, group), 0, :, at].reshape(rows, LANES)
            grad = got_ref[pl.ds(start, group), 1, :, at].reshape(rows, LANES)
            keys = key_ref[:, at]
            values = value_ref[:, at]
            key_sum = key_sums[:, at]
            value_sum = value_sums[:, at]
            back = []
            for half in range(LANES // HEAD_DIM):
                own = (lane >= half * HEAD_DIM) & (lane < (half + 1) * HEAD_DIM)
                query_h = jnp.where(own, query, jnp.zeros_like(query))
                grad_h = jnp.where(own, grad, jnp.zeros_like(grad))
                scores = dot(keys, query_h, ((1,), (1,)))
                scores = jnp.where(valid, scores, -1e30)
                peak = jnp.max(scores, axis=0, keepdims=True)
                terms = jnp.exp2((scores - peak) * exp_scale)
                probs = terms * (1.0 / jnp.sum(terms, axis=0, keepdims=True))
                probs_b = probs.astype(jnp.bfloat16)
                prob_grad = dot(values, grad_h, ((1,), (1,)))
                delta = jnp.sum(probs_b.astype(jnp.float32) * prob_grad, axis=0, keepdims=True)
                score_grad = (probs * (prob_grad - delta)).astype(jnp.bfloat16)
                key_sum = key_sum + dot(score_grad, query_h, ((1,), (0,)))
                value_sum = value_sum + dot(probs_b, grad_h, ((1,), (0,)))
                head = pair * LANES + half * HEAD_DIM
                back.append(dot(key_t[head : head + HEAD_DIM, :], score_grad, ((1,), (0,))))
            key_sums[:, at] = key_sum
            value_sums[:, at] = value_sum
            back = jnp.concatenate(back, axis=0) * scale
            back = jnp.transpose(back).astype(jnp.bfloat16)
            back_ref[pl.ds(start, group), :, at] = back.reshape(group, rows // group, LANES)

    def weight_terms(chunk, to_core, target, added, first_x, last_x):
        columns = slice(chunk % halves * chunk_width, (chunk % halves + 1) * chunk_width)

        @pl.loop(first_x, last_x)
        def _(step_x):
            to_x = lax.rem(x + XS // 2 + step_x, XS)
            block = to_core * (XS // 2) + lax.div(to_x, 2)
            first = pl.multiple_of(lax.rem(to_x, 2) * half_rows, half_rows)
            left = grads_t[chunk // halves, pl.ds(first, half_rows), :]
            terms = dot(left, all_states[block, :, columns], ((1,), (0,)))
            if added is not None:
                terms = terms + added[chunk, to_x].reshape(half_rows, chunk_width).astype(jnp.float32)
            target[chunk, to_x] = terms.astype(jnp.bfloat16).reshape(ZS, unit_rows, chunk_width)

    CORE, FAR, NEAR, MERGED, ALONG_Z = (CHUNKS * stage for stage in range(5))
    own_states.wait()
    wait_bytes(all_states.at[pl.ds(0, ys - 1)], gather_in.at[1])
    sibling = lax.rem(core + 1, cores)
    for chunk in range(CHUNKS):
        kind = chunk // halves
        if chunk % halves == 0:
            sums = key_sums[...] * scale if kind == 0 else value_sums[...]
            grads[kind] = sums.astype(jnp.bfloat16)
            grads_t[kind] = jnp.transpose(grads[kind])
        weight_terms(chunk, sibling, term_away, None, 0, XS)
        there = (sibling, x * ZS + z, y)
        at = CORE + chunk
        send(term_away.at[chunk], term_in.at[chunk], sum_out.at[at], sum_in.at[at], there)


    def state_terms(block, target):
        for kind in range(2):
            lines = all_weights[lax.div(block, 2), pl.ds(lax.rem(block, 2) * 2, 2), :, kind]
            terms = dot(grads[kind], lines.reshape(width, features), ((1,), (0,)))
            total = terms if kind == 0 else total + terms
        target[...] = total.astype(jnp.bfloat16)

    def state_send(offset):
        to_y = lax.rem(y + offset, ys)
        state_terms(to_y, part.at[offset])
        there = (core, x * ZS + z, to_y)
        send(part.at[offset], part_in.at[offset - 1], state_sem.at[0], state_sem.at[1], there)

    low, high = pl.ds(0, ZS // 2), pl.ds(ZS // 2, ZS // 2)
    right_x, far_x, left_x = (lax.rem(x + offset, XS) for offset in range(1, XS))

    def x_send(source, target, sem, to_x):
        send(source, target, sum_out.at[sem], sum_in.at[sem], (core, to_x * ZS + z, y))

    for chunk in range(CHUNKS):
        wait_bytes(term_in.at[chunk], sum_in.at[CORE + chunk])
        weight_terms(chunk, core, term_own, term_in, 0, 1)
        x_send(term_own.at[chunk, far_x, low], far_in.at[chunk, 0], FAR + chunk, right_x)
        x_send(term_own.at[chunk, far_x, high], far_in.at[chunk, 1], FAR + chunk, left_x)
        weight_terms(chunk, core, term_own, term_in, 1, XS)
        x_send(term_own.at[chunk, right_x, high], x_in.at[chunk, 0, high], NEAR + chunk, right_x)
        x_send(term_own.at[chunk, left_x, low], x_in.at[chunk, 1, low], NEAR + chunk, left_x)
        if chunk == halves - 1:
            wait_bytes(all_weights.at[pl.ds(0, cores - 1)], gather_in.at[4])
        if chunk % halves == halves - 1:
            state_send(chunk // halves + 1)

    give_back((GROUPS - 1) * group, peers)
    returned_ref[0] = back_ref[0]

    def merge(chunk):
        wait_bytes(far_in.at[chunk], sum_in.at[FAR + chunk])
        for side, (to_x, half) in enumerate(((right_x, low), (left_x, high))):
            both = term_own[chunk, to_x, half].astype(jnp.float32)
            both = both + far_in[chunk, side].astype(jnp.float32)
            term_own[chunk, to_x, half] = both.astype(jnp.bfloat16)
            x_send(term_own.at[chunk, to_x, half], x_in.at[chunk, side, half], MERGED + chunk, to_x)

    for chunk in range(CHUNKS):
        merge(chunk)
        if chunk == 1:
            state_send(3)
    state_terms(y, part.at[0])

    for chunk in range(CHUNKS):
        wait_bytes(far_in.at[chunk], sum_in.at[NEAR + chunk])
        wait_bytes(far_in.at[chunk], sum_in.at[MERGED + chunk])

        @pl.loop(0, ZS)
        def _(to_z):
            total = term_own[chunk, x, to_z].astype(jnp.float32)
            for other in range(2):
                total = total + x_in[chunk, other, to_z].astype(jnp.float32)
            z_own[chunk, to_z] = total.astype(jnp.bfloat16)

        @pl.loop(1, ZS)
        def _(offset):
            to_z = lax.rem(z + offset, ZS)
            there = (core, x * ZS + to_z, y)
            piece = z_own.at[chunk, to_z]
            at = ALONG_Z + chunk
            send(piece, z_in.at[chunk, offset - 1], sum_out.at[at], sum_in.at[at], there)

    wait_bytes(part_in, state_sem.at[1])
    total = part[0].astype(jnp.float32)
    for other in range(ys - 1):
        total = total + part_in[other].astype(jnp.float32)
    state_out[...] = total.astype(jnp.bfloat16)

    for chunk in range(CHUNKS):
        columns = slice(chunk % halves * chunk_width, (chunk % halves + 1) * chunk_width)
        wait_bytes(z_in.at[chunk], sum_in.at[ALONG_Z + chunk])
        total = z_own[chunk, z].astype(jnp.float32)
        for other in range(ZS - 1):
            total = total + z_in[chunk, other].astype(jnp.float32)
        piece_away[chunk // halves, :, columns] = total.astype(jnp.bfloat16)

    @pl.when(away)
    def _():
        send(piece_away, piece_out, state_sem.at[2], state_sem.at[3], partner_of(core, x, y, z))
        wait_bytes(piece_out, state_sem.at[3])
        wait_bytes(piece_away, state_sem.at[2])

    @pl.when(jnp.logical_not(away))
    def _():
        piece_out[...] = piece_away[...]

    wait_bytes(returned_ref.at[pl.ds(1, peers - 1)], row_in.at[GROUPS])
    wait_bytes(send_ref.at[pl.ds(1, peers - 1)], row_out.at[0])
    wait_bytes(back_ref.at[pl.ds(1, peers - 1)], row_out.at[1])
    wait_bytes(all_states.at[pl.ds(0, ys - 1)], gather_out.at[1])
    wait_bytes(all_weights.at[0, 0, pl.ds(0, ZS - 1)], gather_out.at[2])
    wait_bytes(all_weights.at[0, pl.ds(0, XS - 1)], gather_out.at[3])
    wait_bytes(all_weights.at[pl.ds(0, cores - 1)], gather_out.at[4])
    for chunk in range(CHUNKS):
        wait_bytes(term_away.at[chunk], sum_out.at[CORE + chunk])
        for stage in (FAR, NEAR, MERGED):
            wait_bytes(far_in.at[chunk], sum_out.at[stage + chunk])
        wait_bytes(z_in.at[chunk], sum_out.at[ALONG_Z + chunk])
    wait_bytes(part_in, state_sem.at[0])


def whole(length, owners, queries, out_grads, keys, values, states, weights, cores, ys):
    smem, vmem = pl.BlockSpec(memory_space=pltpu.SMEM), pl.BlockSpec(memory_space=pltpu.VMEM)
    hbm = pl.BlockSpec(memory_space=pl.ANY)
    wire = queries.dtype
    targets, tgt_len, width = queries.shape
    peers, peer_rows = cores * XS * ZS, 2 * tgt_len
    packed = (peers, 2, peer_rows, width)
    src_len, features = states.shape
    unit_rows = weights.shape[0]
    piece = (2, unit_rows, features)
    chunk_width = features * 2 // CHUNKS
    terms = (CHUNKS, XS, ZS, unit_rows, chunk_width)
    return pl.pallas_call(
        functools.partial(whole_kernel, cores, ys),
        out_shape=(
            jax.ShapeDtypeStruct((peers, peer_rows, width), wire),
            jax.ShapeDtypeStruct((src_len, features), wire),
            jax.ShapeDtypeStruct(piece, wire),
        ),
        in_specs=[smem, vmem, hbm, hbm, hbm, hbm, hbm, vmem],
        out_specs=(vmem, vmem, vmem),
        scratch_shapes=[
            pltpu.VMEM((targets * tgt_len, width), wire),
            pltpu.VMEM((targets * tgt_len, width), wire),
            pltpu.VMEM(packed, wire),
            pltpu.VMEM(packed, wire),
            pltpu.VMEM((peers, peer_rows, width), wire),
            pltpu.VMEM((src_len, width), wire),
            pltpu.VMEM((src_len, width), wire),
            pltpu.VMEM((width, src_len), wire),
            pltpu.VMEM((src_len, width), jnp.float32),
            pltpu.VMEM((src_len, width), jnp.float32),
            pltpu.VMEM((2, src_len, width), wire),
            pltpu.VMEM((2, width, src_len), wire),
            pltpu.VMEM((ys, src_len, features), wire),
            pltpu.VMEM((cores, XS, ZS, *piece), wire),
            pltpu.VMEM(terms, wire),
            pltpu.VMEM(terms, wire),
            pltpu.VMEM(terms, wire),
            pltpu.VMEM((CHUNKS, 2, ZS // 2, *terms[3:]), wire),
            pltpu.VMEM((CHUNKS, 2, *terms[2:]), wire),
            pltpu.VMEM((CHUNKS, *terms[2:]), wire),
            pltpu.VMEM((CHUNKS, ZS - 1, *terms[3:]), wire),
            pltpu.VMEM((ys, src_len, features), wire),
            pltpu.VMEM((ys - 1, src_len, features), wire),
            pltpu.VMEM(piece, wire),
            pltpu.VMEM(piece, wire),
            pltpu.SemaphoreType.DMA((GROUPS + 1,)),
            pltpu.SemaphoreType.DMA((2,)),
            pltpu.SemaphoreType.DMA((5,)),
            pltpu.SemaphoreType.DMA((5,)),
            pltpu.SemaphoreType.DMA((5 * CHUNKS,)),
            pltpu.SemaphoreType.DMA((5 * CHUNKS,)),
            pltpu.SemaphoreType.DMA((4,)),
            pltpu.SemaphoreType.DMA((6,)),
        ],
        compiler_params=pltpu.CompilerParams(
            collective_id=1, has_side_effects=True, vmem_limit_bytes=56 << 20
        ),
        name="exchange_attend_reduce",
    )(
        length,
        owners[None],
        queries.reshape(targets * tgt_len, width),
        out_grads.reshape(targets * tgt_len, width),
        keys,
        values,
        states,
        weights,
    )


def on_device(queries, out_grads, owners, src_keys, src_values, states, kv_weight, src_lengths):
    cores, ys = lax.axis_size("grp"), lax.axis_size("mdl")
    tgt_len = queries.shape[1]
    returned, state_sum, weight_sum = whole(
        src_lengths,
        owners,
        queries,
        out_grads,
        src_keys[0],
        src_values[0],
        states[0],
        kv_weight,
        cores,
        ys,
    )
    return unpack(owners, returned, state_sum, weight_sum, tgt_len)


def solution(mesh):
    rows = P(ROWS, None, "mdl")
    return jax.shard_map(
        on_device,
        mesh=mesh,
        in_specs=(rows, rows, P(ROWS), rows, rows, rows, rows, P(ROWS)),
        out_specs=(rows, rows, rows),
        check_vma=False,
    )
```

```python
import functools
import math

import jax
import jax.numpy as jnp
from jax import lax
from jax.experimental import pallas as pl
from jax.experimental.pallas import tpu as pltpu
from jax.sharding import PartitionSpec as P

HEAD_DIM = 64
LANES = 128
ROWS = ("grp", "seq")
MESH = pl.DeviceIdType.MESH
XS, ZS, GROUPS, CHUNKS = 4, 8, 4, 4


def place():
    seq = lax.axis_index("seq")
    return lax.axis_index("grp"), lax.div(seq, ZS), lax.axis_index("mdl"), lax.rem(seq, ZS)


def in_plane(core, x, y, z, offset, cores):
    to_core = lax.rem(core + lax.div(offset, XS * ZS), cores)
    to_x = lax.rem(x + lax.rem(lax.div(offset, ZS), XS), XS)
    to_z = lax.rem(z + lax.rem(offset, ZS), ZS)
    return (to_core, to_x * ZS + to_z, y)


def back_in_plane(core, x, y, z, offset, cores):
    to_core = lax.rem(core + cores - lax.div(offset, XS * ZS), cores)
    to_x = lax.rem(x + XS - lax.rem(lax.div(offset, ZS), XS), XS)
    to_z = lax.rem(z + ZS - lax.rem(offset, ZS), ZS)
    return (to_core, to_x * ZS + to_z, y)


def partner_of(core, x, y, z):
    half = XS // 2
    to_x = lax.rem(y, 2) * half + lax.rem(x, half)
    return (lax.div(y, 2), to_x * ZS + z, core * 2 + lax.div(x, half))


def in_column(partner, z, offset):
    return (partner[0], lax.div(partner[1], ZS) * ZS + lax.rem(z + offset, ZS), partner[2])


def greet(core, x, y, z, cores, ys, partner, away):
    barrier = pltpu.get_barrier_semaphore()
    peers = cores * XS * ZS

    @pl.loop(1, peers)
    def _(offset):
        there = in_plane(core, x, y, z, offset, cores)
        pl.semaphore_signal(barrier, inc=1, device_id=there, device_id_type=MESH)

    @pl.loop(1, ys)
    def _(offset):
        there = (core, x * ZS + z, lax.rem(y + offset, ys))
        pl.semaphore_signal(barrier, inc=1, device_id=there, device_id_type=MESH)

    @pl.when(away)
    def _():
        @pl.loop(0, ZS)
        def _(offset):
            there = in_column(partner, z, offset)
            pl.semaphore_signal(barrier, inc=1, device_id=there, device_id_type=MESH)

    pl.semaphore_wait(barrier, peers + ys - 2 + ZS * away.astype(jnp.int32))


def send(source, target, send_sem, recv_sem, there):
    pltpu.make_async_remote_copy(
        src_ref=source,
        dst_ref=target,
        send_sem=send_sem,
        recv_sem=recv_sem,
        device_id=there,
        device_id_type=MESH,
    ).start()


def wait_bytes(ref, sem):
    pltpu.make_async_copy(ref, ref, sem).wait()


def dot(left, right, dims):
    return lax.dot_general(left, right, (dims, ((), ())), preferred_element_type=jnp.float32)


def peer_of(owner, core, x, z):
    to_core = (lax.shift_right_logical(owner, 5) - core) & 1
    to_x = (lax.shift_right_logical(owner, 3) - x) & (XS - 1)
    to_z = (owner - z) & (ZS - 1)
    return (to_core * XS + to_x) * ZS + to_z


def row_slots(owners_ref, core, x, z, tgt_len):
    targets = owners_ref.shape[1]
    peer_row = jnp.broadcast_to(peer_of(owners_ref[...], core, x, z), (targets, targets))
    down = lax.broadcasted_iota(jnp.int32, (targets, targets), 0)
    across = lax.broadcasted_iota(jnp.int32, (targets, targets), 1)
    peer = jnp.sum(jnp.where(down == across, peer_row, 0), axis=1, keepdims=True)
    earlier = (peer_row == peer) & (across < down)
    slot = peer * 2 + jnp.sum(jnp.where(earlier, 1, 0), axis=1, keepdims=True)
    shape = (targets, targets * tgt_len)
    token = lax.broadcasted_iota(jnp.int32, shape, 1)
    first = lax.broadcasted_iota(jnp.int32, shape, 0) * tgt_len
    here = (token >= first) & (token < first + tgt_len)
    return jnp.sum(jnp.where(here, slot * tgt_len + token - first, 0), axis=0, keepdims=True)


def unpack_kernel(
    owners_ref, back_ref, state_ref, weight_ref, out_ref, state_out, weight_out, used_ref, slot_ref
):
    targets, tgt_len, _ = out_ref.shape
    core, x, _, z = place()

    @pl.loop(0, back_ref.shape[0], unroll=8)
    def _(peer):
        used_ref[peer] = 0

    @pl.loop(0, targets, unroll=4)
    def _(target):
        peer = peer_of(owners_ref[target], core, x, z)
        used = used_ref[peer]
        used_ref[peer] = 1
        slot_ref[target] = peer * 2 + used

    @pl.loop(0, targets, unroll=8)
    def _(target):
        slot = slot_ref[target]
        both = back_ref[lax.shift_right_logical(slot, 1)]
        out_ref[target] = jnp.where((slot & 1) == 0, both[:tgt_len], both[tgt_len:])

    state_out[0] = state_ref[...]
    for kind in range(2):
        weight_out[:, kind, :] = weight_ref[kind].astype(jnp.float32)


def unpack(owners, returned, state, weight, tgt_len):
    peers, _, width = returned.shape
    targets = owners.shape[0]
    kinds, unit_rows, features = weight.shape
    smem, vmem = pl.BlockSpec(memory_space=pltpu.SMEM), pl.BlockSpec(memory_space=pltpu.VMEM)
    return pl.pallas_call(
        unpack_kernel,
        out_shape=(
            jax.ShapeDtypeStruct((targets, tgt_len, width), returned.dtype),
            jax.ShapeDtypeStruct((1, *state.shape), state.dtype),
            jax.ShapeDtypeStruct((unit_rows, kinds, features), jnp.float32),
        ),
        in_specs=[smem, vmem, vmem, vmem],
        out_specs=(vmem, vmem, vmem),
        scratch_shapes=[pltpu.SMEM((peers,), jnp.int32), pltpu.SMEM((targets,), jnp.int32)],
        name="unpack_targets",
    )(owners, returned, state, weight)


def whole_kernel(
    cores,
    ys,
    length_ref,
    owners_ref,
    query_hbm,
    grad_hbm,
    key_hbm,
    value_hbm,
    states_hbm,
    weight_ref,
    returned_ref,
    state_out,
    piece_out,
    query_ref,
    grad_ref,
    send_ref,
    got_ref,
    back_ref,
    key_ref,
    value_ref,
    key_t,
    key_sums,
    value_sums,
    grads,
    grads_t,
    all_states,
    all_weights,
    term_away,
    term_own,
    term_in,
    far_in,
    x_in,
    z_own,
    z_in,
    part,
    part_in,
    piece_away,
    piece_ref,
    row_in,
    row_out,
    gather_in,
    gather_out,
    sum_in,
    sum_out,
    state_sem,
    own_sem,
):
    core, x, y, z = place()
    peers = cores * XS * ZS
    group = peers // GROUPS
    partner = partner_of(core, x, y, z)
    away = partner[2] != y
    src_len, width = key_ref.shape
    unit_rows, chunk_width = term_own.shape[3:]
    features = all_states.shape[2]
    halves = CHUNKS // 2
    half_rows = ZS * unit_rows
    scale = HEAD_DIM**-0.5
    exp_scale = scale * math.log2(math.e)
    rows = group * got_ref.shape[2]

    own_keys = pltpu.make_async_copy(key_hbm, key_ref, own_sem.at[0])
    own_values = pltpu.make_async_copy(value_hbm, value_ref, own_sem.at[1])
    own_states = pltpu.make_async_copy(states_hbm, all_states.at[y], own_sem.at[2])
    own_queries = pltpu.make_async_copy(query_hbm, query_ref, own_sem.at[3])
    own_grads = pltpu.make_async_copy(grad_hbm, grad_ref, own_sem.at[5])
    for copy in (own_queries, own_grads, own_keys, own_values, own_states):
        copy.start()
    for kind in range(2):
        piece_ref[kind] = weight_ref[:, kind, :]
    greet(core, x, y, z, cores, ys, partner, away)

    to_core, to_x = partner[0], lax.div(partner[1], ZS)
    own_piece = pltpu.make_async_copy(piece_ref, all_weights.at[core, x, z], own_sem.at[4])

    @pl.loop(1, ZS)
    def _(offset):
        there = in_column(partner, z, offset)
        send(piece_ref, all_weights.at[to_core, to_x, z], gather_out.at[2], gather_in.at[2], there)

    @pl.when(away)
    def _():
        there = partner_of(core, x, y, z)
        send(piece_ref, all_weights.at[to_core, to_x, z], gather_out.at[0], gather_in.at[0], there)

    @pl.when(jnp.logical_not(away))
    def _():
        own_piece.start()

    @pl.loop(1, ys)
    def _(offset):
        there = (core, x * ZS + z, lax.rem(y + offset, ys))
        send(states_hbm, all_states.at[y], gather_out.at[1], gather_in.at[1], there)

    def dispatch(first, last):
        @pl.loop(first, last)
        def _(offset):
            there = in_plane(core, x, y, z, offset, cores)
            at = lax.div(offset, group)
            send(send_ref.at[offset], got_ref.at[offset], row_out.at[0], row_in.at[at], there)

    tgt_len = got_ref.shape[2] // 2
    taken = row_slots(owners_ref, core, x, z, tgt_len)
    own_queries.wait()
    own_grads.wait()

    def pack(at):
        slot_row = lax.broadcasted_iota(jnp.int32, (rows, taken.shape[1]), 0) + at * rows
        chosen = jnp.where(slot_row == taken, 1.0, 0.0).astype(jnp.bfloat16)
        for kind, ref in enumerate((query_ref, grad_ref)):
            filled = dot(chosen, ref[...], ((1,), (0,))).astype(jnp.bfloat16)
            send_ref[at * group : (at + 1) * group, kind] = filled.reshape(group, rows // group, width)

    pack(0)
    dispatch(1, group)
    pack(1)
    dispatch(group, 2 * group)
    got_ref[0] = send_ref[0]
    for at in range(2, GROUPS):
        pack(at)
    key_sums[...] = jnp.zeros_like(key_sums)
    value_sums[...] = jnp.zeros_like(value_sums)
    own_keys.wait()
    own_values.wait()
    key_t[...] = jnp.transpose(key_ref[...])

    @pl.when(away)
    def _():
        wait_bytes(piece_ref, gather_in.at[0])
        wait_bytes(piece_ref, gather_out.at[0])

    @pl.when(jnp.logical_not(away))
    def _():
        own_piece.wait()

    wait_bytes(all_weights.at[0, 0, pl.ds(0, ZS - 1)], gather_in.at[2])

    @pl.loop(1, XS)
    def _(offset):
        there = (core, lax.rem(x + offset, XS) * ZS + z, y)
        line = all_weights.at[core, x]
        send(line, line, gather_out.at[3], gather_in.at[3], there)

    def give_back(first, last):
        @pl.loop(first, last)
        def _(offset):
            there = back_in_plane(core, x, y, z, offset, cores)
            send(back_ref.at[offset], returned_ref.at[offset], row_out.at[1], row_in.at[GROUPS], there)

    @pl.loop(0, GROUPS)
    def _(step):
        start = step * group

        @pl.when(step == 0)
        def _():
            wait_bytes(got_ref.at[pl.ds(1, group - 1)], row_in.at[0])

        @pl.when(step > 0)
        def _():
            wait_bytes(got_ref.at[pl.ds(start, group)], row_in.at[step])

        @pl.when(step < GROUPS - 2)
        def _():
            dispatch((step + 2) * group, (step + 3) * group)

        @pl.when(step == GROUPS - 1)
        def _():
            give_back(1, (GROUPS - 1) * group)

        valid = lax.broadcasted_iota(jnp.int32, (src_len, rows), 0) < length_ref[0]
        lane = lax.broadcasted_iota(jnp.int32, (rows, LANES), 1)
        for pair in range(width // LANES):
            at = slice(pair * LANES, (pair + 1) * LANES)
            query = got_ref[pl.ds(start, group), 0, :, at].reshape(rows, LANES)
            grad = got_ref[pl.ds(start, group), 1, :, at].reshape(rows, LANES)
            keys = key_ref[:, at]
            values = value_ref[:, at]
            key_sum = key_sums[:, at]
            value_sum = value_sums[:, at]
            back = []
            for half in range(LANES // HEAD_DIM):
                own = (lane >= half * HEAD_DIM) & (lane < (half + 1) * HEAD_DIM)
                query_h = jnp.where(own, query, jnp.zeros_like(query))
                grad_h = jnp.where(own, grad, jnp.zeros_like(grad))
                scores = dot(keys, query_h, ((1,), (1,)))
                scores = jnp.where(valid, scores, -1e30)
                peak = jnp.max(scores, axis=0, keepdims=True)
                terms = jnp.exp2((scores - peak) * exp_scale)
                probs = terms * (1.0 / jnp.sum(terms, axis=0, keepdims=True))
                probs_b = probs.astype(jnp.bfloat16)
                prob_grad = dot(values, grad_h, ((1,), (1,)))
                delta = jnp.sum(probs_b.astype(jnp.float32) * prob_grad, axis=0, keepdims=True)
                score_grad = (probs * (prob_grad - delta)).astype(jnp.bfloat16)
                key_sum = key_sum + dot(score_grad, query_h, ((1,), (0,)))
                value_sum = value_sum + dot(probs_b, grad_h, ((1,), (0,)))
                head = pair * LANES + half * HEAD_DIM
                back.append(dot(key_t[head : head + HEAD_DIM, :], score_grad, ((1,), (0,))))
            key_sums[:, at] = key_sum
            value_sums[:, at] = value_sum
            back = jnp.concatenate(back, axis=0) * scale
            back = jnp.transpose(back).astype(jnp.bfloat16)
            back_ref[pl.ds(start, group), :, at] = back.reshape(group, rows // group, LANES)

        @pl.when(step == GROUPS - 2)
        def _():
            wait_bytes(all_weights.at[0, pl.ds(0, XS - 1)], gather_in.at[3])

            @pl.loop(1, cores)
            def _(offset):
                there = (lax.rem(core + offset, cores), x * ZS + z, y)
                half = all_weights.at[core]
                send(half, half, gather_out.at[4], gather_in.at[4], there)

    def weight_terms(chunk, to_core, target, added, first_x, last_x):
        columns = slice(chunk % halves * chunk_width, (chunk % halves + 1) * chunk_width)

        @pl.loop(first_x, last_x)
        def _(step_x):
            to_x = lax.rem(x + XS // 2 + step_x, XS)
            block = to_core * (XS // 2) + lax.div(to_x, 2)
            first = pl.multiple_of(lax.rem(to_x, 2) * half_rows, half_rows)
            left = grads_t[chunk // halves, pl.ds(first, half_rows), :]
            terms = dot(left, all_states[block, :, columns], ((1,), (0,)))
            if added is not None:
                terms = terms + added[chunk, to_x].reshape(half_rows, chunk_width).astype(jnp.float32)
            target[chunk, to_x] = terms.astype(jnp.bfloat16).reshape(ZS, unit_rows, chunk_width)

    CORE, FAR, NEAR, MERGED, ALONG_Z = (CHUNKS * stage for stage in range(5))
    own_states.wait()
    wait_bytes(all_states.at[pl.ds(0, ys - 1)], gather_in.at[1])
    sibling = lax.rem(core + 1, cores)
    for chunk in range(CHUNKS):
        kind = chunk // halves
        if chunk % halves == 0:
            sums = key_sums[...] * scale if kind == 0 else value_sums[...]
            grads[kind] = sums.astype(jnp.bfloat16)
            grads_t[kind] = jnp.transpose(grads[kind])
        weight_terms(chunk, sibling, term_away, None, 0, XS)
        there = (sibling, x * ZS + z, y)
        at = CORE + chunk
        send(term_away.at[chunk], term_in.at[chunk], sum_out.at[at], sum_in.at[at], there)


    def state_terms(block, target):
        for kind in range(2):
            lines = all_weights[lax.div(block, 2), pl.ds(lax.rem(block, 2) * 2, 2), :, kind]
            terms = dot(grads[kind], lines.reshape(width, features), ((1,), (0,)))
            total = terms if kind == 0 else total + terms
        target[...] = total.astype(jnp.bfloat16)

    def state_send(offset):
        to_y = lax.rem(y + offset, ys)
        state_terms(to_y, part.at[offset])
        there = (core, x * ZS + z, to_y)
        send(part.at[offset], part_in.at[offset - 1], state_sem.at[0], state_sem.at[1], there)

    low, high = pl.ds(0, ZS // 2), pl.ds(ZS // 2, ZS // 2)
    right_x, far_x, left_x = (lax.rem(x + offset, XS) for offset in range(1, XS))

    def x_send(source, target, sem, to_x):
        send(source, target, sum_out.at[sem], sum_in.at[sem], (core, to_x * ZS + z, y))

    for chunk in range(CHUNKS):
        wait_bytes(term_in.at[chunk], sum_in.at[CORE + chunk])
        weight_terms(chunk, core, term_own, term_in, 0, 1)
        x_send(term_own.at[chunk, far_x, low], far_in.at[chunk, 0], FAR + chunk, right_x)
        x_send(term_own.at[chunk, far_x, high], far_in.at[chunk, 1], FAR + chunk, left_x)
        weight_terms(chunk, core, term_own, term_in, 1, XS)
        x_send(term_own.at[chunk, right_x, high], x_in.at[chunk, 0, high], NEAR + chunk, right_x)
        x_send(term_own.at[chunk, left_x, low], x_in.at[chunk, 1, low], NEAR + chunk, left_x)
        if chunk == halves - 1:
            wait_bytes(all_weights.at[pl.ds(0, cores - 1)], gather_in.at[4])
        if chunk % halves == halves - 1:
            state_send(chunk // halves + 1)

    give_back((GROUPS - 1) * group, peers)
    returned_ref[0] = back_ref[0]

    def merge(chunk):
        wait_bytes(far_in.at[chunk], sum_in.at[FAR + chunk])
        for side, (to_x, half) in enumerate(((right_x, low), (left_x, high))):
            both = term_own[chunk, to_x, half].astype(jnp.float32)
            both = both + far_in[chunk, side].astype(jnp.float32)
            term_own[chunk, to_x, half] = both.astype(jnp.bfloat16)
            x_send(term_own.at[chunk, to_x, half], x_in.at[chunk, side, half], MERGED + chunk, to_x)

    for chunk in range(CHUNKS):
        merge(chunk)
        if chunk == 1:
            state_send(3)
    state_terms(y, part.at[0])

    for chunk in range(CHUNKS):
        wait_bytes(far_in.at[chunk], sum_in.at[NEAR + chunk])
        wait_bytes(far_in.at[chunk], sum_in.at[MERGED + chunk])

        @pl.loop(0, ZS)
        def _(to_z):
            total = term_own[chunk, x, to_z].astype(jnp.float32)
            for other in range(2):
                total = total + x_in[chunk, other, to_z].astype(jnp.float32)
            z_own[chunk, to_z] = total.astype(jnp.bfloat16)

        @pl.loop(1, ZS)
        def _(offset):
            to_z = lax.rem(z + offset, ZS)
            there = (core, x * ZS + to_z, y)
            piece = z_own.at[chunk, to_z]
            at = ALONG_Z + chunk
            send(piece, z_in.at[chunk, offset - 1], sum_out.at[at], sum_in.at[at], there)

    wait_bytes(part_in, state_sem.at[1])
    total = part[0].astype(jnp.float32)
    for other in range(ys - 1):
        total = total + part_in[other].astype(jnp.float32)
    state_out[...] = total.astype(jnp.bfloat16)

    for chunk in range(CHUNKS):
        columns = slice(chunk % halves * chunk_width, (chunk % halves + 1) * chunk_width)
        wait_bytes(z_in.at[chunk], sum_in.at[ALONG_Z + chunk])
        total = z_own[chunk, z].astype(jnp.float32)
        for other in range(ZS - 1):
            total = total + z_in[chunk, other].astype(jnp.float32)
        piece_away[chunk // halves, :, columns] = total.astype(jnp.bfloat16)

    @pl.when(away)
    def _():
        send(piece_away, piece_out, state_sem.at[2], state_sem.at[3], partner_of(core, x, y, z))
        wait_bytes(piece_out, state_sem.at[3])
        wait_bytes(piece_away, state_sem.at[2])

    @pl.when(jnp.logical_not(away))
    def _():
        piece_out[...] = piece_away[...]

    wait_bytes(returned_ref.at[pl.ds(1, peers - 1)], row_in.at[GROUPS])
    wait_bytes(send_ref.at[pl.ds(1, peers - 1)], row_out.at[0])
    wait_bytes(back_ref.at[pl.ds(1, peers - 1)], row_out.at[1])
    wait_bytes(all_states.at[pl.ds(0, ys - 1)], gather_out.at[1])
    wait_bytes(all_weights.at[0, 0, pl.ds(0, ZS - 1)], gather_out.at[2])
    wait_bytes(all_weights.at[0, pl.ds(0, XS - 1)], gather_out.at[3])
    wait_bytes(all_weights.at[pl.ds(0, cores - 1)], gather_out.at[4])
    for chunk in range(CHUNKS):
        wait_bytes(term_away.at[chunk], sum_out.at[CORE + chunk])
        for stage in (FAR, NEAR, MERGED):
            wait_bytes(far_in.at[chunk], sum_out.at[stage + chunk])
        wait_bytes(z_in.at[chunk], sum_out.at[ALONG_Z + chunk])
    wait_bytes(part_in, state_sem.at[0])


def whole(length, owners, queries, out_grads, keys, values, states, weights, cores, ys):
    smem, vmem = pl.BlockSpec(memory_space=pltpu.SMEM), pl.BlockSpec(memory_space=pltpu.VMEM)
    hbm = pl.BlockSpec(memory_space=pl.ANY)
    wire = queries.dtype
    targets, tgt_len, width = queries.shape
    peers, peer_rows = cores * XS * ZS, 2 * tgt_len
    packed = (peers, 2, peer_rows, width)
    src_len, features = states.shape
    unit_rows = weights.shape[0]
    piece = (2, unit_rows, features)
    chunk_width = features * 2 // CHUNKS
    terms = (CHUNKS, XS, ZS, unit_rows, chunk_width)
    return pl.pallas_call(
        functools.partial(whole_kernel, cores, ys),
        out_shape=(
            jax.ShapeDtypeStruct((peers, peer_rows, width), wire),
            jax.ShapeDtypeStruct((src_len, features), wire),
            jax.ShapeDtypeStruct(piece, wire),
        ),
        in_specs=[smem, vmem, hbm, hbm, hbm, hbm, hbm, vmem],
        out_specs=(vmem, vmem, vmem),
        scratch_shapes=[
            pltpu.VMEM((targets * tgt_len, width), wire),
            pltpu.VMEM((targets * tgt_len, width), wire),
            pltpu.VMEM(packed, wire),
            pltpu.VMEM(packed, wire),
            pltpu.VMEM((peers, peer_rows, width), wire),
            pltpu.VMEM((src_len, width), wire),
            pltpu.VMEM((src_len, width), wire),
            pltpu.VMEM((width, src_len), wire),
            pltpu.VMEM((src_len, width), jnp.float32),
            pltpu.VMEM((src_len, width), jnp.float32),
            pltpu.VMEM((2, src_len, width), wire),
            pltpu.VMEM((2, width, src_len), wire),
            pltpu.VMEM((ys, src_len, features), wire),
            pltpu.VMEM((cores, XS, ZS, *piece), wire),
            pltpu.VMEM(terms, wire),
            pltpu.VMEM(terms, wire),
            pltpu.VMEM(terms, wire),
            pltpu.VMEM((CHUNKS, 2, ZS // 2, *terms[3:]), wire),
            pltpu.VMEM((CHUNKS, 2, *terms[2:]), wire),
            pltpu.VMEM((CHUNKS, *terms[2:]), wire),
            pltpu.VMEM((CHUNKS, ZS - 1, *terms[3:]), wire),
            pltpu.VMEM((ys, src_len, features), wire),
            pltpu.VMEM((ys - 1, src_len, features), wire),
            pltpu.VMEM(piece, wire),
            pltpu.VMEM(piece, wire),
            pltpu.SemaphoreType.DMA((GROUPS + 1,)),
            pltpu.SemaphoreType.DMA((2,)),
            pltpu.SemaphoreType.DMA((5,)),
            pltpu.SemaphoreType.DMA((5,)),
            pltpu.SemaphoreType.DMA((5 * CHUNKS,)),
            pltpu.SemaphoreType.DMA((5 * CHUNKS,)),
            pltpu.SemaphoreType.DMA((4,)),
            pltpu.SemaphoreType.DMA((6,)),
        ],
        compiler_params=pltpu.CompilerParams(
            collective_id=1, has_side_effects=True, vmem_limit_bytes=56 << 20
        ),
        name="exchange_attend_reduce",
    )(
        length,
        owners[None],
        queries.reshape(targets * tgt_len, width),
        out_grads.reshape(targets * tgt_len, width),
        keys,
        values,
        states,
        weights,
    )


def on_device(queries, out_grads, owners, src_keys, src_values, states, kv_weight, src_lengths):
    cores, ys = lax.axis_size("grp"), lax.axis_size("mdl")
    tgt_len = queries.shape[1]
    returned, state_sum, weight_sum = whole(
        src_lengths,
        owners,
        queries,
        out_grads,
        src_keys[0],
        src_values[0],
        states[0],
        kv_weight,
        cores,
        ys,
    )
    return unpack(owners, returned, state_sum, weight_sum, tgt_len)


def solution(mesh):
    rows = P(ROWS, None, "mdl")
    return jax.shard_map(
        on_device,
        mesh=mesh,
        in_specs=(rows, rows, P(ROWS), rows, rows, rows, rows, P(ROWS)),
        out_specs=(rows, rows, rows),
        check_vma=False,
    )
```

```python
import functools
import math

import jax
import jax.numpy as jnp
from jax import lax
from jax.experimental import pallas as pl
from jax.experimental.pallas import tpu as pltpu
from jax.sharding import PartitionSpec as P

HEAD_DIM = 64
LANES = 128
ROWS = ("grp", "seq")
MESH = pl.DeviceIdType.MESH
XS, ZS, GROUPS, CHUNKS = 4, 8, 4, 4


def place():
    seq = lax.axis_index("seq")
    return lax.axis_index("grp"), lax.div(seq, ZS), lax.axis_index("mdl"), lax.rem(seq, ZS)


def in_plane(core, x, y, z, offset, cores):
    to_core = lax.rem(core + lax.div(offset, XS * ZS), cores)
    to_x = lax.rem(x + lax.rem(lax.div(offset, ZS), XS), XS)
    to_z = lax.rem(z + lax.rem(offset, ZS), ZS)
    return (to_core, to_x * ZS + to_z, y)


def back_in_plane(core, x, y, z, offset, cores):
    to_core = lax.rem(core + cores - lax.div(offset, XS * ZS), cores)
    to_x = lax.rem(x + XS - lax.rem(lax.div(offset, ZS), XS), XS)
    to_z = lax.rem(z + ZS - lax.rem(offset, ZS), ZS)
    return (to_core, to_x * ZS + to_z, y)


def partner_of(core, x, y, z):
    half = XS // 2
    to_x = lax.rem(y, 2) * half + lax.rem(x, half)
    return (lax.div(y, 2), to_x * ZS + z, core * 2 + lax.div(x, half))


def in_column(partner, z, offset):
    return (partner[0], lax.div(partner[1], ZS) * ZS + lax.rem(z + offset, ZS), partner[2])


def greet(core, x, y, z, cores, ys, partner, away):
    barrier = pltpu.get_barrier_semaphore()
    peers = cores * XS * ZS

    @pl.loop(1, peers)
    def _(offset):
        there = in_plane(core, x, y, z, offset, cores)
        pl.semaphore_signal(barrier, inc=1, device_id=there, device_id_type=MESH)

    @pl.loop(1, ys)
    def _(offset):
        there = (core, x * ZS + z, lax.rem(y + offset, ys))
        pl.semaphore_signal(barrier, inc=1, device_id=there, device_id_type=MESH)

    @pl.when(away)
    def _():
        @pl.loop(0, ZS)
        def _(offset):
            there = in_column(partner, z, offset)
            pl.semaphore_signal(barrier, inc=1, device_id=there, device_id_type=MESH)

    pl.semaphore_wait(barrier, peers + ys - 2 + ZS * away.astype(jnp.int32))


def send(source, target, send_sem, recv_sem, there):
    pltpu.make_async_remote_copy(
        src_ref=source,
        dst_ref=target,
        send_sem=send_sem,
        recv_sem=recv_sem,
        device_id=there,
        device_id_type=MESH,
    ).start()


def wait_bytes(ref, sem):
    pltpu.make_async_copy(ref, ref, sem).wait()


def dot(left, right, dims):
    return lax.dot_general(left, right, (dims, ((), ())), preferred_element_type=jnp.float32)


def peer_of(owner, core, x, z):
    to_core = (lax.shift_right_logical(owner, 5) - core) & 1
    to_x = (lax.shift_right_logical(owner, 3) - x) & (XS - 1)
    to_z = (owner - z) & (ZS - 1)
    return (to_core * XS + to_x) * ZS + to_z


def row_slots(owners_ref, core, x, z, tgt_len):
    targets = owners_ref.shape[1]
    peer_row = jnp.broadcast_to(peer_of(owners_ref[...], core, x, z), (targets, targets))
    down = lax.broadcasted_iota(jnp.int32, (targets, targets), 0)
    across = lax.broadcasted_iota(jnp.int32, (targets, targets), 1)
    peer = jnp.sum(jnp.where(down == across, peer_row, 0), axis=1, keepdims=True)
    earlier = (peer_row == peer) & (across < down)
    slot = peer * 2 + jnp.sum(jnp.where(earlier, 1, 0), axis=1, keepdims=True)
    shape = (targets, targets * tgt_len)
    token = lax.broadcasted_iota(jnp.int32, shape, 1)
    first = lax.broadcasted_iota(jnp.int32, shape, 0) * tgt_len
    here = (token >= first) & (token < first + tgt_len)
    return jnp.sum(jnp.where(here, slot * tgt_len + token - first, 0), axis=0, keepdims=True)


def unpack_kernel(
    owners_ref, back_ref, state_ref, weight_ref, out_ref, state_out, weight_out, used_ref, slot_ref
):
    targets, tgt_len, _ = out_ref.shape
    core, x, _, z = place()

    @pl.loop(0, back_ref.shape[0], unroll=8)
    def _(peer):
        used_ref[peer] = 0

    @pl.loop(0, targets, unroll=4)
    def _(target):
        peer = peer_of(owners_ref[target], core, x, z)
        used = used_ref[peer]
        used_ref[peer] = 1
        slot_ref[target] = peer * 2 + used

    @pl.loop(0, targets, unroll=8)
    def _(target):
        slot = slot_ref[target]
        both = back_ref[lax.shift_right_logical(slot, 1)]
        out_ref[target] = jnp.where((slot & 1) == 0, both[:tgt_len], both[tgt_len:])

    state_out[0] = state_ref[...]
    for kind in range(2):
        weight_out[:, kind, :] = weight_ref[kind].astype(jnp.float32)


def unpack(owners, returned, state, weight, tgt_len):
    peers, _, width = returned.shape
    targets = owners.shape[0]
    kinds, unit_rows, features = weight.shape
    smem, vmem = pl.BlockSpec(memory_space=pltpu.SMEM), pl.BlockSpec(memory_space=pltpu.VMEM)
    return pl.pallas_call(
        unpack_kernel,
        out_shape=(
            jax.ShapeDtypeStruct((targets, tgt_len, width), returned.dtype),
            jax.ShapeDtypeStruct((1, *state.shape), state.dtype),
            jax.ShapeDtypeStruct((unit_rows, kinds, features), jnp.float32),
        ),
        in_specs=[smem, vmem, vmem, vmem],
        out_specs=(vmem, vmem, vmem),
        scratch_shapes=[pltpu.SMEM((peers,), jnp.int32), pltpu.SMEM((targets,), jnp.int32)],
        name="unpack_targets",
    )(owners, returned, state, weight)


def whole_kernel(
    cores,
    ys,
    length_ref,
    owners_ref,
    query_hbm,
    grad_hbm,
    key_hbm,
    value_hbm,
    states_hbm,
    weight_ref,
    returned_ref,
    state_out,
    piece_out,
    query_ref,
    grad_ref,
    send_ref,
    got_ref,
    back_ref,
    key_ref,
    value_ref,
    key_t,
    key_sums,
    value_sums,
    grads,
    grads_t,
    all_states,
    all_weights,
    term_away,
    term_own,
    term_in,
    far_in,
    x_in,
    z_own,
    z_in,
    part,
    part_in,
    piece_away,
    piece_ref,
    row_in,
    row_out,
    gather_in,
    gather_out,
    sum_in,
    sum_out,
    state_sem,
    own_sem,
):
    core, x, y, z = place()
    peers = cores * XS * ZS
    group = peers // GROUPS
    partner = partner_of(core, x, y, z)
    away = partner[2] != y
    src_len, width = key_ref.shape
    unit_rows, chunk_width = term_own.shape[3:]
    features = all_states.shape[2]
    halves = CHUNKS // 2
    half_rows = ZS * unit_rows
    scale = HEAD_DIM**-0.5
    exp_scale = scale * math.log2(math.e)
    rows = group * got_ref.shape[2]

    own_keys = pltpu.make_async_copy(key_hbm, key_ref, own_sem.at[0])
    own_values = pltpu.make_async_copy(value_hbm, value_ref, own_sem.at[1])
    own_states = pltpu.make_async_copy(states_hbm, all_states.at[y], own_sem.at[2])
    own_queries = pltpu.make_async_copy(query_hbm, query_ref, own_sem.at[3])
    own_grads = pltpu.make_async_copy(grad_hbm, grad_ref, own_sem.at[5])
    for copy in (own_queries, own_grads, own_keys, own_values, own_states):
        copy.start()
    for kind in range(2):
        piece_ref[kind] = weight_ref[:, kind, :]
    greet(core, x, y, z, cores, ys, partner, away)

    to_core, to_x = partner[0], lax.div(partner[1], ZS)
    own_piece = pltpu.make_async_copy(piece_ref, all_weights.at[core, x, z], own_sem.at[4])

    @pl.loop(1, ZS)
    def _(offset):
        there = in_column(partner, z, offset)
        send(piece_ref, all_weights.at[to_core, to_x, z], gather_out.at[2], gather_in.at[2], there)

    @pl.when(away)
    def _():
        there = partner_of(core, x, y, z)
        send(piece_ref, all_weights.at[to_core, to_x, z], gather_out.at[0], gather_in.at[0], there)

    @pl.when(jnp.logical_not(away))
    def _():
        own_piece.start()

    @pl.loop(1, ys)
    def _(offset):
        there = (core, x * ZS + z, lax.rem(y + offset, ys))
        send(states_hbm, all_states.at[y], gather_out.at[1], gather_in.at[1], there)

    def dispatch(first, last):
        @pl.loop(first, last)
        def _(offset):
            there = in_plane(core, x, y, z, offset, cores)
            at = lax.div(offset, group)
            send(send_ref.at[offset], got_ref.at[offset], row_out.at[0], row_in.at[at], there)

    tgt_len = got_ref.shape[2] // 2
    taken = row_slots(owners_ref, core, x, z, tgt_len)
    own_queries.wait()
    own_grads.wait()

    def pack(at):
        slot_row = lax.broadcasted_iota(jnp.int32, (rows, taken.shape[1]), 0) + at * rows
        chosen = jnp.where(slot_row == taken, 1.0, 0.0).astype(jnp.bfloat16)
        for kind, ref in enumerate((query_ref, grad_ref)):
            filled = dot(chosen, ref[...], ((1,), (0,))).astype(jnp.bfloat16)
            send_ref[at * group : (at + 1) * group, kind] = filled.reshape(group, rows // group, width)

    pack(0)
    dispatch(1, group)
    pack(1)
    dispatch(group, 2 * group)
    got_ref[0] = send_ref[0]
    for at in range(2, GROUPS):
        pack(at)
    key_sums[...] = jnp.zeros_like(key_sums)
    value_sums[...] = jnp.zeros_like(value_sums)
    own_keys.wait()
    own_values.wait()
    key_t[...] = jnp.transpose(key_ref[...])

    @pl.when(away)
    def _():
        wait_bytes(piece_ref, gather_in.at[0])
        wait_bytes(piece_ref, gather_out.at[0])

    @pl.when(jnp.logical_not(away))
    def _():
        own_piece.wait()

    wait_bytes(all_weights.at[0, 0, pl.ds(0, ZS - 1)], gather_in.at[2])

    @pl.loop(1, XS)
    def _(offset):
        there = (core, lax.rem(x + offset, XS) * ZS + z, y)
        line = all_weights.at[core, x]
        send(line, line, gather_out.at[3], gather_in.at[3], there)

    def give_back(first, last):
        @pl.loop(first, last)
        def _(offset):
            there = back_in_plane(core, x, y, z, offset, cores)
            send(back_ref.at[offset], returned_ref.at[offset], row_out.at[1], row_in.at[GROUPS], there)

    @pl.loop(0, GROUPS)
    def _(step):
        start = step * group

        @pl.when(step == 0)
        def _():
            wait_bytes(got_ref.at[pl.ds(1, group - 1)], row_in.at[0])

        @pl.when(step > 0)
        def _():
            wait_bytes(got_ref.at[pl.ds(start, group)], row_in.at[step])

        @pl.when(step < GROUPS - 2)
        def _():
            dispatch((step + 2) * group, (step + 3) * group)

        @pl.when(step == GROUPS - 1)
        def _():
            give_back(2 * group, (GROUPS - 1) * group)

        valid = lax.broadcasted_iota(jnp.int32, (src_len, rows), 0) < length_ref[0]
        lane = lax.broadcasted_iota(jnp.int32, (rows, LANES), 1)
        for pair in range(width // LANES):
            at = slice(pair * LANES, (pair + 1) * LANES)
            query = got_ref[pl.ds(start, group), 0, :, at].reshape(rows, LANES)
            grad = got_ref[pl.ds(start, group), 1, :, at].reshape(rows, LANES)
            keys = key_ref[:, at]
            values = value_ref[:, at]
            key_sum = key_sums[:, at]
            value_sum = value_sums[:, at]
            back = []
            for half in range(LANES // HEAD_DIM):
                own = (lane >= half * HEAD_DIM) & (lane < (half + 1) * HEAD_DIM)
                query_h = jnp.where(own, query, jnp.zeros_like(query))
                grad_h = jnp.where(own, grad, jnp.zeros_like(grad))
                scores = dot(keys, query_h, ((1,), (1,)))
                scores = jnp.where(valid, scores, -1e30)
                peak = jnp.max(scores, axis=0, keepdims=True)
                terms = jnp.exp2((scores - peak) * exp_scale)
                probs = terms * (1.0 / jnp.sum(terms, axis=0, keepdims=True))
                probs_b = probs.astype(jnp.bfloat16)
                prob_grad = dot(values, grad_h, ((1,), (1,)))
                delta = jnp.sum(probs_b.astype(jnp.float32) * prob_grad, axis=0, keepdims=True)
                score_grad = (probs * (prob_grad - delta)).astype(jnp.bfloat16)
                key_sum = key_sum + dot(score_grad, query_h, ((1,), (0,)))
                value_sum = value_sum + dot(probs_b, grad_h, ((1,), (0,)))
                head = pair * LANES + half * HEAD_DIM
                back.append(dot(key_t[head : head + HEAD_DIM, :], score_grad, ((1,), (0,))))
            key_sums[:, at] = key_sum
            value_sums[:, at] = value_sum
            back = jnp.concatenate(back, axis=0) * scale
            back = jnp.transpose(back).astype(jnp.bfloat16)
            back_ref[pl.ds(start, group), :, at] = back.reshape(group, rows // group, LANES)

        @pl.when(step == GROUPS - 2)
        def _():
            wait_bytes(all_weights.at[0, pl.ds(0, XS - 1)], gather_in.at[3])

            @pl.loop(1, cores)
            def _(offset):
                there = (lax.rem(core + offset, cores), x * ZS + z, y)
                half = all_weights.at[core]
                send(half, half, gather_out.at[4], gather_in.at[4], there)

            give_back(1, 2 * group)

    def weight_terms(chunk, to_core, target, added, first_x, last_x):
        columns = slice(chunk % halves * chunk_width, (chunk % halves + 1) * chunk_width)

        @pl.loop(first_x, last_x)
        def _(step_x):
            to_x = lax.rem(x + XS // 2 + step_x, XS)
            block = to_core * (XS // 2) + lax.div(to_x, 2)
            first = pl.multiple_of(lax.rem(to_x, 2) * half_rows, half_rows)
            left = grads_t[chunk // halves, pl.ds(first, half_rows), :]
            terms = dot(left, all_states[block, :, columns], ((1,), (0,)))
            if added is not None:
                terms = terms + added[chunk, to_x].reshape(half_rows, chunk_width).astype(jnp.float32)
            target[chunk, to_x] = terms.astype(jnp.bfloat16).reshape(ZS, unit_rows, chunk_width)

    CORE, FAR, NEAR, MERGED, ALONG_Z = (CHUNKS * stage for stage in range(5))
    own_states.wait()
    wait_bytes(all_states.at[pl.ds(0, ys - 1)], gather_in.at[1])
    sibling = lax.rem(core + 1, cores)
    for chunk in range(CHUNKS):
        kind = chunk // halves
        if chunk % halves == 0:
            sums = key_sums[...] * scale if kind == 0 else value_sums[...]
            grads[kind] = sums.astype(jnp.bfloat16)
            grads_t[kind] = jnp.transpose(grads[kind])
        weight_terms(chunk, sibling, term_away, None, 0, XS)
        there = (sibling, x * ZS + z, y)
        at = CORE + chunk
        send(term_away.at[chunk], term_in.at[chunk], sum_out.at[at], sum_in.at[at], there)


    def state_terms(block, target):
        for kind in range(2):
            lines = all_weights[lax.div(block, 2), pl.ds(lax.rem(block, 2) * 2, 2), :, kind]
            terms = dot(grads[kind], lines.reshape(width, features), ((1,), (0,)))
            total = terms if kind == 0 else total + terms
        target[...] = total.astype(jnp.bfloat16)

    def state_send(offset):
        to_y = lax.rem(y + offset, ys)
        state_terms(to_y, part.at[offset])
        there = (core, x * ZS + z, to_y)
        send(part.at[offset], part_in.at[offset - 1], state_sem.at[0], state_sem.at[1], there)

    low, high = pl.ds(0, ZS // 2), pl.ds(ZS // 2, ZS // 2)
    right_x, far_x, left_x = (lax.rem(x + offset, XS) for offset in range(1, XS))

    def x_send(source, target, sem, to_x):
        send(source, target, sum_out.at[sem], sum_in.at[sem], (core, to_x * ZS + z, y))

    for chunk in range(CHUNKS):
        wait_bytes(term_in.at[chunk], sum_in.at[CORE + chunk])
        weight_terms(chunk, core, term_own, term_in, 0, 1)
        x_send(term_own.at[chunk, far_x, low], far_in.at[chunk, 0], FAR + chunk, right_x)
        x_send(term_own.at[chunk, far_x, high], far_in.at[chunk, 1], FAR + chunk, left_x)
        weight_terms(chunk, core, term_own, term_in, 1, XS)
        x_send(term_own.at[chunk, right_x, high], x_in.at[chunk, 0, high], NEAR + chunk, right_x)
        x_send(term_own.at[chunk, left_x, low], x_in.at[chunk, 1, low], NEAR + chunk, left_x)
        if chunk == halves - 1:
            wait_bytes(all_weights.at[pl.ds(0, cores - 1)], gather_in.at[4])
        if chunk % halves == halves - 1:
            state_send(chunk // halves + 1)

    give_back((GROUPS - 1) * group, peers)
    returned_ref[0] = back_ref[0]

    def merge(chunk):
        wait_bytes(far_in.at[chunk], sum_in.at[FAR + chunk])
        for side, (to_x, half) in enumerate(((right_x, low), (left_x, high))):
            both = term_own[chunk, to_x, half].astype(jnp.float32)
            both = both + far_in[chunk, side].astype(jnp.float32)
            term_own[chunk, to_x, half] = both.astype(jnp.bfloat16)
            x_send(term_own.at[chunk, to_x, half], x_in.at[chunk, side, half], MERGED + chunk, to_x)

    for chunk in range(CHUNKS):
        merge(chunk)
        if chunk == 1:
            state_send(3)
    state_terms(y, part.at[0])

    for chunk in range(CHUNKS):
        wait_bytes(far_in.at[chunk], sum_in.at[NEAR + chunk])
        wait_bytes(far_in.at[chunk], sum_in.at[MERGED + chunk])

        @pl.loop(0, ZS)
        def _(to_z):
            total = term_own[chunk, x, to_z].astype(jnp.float32)
            for other in range(2):
                total = total + x_in[chunk, other, to_z].astype(jnp.float32)
            z_own[chunk, to_z] = total.astype(jnp.bfloat16)

        @pl.loop(1, ZS)
        def _(offset):
            to_z = lax.rem(z + offset, ZS)
            there = (core, x * ZS + to_z, y)
            piece = z_own.at[chunk, to_z]
            at = ALONG_Z + chunk
            send(piece, z_in.at[chunk, offset - 1], sum_out.at[at], sum_in.at[at], there)

    wait_bytes(part_in, state_sem.at[1])
    total = part[0].astype(jnp.float32)
    for other in range(ys - 1):
        total = total + part_in[other].astype(jnp.float32)
    state_out[...] = total.astype(jnp.bfloat16)

    for chunk in range(CHUNKS):
        columns = slice(chunk % halves * chunk_width, (chunk % halves + 1) * chunk_width)
        wait_bytes(z_in.at[chunk], sum_in.at[ALONG_Z + chunk])
        total = z_own[chunk, z].astype(jnp.float32)
        for other in range(ZS - 1):
            total = total + z_in[chunk, other].astype(jnp.float32)
        piece_away[chunk // halves, :, columns] = total.astype(jnp.bfloat16)

    @pl.when(away)
    def _():
        send(piece_away, piece_out, state_sem.at[2], state_sem.at[3], partner_of(core, x, y, z))
        wait_bytes(piece_out, state_sem.at[3])
        wait_bytes(piece_away, state_sem.at[2])

    @pl.when(jnp.logical_not(away))
    def _():
        piece_out[...] = piece_away[...]

    wait_bytes(returned_ref.at[pl.ds(1, peers - 1)], row_in.at[GROUPS])
    wait_bytes(send_ref.at[pl.ds(1, peers - 1)], row_out.at[0])
    wait_bytes(back_ref.at[pl.ds(1, peers - 1)], row_out.at[1])
    wait_bytes(all_states.at[pl.ds(0, ys - 1)], gather_out.at[1])
    wait_bytes(all_weights.at[0, 0, pl.ds(0, ZS - 1)], gather_out.at[2])
    wait_bytes(all_weights.at[0, pl.ds(0, XS - 1)], gather_out.at[3])
    wait_bytes(all_weights.at[pl.ds(0, cores - 1)], gather_out.at[4])
    for chunk in range(CHUNKS):
        wait_bytes(term_away.at[chunk], sum_out.at[CORE + chunk])
        for stage in (FAR, NEAR, MERGED):
            wait_bytes(far_in.at[chunk], sum_out.at[stage + chunk])
        wait_bytes(z_in.at[chunk], sum_out.at[ALONG_Z + chunk])
    wait_bytes(part_in, state_sem.at[0])


def whole(length, owners, queries, out_grads, keys, values, states, weights, cores, ys):
    smem, vmem = pl.BlockSpec(memory_space=pltpu.SMEM), pl.BlockSpec(memory_space=pltpu.VMEM)
    hbm = pl.BlockSpec(memory_space=pl.ANY)
    wire = queries.dtype
    targets, tgt_len, width = queries.shape
    peers, peer_rows = cores * XS * ZS, 2 * tgt_len
    packed = (peers, 2, peer_rows, width)
    src_len, features = states.shape
    unit_rows = weights.shape[0]
    piece = (2, unit_rows, features)
    chunk_width = features * 2 // CHUNKS
    terms = (CHUNKS, XS, ZS, unit_rows, chunk_width)
    return pl.pallas_call(
        functools.partial(whole_kernel, cores, ys),
        out_shape=(
            jax.ShapeDtypeStruct((peers, peer_rows, width), wire),
            jax.ShapeDtypeStruct((src_len, features), wire),
            jax.ShapeDtypeStruct(piece, wire),
        ),
        in_specs=[smem, vmem, hbm, hbm, hbm, hbm, hbm, vmem],
        out_specs=(vmem, vmem, vmem),
        scratch_shapes=[
            pltpu.VMEM((targets * tgt_len, width), wire),
            pltpu.VMEM((targets * tgt_len, width), wire),
            pltpu.VMEM(packed, wire),
            pltpu.VMEM(packed, wire),
            pltpu.VMEM((peers, peer_rows, width), wire),
            pltpu.VMEM((src_len, width), wire),
            pltpu.VMEM((src_len, width), wire),
            pltpu.VMEM((width, src_len), wire),
            pltpu.VMEM((src_len, width), jnp.float32),
            pltpu.VMEM((src_len, width), jnp.float32),
            pltpu.VMEM((2, src_len, width), wire),
            pltpu.VMEM((2, width, src_len), wire),
            pltpu.VMEM((ys, src_len, features), wire),
            pltpu.VMEM((cores, XS, ZS, *piece), wire),
            pltpu.VMEM(terms, wire),
            pltpu.VMEM(terms, wire),
            pltpu.VMEM(terms, wire),
            pltpu.VMEM((CHUNKS, 2, ZS // 2, *terms[3:]), wire),
            pltpu.VMEM((CHUNKS, 2, *terms[2:]), wire),
            pltpu.VMEM((CHUNKS, *terms[2:]), wire),
            pltpu.VMEM((CHUNKS, ZS - 1, *terms[3:]), wire),
            pltpu.VMEM((ys, src_len, features), wire),
            pltpu.VMEM((ys - 1, src_len, features), wire),
            pltpu.VMEM(piece, wire),
            pltpu.VMEM(piece, wire),
            pltpu.SemaphoreType.DMA((GROUPS + 1,)),
            pltpu.SemaphoreType.DMA((2,)),
            pltpu.SemaphoreType.DMA((5,)),
            pltpu.SemaphoreType.DMA((5,)),
            pltpu.SemaphoreType.DMA((5 * CHUNKS,)),
            pltpu.SemaphoreType.DMA((5 * CHUNKS,)),
            pltpu.SemaphoreType.DMA((4,)),
            pltpu.SemaphoreType.DMA((6,)),
        ],
        compiler_params=pltpu.CompilerParams(
            collective_id=1, has_side_effects=True, vmem_limit_bytes=56 << 20
        ),
        name="exchange_attend_reduce",
    )(
        length,
        owners[None],
        queries.reshape(targets * tgt_len, width),
        out_grads.reshape(targets * tgt_len, width),
        keys,
        values,
        states,
        weights,
    )


def on_device(queries, out_grads, owners, src_keys, src_values, states, kv_weight, src_lengths):
    cores, ys = lax.axis_size("grp"), lax.axis_size("mdl")
    tgt_len = queries.shape[1]
    returned, state_sum, weight_sum = whole(
        src_lengths,
        owners,
        queries,
        out_grads,
        src_keys[0],
        src_values[0],
        states[0],
        kv_weight,
        cores,
        ys,
    )
    return unpack(owners, returned, state_sum, weight_sum, tgt_len)


def solution(mesh):
    rows = P(ROWS, None, "mdl")
    return jax.shard_map(
        on_device,
        mesh=mesh,
        in_specs=(rows, rows, P(ROWS), rows, rows, rows, rows, P(ROWS)),
        out_specs=(rows, rows, rows),
        check_vma=False,
    )
```
